768 devices in a mesh: gx: 8 (over x, core), gy: 8 (over y), gz: 12 (over z).
Axes of the slice: x: 4, y: 8, z: 12, core: 2. Of those that a mesh axis runs over, the one named last changes fastest.
Arguments:
- right_side: float32 [64, 64, 1536], P('gx', 'gy', 'gz'), may hold values from -8 to 8
- geometry: float32 [4, 64, 64, 1536], P(None, 'gx', 'gy', 'gz'), may hold values from 0.02 to 0.2
- element_shape_class: int32 [8, 8, 192], P('gx', 'gy', 'gz'), may hold values from 0 to 31
- fdm_vectors: float32 [32, 3, 10, 10], replicated, may hold values from -1 to 2
- fdm_values: float32 [32, 3, 10], replicated, may hold values from 0.3 to 10
Outputs:
- solution: float32 [64, 64, 1536], P('gx', 'gy', 'gz')
- residual: float32 [64, 64, 1536], P('gx', 'gy', 'gz')
The draws below stay inside these ranges and needn't reach their ends.
All inputs are finite; a program needn't handle non-finite values.
Results may differ from the reference program's by a relative error of at most 0.0003.
Values sent between devices are 32-bit elements; how exact they have to be, the bound alone decides.
No kernel may reach another device: no remote copies, remote signals or barrier semaphores. Data moves between devices by JAX's collectives and lax.ppermute only.
A program may use at most 32 MiB of HBM per device.

```python
import math
import jax
import jax.numpy as jnp
import numpy as np
from jax import lax

EXTENDED = 10
SHAPE_CLASSES = 32
ITERS = 2
ELEMENTS_FIRST = 8
ELEMENTS_SECOND = 8
ELEMENTS_THIRD = 192
NX = 64
NY = 64
NZ = 1536


def unique_index(length):
    position = jnp.arange(length, dtype=jnp.int32)
    return position // 8 * 7 + position % 8


def draw_right_side(key, part):
    count_x = 7 * ELEMENTS_FIRST + 1
    count_y = 7 * ELEMENTS_SECOND + 1
    count_along_depth = 7 * ELEMENTS_THIRD + 1
    along_first = jnp.arange(count_x, dtype=jnp.float32) / count_x
    along_second = jnp.arange(count_y, dtype=jnp.float32) / count_y
    along_third = jnp.arange(count_along_depth, dtype=jnp.float32) / count_along_depth
    scale_field = jnp.sqrt(1.0 + 2.0 * (along_first[:, None, None] + along_second[None, :, None] + along_third[None, None, :]) / 3.0)
    base_values = jax.random.truncated_normal(key, -4.0, 4.0, (count_x, count_y, count_along_depth), jnp.float32)
    unique_field = base_values * scale_field
    spread = jnp.take(unique_field, unique_index(NX), axis=0)
    spread = jnp.take(spread, unique_index(NY), axis=1)
    return jnp.take(spread, unique_index(NZ), axis=2)


def draw_fdm_vectors(key, part):
    full_shape = (SHAPE_CLASSES, 3, EXTENDED, EXTENDED)
    identity = (lax.broadcasted_iota(jnp.int32, full_shape, 2) == lax.broadcasted_iota(jnp.int32, full_shape, 3)).astype(jnp.float32)
    spread = 0.25 * jax.random.truncated_normal(key, -3.0, 3.0, full_shape, jnp.float32)
    return identity + spread


def touch_ends(drawn, rng, least, high):
    spot = [jax.random.randint(jax.random.fold_in(rng, axis), (), 0, length) for axis, length in enumerate(drawn.shape)]
    longest = drawn.shape.index(max(drawn.shape))
    neighbour = spot[:longest] + [(spot[longest] + 1) % drawn.shape[longest]] + spot[longest + 1:]
    return drawn.at[tuple(spot)].set(least).at[tuple(neighbour)].set(high)


def levels(key, dims, cuts, low, largest):
    def one(axis_at, blocks):
        steps = jax.random.uniform(jax.random.fold_in(jax.random.fold_in(key, 6), axis_at), (blocks,), jnp.float32, low / len(cuts), largest / len(cuts))
        return jnp.repeat(jnp.exp(steps), dims[axis_at] // blocks).reshape((-1,) + (1,) * (len(dims) - axis_at - 1))

    level = one(*cuts[0])
    for cut in cuts[1:]:
        level = level * one(*cut)
    return level


def setup_inputs(seed: int = 0) -> dict:
    keys = jax.random.split(jax.random.key(seed), 6)
    right_side = draw_right_side(jax.random.fold_in(keys[5], 71), 0)
    geometry = jnp.clip(jnp.exp(math.log(0.2) - 2.3025851 * jax.random.uniform(keys[1], (4, NX, NY, NZ), jnp.float32) ** levels(keys[1], (4, NX, NY, NZ), ((1, 8), (2, 8), (3, 12)), -0.2, 0.2)), 0.02, 0.2)
    element_shape_class = touch_ends(jax.random.randint(keys[2], (ELEMENTS_FIRST, ELEMENTS_SECOND, ELEMENTS_THIRD), 0, SHAPE_CLASSES), jax.random.fold_in(keys[2], 1), 0, SHAPE_CLASSES - 1).astype(jnp.int32)
    fdm_vectors = draw_fdm_vectors(jax.random.fold_in(keys[5], 71), 0)
    fdm_values = jnp.clip(jnp.exp(jax.random.uniform(keys[4], (SHAPE_CLASSES, 3, EXTENDED), jnp.float32, math.log(0.3), math.log(10.0))), 0.3, 10.0)
    return {"right_side": right_side, "geometry": geometry, "element_shape_class": element_shape_class, "fdm_vectors": fdm_vectors, "fdm_values": fdm_values}


HIGHEST = lax.Precision.HIGHEST
FORWARD_FORMS = ("ai,eiyz->eayz", "aj,xejz->xeaz", "ak,xyek->xyea")


def derivative_table():
    points = np.array([-1.0, -0.8717401485096066, -0.5917001814331423, -0.2092992179024789,
                       0.2092992179024789, 0.5917001814331423, 0.8717401485096066, 1.0])
    previous = np.ones(8)
    current = points * 1.0
    for order in range(1, 7):
        following = ((2 * order + 1) * points * current - order * previous) / (order + 1)
        previous = current
        current = following
    legendre = current
    spacing = points[:, None] - points[None, :] + np.eye(8)
    off_diagonal = legendre[:, None] / (legendre[None, :] * spacing)
    positions = np.arange(8)
    end_values = np.where(positions == 0, -14.0, 0.0) + np.where(positions == 7, 14.0, 0.0)
    return np.where(np.eye(8) > 0, np.eye(8) * end_values[None, :], off_diagonal)


def apply_along(field, matrix, dim_index):
    sizes = list(field.shape)
    split_shape = sizes[:dim_index] + [sizes[dim_index] // 8, 8] + sizes[dim_index + 1:]
    blocks = field.reshape(split_shape)
    return jnp.einsum(FORWARD_FORMS[dim_index], matrix, blocks, precision=HIGHEST).reshape(sizes)


def local_operator(field, geometry, derivative):
    total = geometry[3] * field
    for dim_index in range(3):
        gradient = apply_along(field, derivative, dim_index)
        total = total + apply_along(geometry[dim_index] * gradient, derivative.T, dim_index)
    return total


def pair_add(padded, dim_index):
    length = padded.shape[dim_index] - 2
    middle = lax.slice_in_dim(padded, 1, length + 1, axis=dim_index)
    following = lax.slice_in_dim(padded, 2, length + 2, axis=dim_index)
    previous = lax.slice_in_dim(padded, 0, length, axis=dim_index)
    position = lax.broadcasted_iota(jnp.int32, middle.shape, dim_index) % 8
    return middle + jnp.where(position == 7, following, 0.0) + jnp.where(position == 0, previous, 0.0)


def pad_axis(array_in, dim_index, before, after):
    config = [(before, after) if place == dim_index else (0, 0) for place in range(array_in.ndim)]
    return jnp.pad(array_in, config)


def extend_axis(padded, dim_index):
    sizes = list(padded.shape)
    length = sizes[dim_index] - 4
    element_count = length // 8
    left_layer = lax.slice_in_dim(padded, 0, length, 8, dim_index)
    own_nodes = lax.slice_in_dim(padded, 2, length + 2, 1, dim_index)
    right_layer = lax.slice_in_dim(padded, 11, length + 4, 8, dim_index)
    single_shape = sizes[:dim_index] + [element_count, 1] + sizes[dim_index + 1:]
    block_shape = sizes[:dim_index] + [element_count, 8] + sizes[dim_index + 1:]
    return jnp.concatenate([left_layer.reshape(single_shape), own_nodes.reshape(block_shape), right_layer.reshape(single_shape)], dim_index + 1)


def contract_axis(blocks, dim_index):
    sizes = list(blocks.shape)
    length = sizes[dim_index] * 8
    merged_shape = sizes[:dim_index] + [length] + sizes[dim_index + 2:]
    left_layer = lax.slice_in_dim(blocks, 0, 1, axis=dim_index + 1)
    own_nodes = lax.slice_in_dim(blocks, 1, 9, axis=dim_index + 1)
    right_layer = lax.slice_in_dim(blocks, 9, 10, axis=dim_index + 1)
    zero_three = jnp.zeros(sizes[:dim_index + 1] + [3] + sizes[dim_index + 2:], blocks.dtype)
    zero_four = jnp.zeros(sizes[:dim_index + 1] + [4] + sizes[dim_index + 2:], blocks.dtype)
    zero_seven = jnp.zeros(sizes[:dim_index + 1] + [7] + sizes[dim_index + 2:], blocks.dtype)
    left_extension_spread = jnp.concatenate([left_layer, zero_seven], dim_index + 1).reshape(merged_shape)
    right_spread = jnp.concatenate([zero_three, right_layer, zero_four], dim_index + 1).reshape(merged_shape)
    right_spread = lax.slice_in_dim(right_spread, 0, length - 4, axis=dim_index)
    return pad_axis(own_nodes.reshape(merged_shape), dim_index, 2, 2) + pad_axis(left_extension_spread, dim_index, 0, 4) + pad_axis(right_spread, dim_index, 8, 0)


def fdm_solve(extended, vectors, values):
    count_x = extended.shape[0]
    count_y = extended.shape[2]
    count_along_depth = extended.shape[4]
    blocks = jnp.transpose(extended, (1, 3, 5, 0, 2, 4)).reshape(10, 10, 10, -1)
    first = jnp.einsum("ame,abce->mbce", vectors[0], blocks, precision=HIGHEST)
    second = jnp.einsum("bne,mbce->mnce", vectors[1], first, precision=HIGHEST)
    third = jnp.einsum("cpe,mnce->mnpe", vectors[2], second, precision=HIGHEST)
    eigenvalue_sum = values[0][:, None, None, :] + values[1][None, :, None, :] + values[2][None, None, :, :]
    scaled = third / eigenvalue_sum
    back_one = jnp.einsum("ame,mnpe->anpe", vectors[0], scaled, precision=HIGHEST)
    back_two = jnp.einsum("bne,anpe->abpe", vectors[1], back_one, precision=HIGHEST)
    result = jnp.einsum("cpe,abpe->abce", vectors[2], back_two, precision=HIGHEST)
    return jnp.transpose(result.reshape(10, 10, 10, count_x, count_y, count_along_depth), (3, 0, 4, 1, 5, 2))


def shared_weight(length, device, devices):
    position = device * length + jnp.arange(length, dtype=jnp.int32)
    shared = ((position % 8 == 7) & (position < length * devices - 1)) | ((position % 8 == 0) & (position > 0))
    return jnp.where(shared, 0.5, 1.0).astype(jnp.float32)


def assemble(field):
    summed = jnp.pad(field, 1)
    for dim_index in range(3):
        summed = pair_add(summed, dim_index)
    return summed


def precondition(residual, vectors, values):
    extended = jnp.pad(residual, 2)
    for dim_index in (0, 2, 4):
        extended = extend_axis(extended, dim_index)
    solved = fdm_solve(extended, vectors, values)
    for dim_index in (4, 2, 0):
        solved = contract_axis(solved, dim_index)
    inner = solved[2:-2, 2:-2, 2:-2]
    return assemble(inner)


def reference(right_side, geometry, element_shape_class, fdm_vectors, fdm_values):
    derivative = jnp.asarray(derivative_table(), jnp.float32)
    weight = (shared_weight(right_side.shape[0], 0, 1)[:, None, None]
              * shared_weight(right_side.shape[1], 0, 1)[None, :, None]
              * shared_weight(right_side.shape[2], 0, 1)[None, None, :])
    flat_class = element_shape_class.reshape(-1).astype(jnp.int32)
    vectors = jnp.transpose(fdm_vectors[flat_class], (1, 2, 3, 0))
    values = jnp.transpose(fdm_values[flat_class], (1, 2, 0))
    solution = jnp.zeros_like(right_side)
    residual = right_side
    direction = jnp.zeros_like(right_side)
    rho_before = jnp.ones((), jnp.float32)
    for number in range(ITERS):
        precond = precondition(residual, vectors, values)
        rho_now = jnp.sum(weight * residual * precond)
        if number == 0:
            direction = precond
        else:
            direction = precond + (rho_now / rho_before) * direction
        image_field = assemble(local_operator(direction, geometry, derivative))
        step_size = rho_now / jnp.sum(weight * direction * image_field)
        solution = solution + step_size * direction
        residual = residual - step_size * image_field
        rho_before = rho_now
    return solution, residual
```

```python
import jax
import jax.numpy as jnp
import numpy as np
from jax import lax
from jax.sharding import PartitionSpec as P

ITERS = 2


HIGHEST = lax.Precision.HIGHEST
FORWARD_FORMS = ("ai,eiyz->eayz", "aj,xejz->xeaz", "ak,xyek->xyea")


def swap_ends(block, axis, dim, width):
    count = lax.axis_size(axis)
    forward = [(i, i + 1) for i in range(count - 1)]
    backward = [(target, source) for source, target in forward]
    length = block.shape[dim]
    low = lax.ppermute(lax.slice_in_dim(block, length - width, length, axis=dim), axis, forward)
    high = lax.ppermute(lax.slice_in_dim(block, 0, width, axis=dim), axis, backward)
    return low, high


def cut(block, start, stop, dim):
    return lax.slice_in_dim(block, start, stop, axis=dim)


def extend_one(field, axis, dim, add):
    low, high = swap_ends(field, axis, dim, 2)
    first, last = cut(field, 0, 1, dim), cut(field, 7, 8, dim)
    if add:
        first = first + cut(low, 1, 2, dim)
        last = last + cut(high, 0, 1, dim)
    return jnp.concatenate(
        [cut(low, 0, 1, dim), first, cut(field, 1, 7, dim), last, cut(high, 1, 2, dim)], axis=dim
    )


def extend_many(field, axis, add):
    low, high = swap_ends(field, axis, 2, 2)
    rows, columns, length = field.shape
    padded = jnp.concatenate([low, field, high], axis=2)
    own = field.reshape(rows, columns, length // 8, 8)
    first, last = own[..., 0:1], own[..., 7:8]
    if add:
        first = first + padded[..., 1 : length + 1 : 8][..., None]
        last = last + padded[..., 10 : length + 3 : 8][..., None]
    return jnp.concatenate(
        [
            padded[..., 0:length:8][..., None],
            first,
            own[..., 1:7],
            last,
            padded[..., 11 : length + 4 : 8][..., None],
        ],
        axis=3,
    )


def extended_blocks(field, add):
    field = extend_one(field, "gx", 0, add)
    field = extend_one(field, "gy", 1, add)
    return extend_many(field, "gz", add)


def fold_one(block, axis, dim):
    low, high = swap_ends(block, axis, dim, 2)
    return jnp.concatenate(
        [
            cut(block, 1, 3, dim) + low,
            cut(block, 3, 7, dim),
            cut(block, 7, 9, dim) + high,
        ],
        axis=dim,
    )


def fold_many(blocks, axis):
    count = lax.axis_size(axis)
    forward = [(i, i + 1) for i in range(count - 1)]
    backward = [(target, source) for source, target in forward]
    low = lax.ppermute(blocks[:, :, -1:, 8:10], axis, forward)
    high = lax.ppermute(blocks[:, :, :1, 0:2], axis, backward)
    before = jnp.concatenate([low, blocks[:, :, :-1, 8:10]], axis=2)
    after = jnp.concatenate([blocks[:, :, 1:, 0:2], high], axis=2)
    folded = jnp.concatenate(
        [blocks[..., 1:3] + before, blocks[..., 3:7], blocks[..., 7:9] + after], axis=3
    )
    return folded.reshape(folded.shape[0], folded.shape[1], -1)


def folded_field(blocks):
    field = fold_many(blocks, "gz")
    field = fold_one(field, "gy", 1)
    return fold_one(field, "gx", 0)


def derivative_table():
    points = np.array(
        [
            -1.0,
            -0.8717401485096066,
            -0.5917001814331423,
            -0.2092992179024789,
            0.2092992179024789,
            0.5917001814331423,
            0.8717401485096066,
            1.0,
        ]
    )
    previous = np.ones(8)
    current = points * 1.0
    for order in range(1, 7):
        following = ((2 * order + 1) * points * current - order * previous) / (order + 1)
        previous = current
        current = following
    spacing = points[:, None] - points[None, :] + np.eye(8)
    off_diagonal = current[:, None] / (current[None, :] * spacing)
    positions = np.arange(8)
    end_values = np.where(positions == 0, -14.0, 0.0) + np.where(positions == 7, 14.0, 0.0)
    return np.where(np.eye(8) > 0, np.eye(8) * end_values[None, :], off_diagonal)


def apply_along(field, matrix, dim_index):
    sizes = list(field.shape)
    split_shape = sizes[:dim_index] + [sizes[dim_index] // 8, 8] + sizes[dim_index + 1 :]
    blocks = field.reshape(split_shape)
    return jnp.einsum(FORWARD_FORMS[dim_index], matrix, blocks, precision=HIGHEST).reshape(sizes)


def local_operator(field, geometry, derivative):
    total = geometry[3] * field
    for dim_index in range(3):
        gradient = apply_along(field, derivative, dim_index)
        total = total + apply_along(geometry[dim_index] * gradient, derivative.T, dim_index)
    return total


def pair_add(padded, dim_index):
    length = padded.shape[dim_index] - 2
    middle = lax.slice_in_dim(padded, 1, length + 1, axis=dim_index)
    following = lax.slice_in_dim(padded, 2, length + 2, axis=dim_index)
    previous = lax.slice_in_dim(padded, 0, length, axis=dim_index)
    position = lax.broadcasted_iota(jnp.int32, middle.shape, dim_index) % 8
    return (
        middle + jnp.where(position == 7, following, 0.0) + jnp.where(position == 0, previous, 0.0)
    )


def fdm_solve(blocks, vectors, values):
    blocks = jnp.transpose(blocks, (0, 1, 3, 2))
    first = jnp.einsum("ame,abce->mbce", vectors[0], blocks, precision=HIGHEST)
    second = jnp.einsum("bne,mbce->mnce", vectors[1], first, precision=HIGHEST)
    third = jnp.einsum("cpe,mnce->mnpe", vectors[2], second, precision=HIGHEST)
    eigenvalue_sum = (
        values[0][:, None, None, :] + values[1][None, :, None, :] + values[2][None, None, :, :]
    )
    scaled = third / eigenvalue_sum
    back_one = jnp.einsum("ame,mnpe->anpe", vectors[0], scaled, precision=HIGHEST)
    back_two = jnp.einsum("bne,anpe->abpe", vectors[1], back_one, precision=HIGHEST)
    result = jnp.einsum("cpe,abpe->abce", vectors[2], back_two, precision=HIGHEST)
    return jnp.transpose(result, (0, 1, 3, 2))


def exchange(row, axes):
    count = 1
    for axis in axes:
        count = count * lax.axis_size(axis)
    sent = jnp.broadcast_to(row[None, None, :], (count, 1, row.shape[0]))
    return lax.all_to_all(sent, axes, 0, 0)[:, 0]


def combine(rows):
    size = jnp.max(rows[:, 4])
    ratio = rows[:, 4] / jnp.where(size > 0, size, 1.0)
    factor = ratio * ratio
    return jnp.stack(
        [
            jnp.sum(rows[:, 0]),
            jnp.sum(rows[:, 1]),
            jnp.sum(rows[:, 2] * factor),
            jnp.sum(rows[:, 3] * factor),
            size,
        ]
    )


def shared_sum(field):
    for axis, dim in (("gx", 0), ("gy", 1), ("gz", 2)):
        low, high = swap_ends(field, axis, dim, 1)
        field = pair_add(jnp.concatenate([low, field, high], axis=dim), dim)
    return field


def on_device(right_side, geometry, element_shape_class, fdm_vectors, fdm_values):
    derivative = jnp.asarray(derivative_table(), jnp.float32)
    classes = fdm_vectors.shape[0]
    flat_class = element_shape_class.reshape(-1)
    onehot = (flat_class[:, None] == jnp.arange(classes, dtype=jnp.int32)[None, :]).astype(
        jnp.float32
    )
    vectors = jnp.dot(onehot, fdm_vectors.reshape(classes, -1), precision=HIGHEST).T.reshape(
        3, 10, 10, -1
    )
    values = jnp.dot(onehot, fdm_values.reshape(classes, -1), precision=HIGHEST).T.reshape(
        3, 10, -1
    )
    blocks = extended_blocks(right_side, False)
    solved = fdm_solve(blocks, vectors, values)
    rho = jnp.sum(blocks * solved)
    p = folded_field(solved)
    local_q = local_operator(p, geometry, derivative)
    d = jnp.sum(p * local_q)
    blocks = extended_blocks(local_q, True)
    q = blocks[1:9, 1:9, :, 1:9].reshape(right_side.shape)
    size = jnp.max(jnp.abs(blocks))
    unit = 1.0 / jnp.where(size > 0, size, 1.0)
    solved = fdm_solve(blocks, vectors, values)
    g_scaled = jnp.sum((blocks * unit) * (solved * unit))
    s = folded_field(solved)
    local_t = local_operator(s, geometry, derivative)
    h_scaled = jnp.sum((s * unit) * (local_t * unit))
    row = jnp.stack([rho, d, g_scaled, h_scaled, size])
    row = combine(exchange(jnp.pad(row, (0, 123)), ("gx", "gy")))
    row = combine(exchange(jnp.pad(row, (0, 123)), ("gz",)))
    t = shared_sum(local_t)
    rho, d, g_scaled, h_scaled, size = row[0], row[1], row[2], row[3], row[4]
    alpha_one = rho / d
    reach = alpha_one * size
    g = reach * reach * g_scaled
    h = reach * reach * h_scaled
    stretch = g / rho
    alpha_two = (g - rho) / (h - stretch * g / alpha_one)
    along = alpha_one + alpha_two * stretch
    across = alpha_one * alpha_two
    return (along * p - across * s, right_side - along * q + across * t)


def solution(mesh):
    placed = (P("gx", "gy", "gz"), P(None, "gx", "gy", "gz"), P("gx", "gy", "gz"), P(), P())
    return jax.shard_map(
        on_device,
        mesh=mesh,
        in_specs=placed,
        out_specs=(P("gx", "gy", "gz"), P("gx", "gy", "gz")),
        check_vma=False,
    )
```

```python
import functools

import jax
import jax.numpy as jnp
import numpy as np
from jax import lax
from jax.experimental import pallas as pl
from jax.experimental.pallas import tpu as pltpu
from jax.sharding import PartitionSpec as P

HIGHEST = lax.Precision.HIGHEST
LANES = 128
REACH = 4
CHUNKS = ((0, 24), (24, 24), (48, 24), (72, 28))


def swap_ends(block, axis, dim, width):
    count = lax.axis_size(axis)
    forward = [(i, i + 1) for i in range(count - 1)]
    backward = [(target, source) for source, target in forward]
    length = block.shape[dim]
    low = lax.ppermute(lax.slice_in_dim(block, length - width, length, axis=dim), axis, forward)
    high = lax.ppermute(lax.slice_in_dim(block, 0, width, axis=dim), axis, backward)
    return low, high


def cut(block, start, stop, dim):
    return lax.slice_in_dim(block, start, stop, axis=dim)


def extend_one(field, axis, dim, add):
    low, high = swap_ends(field, axis, dim, 2)
    first, last = cut(field, 0, 1, dim), cut(field, 7, 8, dim)
    if add:
        first = first + cut(low, 1, 2, dim)
        last = last + cut(high, 0, 1, dim)
    return jnp.concatenate(
        [cut(low, 0, 1, dim), first, cut(field, 1, 7, dim), last, cut(high, 1, 2, dim)], axis=dim
    )


def derivative_table():
    points = np.array(
        [
            -1.0,
            -0.8717401485096066,
            -0.5917001814331423,
            -0.2092992179024789,
            0.2092992179024789,
            0.5917001814331423,
            0.8717401485096066,
            1.0,
        ]
    )
    previous = np.ones(8)
    current = points * 1.0
    for order in range(1, 7):
        following = ((2 * order + 1) * points * current - order * previous) / (order + 1)
        previous = current
        current = following
    spacing = points[:, None] - points[None, :] + np.eye(8)
    off_diagonal = current[:, None] / (current[None, :] * spacing)
    positions = np.arange(8)
    end_values = np.where(positions == 0, -14.0, 0.0) + np.where(positions == 7, 14.0, 0.0)
    return np.where(np.eye(8) > 0, np.eye(8) * end_values[None, :], off_diagonal)


def fold_one(block, axis, dim):
    low, high = swap_ends(block, axis, dim, 2)
    return jnp.concatenate(
        [
            cut(block, 1, 3, dim) + low,
            cut(block, 3, 7, dim),
            cut(block, 7, 9, dim) + high,
        ],
        axis=dim,
    )


def own_lanes(count):
    lane = lax.broadcasted_iota(jnp.int32, (1, LANES), 1)
    return (lane >= REACH) & (lane < REACH + count)


def solve_step(source, target, table, base, transposed, scale=None):
    for start, size in CHUNKS:
        entries = [source[pl.ds(10 * start + k, size, stride=10), :] for k in range(10)]
        for out in range(10):
            total = None
            for k in range(10):
                row = base + (10 * out + k if transposed else 10 * k + out)
                term = table[row : row + 1, :] * entries[k]
                total = term if total is None else total + term
            if scale is not None:
                total = total / (table[300 + out : 301 + out, :] + scale[start : start + size, :])
            target[pl.ds(100 * out + start, size), :] = total


def solve_kernel(count, shared, field, low, high, table, valid, *refs):
    if shared:
        folded, inner, size_row, assembled, blocks, left, right, pair = refs
    else:
        folded, inner, blocks, left, right, pair = refs
    blocks[pl.ds(1000, 40), :] = jnp.zeros((40, LANES), jnp.float32)
    left[pl.ds(1000, 40), :] = jnp.zeros((40, LANES), jnp.float32)
    right[pl.ds(1000, 40), :] = jnp.zeros((40, LANES), jnp.float32)
    for a in range(10):
        for b in range(10):
            if b == 0:
                nodes = low[a, 0]
            elif b == 9:
                nodes = high[a, 1]
            else:
                nodes = field[a, b - 1]
                if shared and b == 1:
                    nodes = nodes + low[a, 1]
                if shared and b == 8:
                    nodes = nodes + high[a, 0]
                if shared and 1 <= a <= 8:
                    assembled[pl.ds(64 * (a - 1) + 8 * (b - 1), 8), :] = nodes
            blocks[pl.ds(100 * a + 10 * b + 1, 8), :] = nodes
    blocks[pl.ds(0, 100, stride=10), :] = pltpu.roll(
        blocks[pl.ds(7, 100, stride=10), :], 1, 1
    )
    blocks[pl.ds(9, 100, stride=10), :] = pltpu.roll(
        blocks[pl.ds(2, 100, stride=10), :], LANES - 1, 1
    )
    for n in range(10):
        pair[pl.ds(10 * n, 10), :] = table[310 + n : 311 + n, :] + table[320:330, :]
    solve_step(blocks, left, table, 200, False)
    solve_step(left, right, table, 100, False)
    solve_step(right, left, table, 0, False, pair)
    solve_step(left, right, table, 200, True)
    solve_step(right, left, table, 100, True)
    solve_step(left, right, table, 0, True)
    exists = valid[...] > 0.0
    own = own_lanes(count)
    unit = 1.0
    if shared:
        largest = jnp.zeros((8, LANES), jnp.float32)
        for row in range(0, 1000, 8):
            largest = jnp.maximum(largest, jnp.abs(blocks[row : row + 8, :]))
        size = jnp.max(jnp.where(own, largest, 0.0))
        unit = 1.0 / jnp.where(size > 0.0, size, 1.0)
        size_row[...] = jnp.full((1, LANES), size, jnp.float32)
    total = jnp.zeros((8, LANES), jnp.float32)
    for row in range(0, 1000, 8):
        total = total + (blocks[row : row + 8, :] * unit) * (right[row : row + 8, :] * unit)
    inner[...] = jnp.sum(jnp.where(own, total, 0.0), axis=0, keepdims=True)

    def entry(c):
        return jnp.where(exists, right[pl.ds(c, 100, stride=10), :], 0.0)

    first, second, second_last, last = entry(0), entry(1), entry(8), entry(9)
    right[pl.ds(1, 100, stride=10), :] = second + pltpu.roll(second_last, 1, 1)
    right[pl.ds(2, 100, stride=10), :] = entry(2) + pltpu.roll(last, 1, 1)
    right[pl.ds(7, 100, stride=10), :] = entry(7) + pltpu.roll(first, LANES - 1, 1)
    right[pl.ds(8, 100, stride=10), :] = second_last + pltpu.roll(second, LANES - 1, 1)
    for a in range(10):
        for b in range(10):
            folded[a, b] = right[pl.ds(100 * a + 10 * b + 1, 8), :]


def block_solve(field, low, high, table, valid, count, shared):
    row = jax.ShapeDtypeStruct((1, LANES), jnp.float32)
    outs = [jax.ShapeDtypeStruct((10, 10, 8, LANES), jnp.float32), row]
    if shared:
        outs += [row, jax.ShapeDtypeStruct((512, LANES), jnp.float32)]
    return pl.pallas_call(
        functools.partial(solve_kernel, count, shared),
        out_shape=outs,
        scratch_shapes=[pltpu.VMEM((1040, LANES), jnp.float32)] * 3
        + [pltpu.VMEM((104, LANES), jnp.float32)],
        name="block_solve_shared" if shared else "block_solve_first",
    )(field, low, high, table, valid)


def both_ways(nodes, metric, derivative):
    slopes = []
    for a in range(8):
        total = None
        for i in range(8):
            if derivative[a, i] != 0.0:
                term = float(derivative[a, i]) * nodes[i]
                total = term if total is None else total + term
        slopes.append(metric[a] * total)
    outs = []
    for i in range(8):
        total = None
        for a in range(8):
            if derivative[a, i] != 0.0:
                term = float(derivative[a, i]) * slopes[a]
                total = term if total is None else total + term
        outs.append(total)
    return outs


def to_lines(sources, count):
    lane = lax.broadcasted_iota(jnp.int32, (LANES, LANES), 0)
    place = lax.broadcasted_iota(jnp.int32, (LANES, LANES), 1)
    total = jnp.zeros((64 * len(sources), LANES), jnp.float32)
    for k in range(8):
        pick = (
            (place == 8 * (lane - REACH) + k) & (lane >= REACH) & (lane < REACH + count)
        ).astype(jnp.bfloat16)
        rest = jnp.concatenate([s[pl.ds(k, 64, stride=8), :] for s in sources], axis=0)
        rest = jnp.where(own_lanes(count), rest, 0.0)
        for _ in range(3):
            part = rest.astype(jnp.bfloat16)
            total = total + jnp.dot(part, pick, preferred_element_type=jnp.float32)
            rest = rest - part.astype(jnp.float32)
    return total


def apply_local(derivative, folded, low, high, geometry, field, image):
    for x in range(8):
        for y in range(8):
            nodes = folded[x + 1, y]
            if x < 2:
                nodes = nodes + low[x, y]
            if x > 5:
                nodes = nodes + high[x - 6, y]
            field[pl.ds(64 * x + 8 * y, 8), :] = nodes
    for row in range(0, 512, 8):
        image[row : row + 8, :] = geometry[1536 + row : 1544 + row, :] * field[row : row + 8, :]
    for line in range(8):
        for dim in range(3):
            if dim == 0:
                spots = [pl.ds(64 * i + 8 * line, 8) for i in range(8)]
                places = spots
            elif dim == 1:
                spots = [pl.ds(64 * line + 8 * i, 8) for i in range(8)]
                places = [pl.ds(512 + 64 * line + 8 * i, 8) for i in range(8)]
            else:
                spots = [pl.ds(64 * line + i, 8, stride=8) for i in range(8)]
                places = [pl.ds(1024 + 64 * line + i, 8, stride=8) for i in range(8)]
            outs = both_ways(
                [field[s, :] for s in spots], [geometry[s, :] for s in places], derivative
            )
            for spot, out in zip(spots, outs):
                image[spot, :] = image[spot, :] + out


def first_operator_kernel(count, derivative, folded, low, high, geometry, field, image, inner):
    apply_local(derivative, folded, low, high, geometry, field, image)
    total = jnp.zeros((8, LANES), jnp.float32)
    for row in range(0, 512, 8):
        total = total + field[row : row + 8, :] * image[row : row + 8, :]
    inner[...] = jnp.sum(jnp.where(own_lanes(count), total, 0.0), axis=0, keepdims=True)
    first = image[pl.ds(0, 64, stride=8), :]
    last = image[pl.ds(7, 64, stride=8), :]
    image[pl.ds(0, 64, stride=8), :] = first + pltpu.roll(last, 1, 1)
    image[pl.ds(7, 64, stride=8), :] = last + pltpu.roll(first, LANES - 1, 1)


def first_operator(folded, low, high, geometry, count):
    full = jax.ShapeDtypeStruct((512, LANES), jnp.float32)
    return pl.pallas_call(
        functools.partial(first_operator_kernel, count, derivative_table()),
        out_shape=[full, full, jax.ShapeDtypeStruct((1, LANES), jnp.float32)],
        name="first_operator",
    )(folded, low, high, geometry)


def spread(values):
    lane = lax.broadcasted_iota(jnp.int32, (1, LANES), 1)
    row = jnp.zeros((1, LANES), jnp.float32)
    for place, value in enumerate(values):
        row = jnp.where(lane == place, value, row)
    return row


def second_operator_kernel(
    count, derivative, folded, low, high, geometry, rho, d, g, size, lines, payload, field, image
):
    apply_local(derivative, folded, low, high, geometry, field, image)
    largest = size[0, 0]
    unit = 1.0 / jnp.where(largest > 0.0, largest, 1.0)
    own = own_lanes(count)
    total = jnp.zeros((8, LANES), jnp.float32)
    for row in range(0, 512, 8):
        total = total + (field[row : row + 8, :] * unit) * (image[row : row + 8, :] * unit)
    h = jnp.sum(jnp.where(own, total, 0.0))
    row = spread([jnp.sum(rho[...]), jnp.sum(d[...]), jnp.sum(g[...]), h, largest])
    payload[...] = jnp.broadcast_to(row, payload.shape)
    lines[...] = to_lines([field, image], count)


def second_operator(folded, low, high, geometry, rho, d, g, size, count, devices):
    return pl.pallas_call(
        functools.partial(second_operator_kernel, count, derivative_table()),
        out_shape=[
            jax.ShapeDtypeStruct((128, LANES), jnp.float32),
            jax.ShapeDtypeStruct((devices, LANES), jnp.float32),
        ],
        scratch_shapes=[pltpu.VMEM((512, LANES), jnp.float32)] * 2,
        name="second_operator",
    )(folded, low, high, geometry, rho, d, g, size)


def lines_kernel(count, one, two, lines):
    lines[...] = to_lines([one, two], count)


def as_lines(one, two, count):
    return pl.pallas_call(
        functools.partial(lines_kernel, count),
        out_shape=jax.ShapeDtypeStruct((128, LANES), jnp.float32),
        name="as_lines",
    )(one, two)


def combine(rows, first):
    size_each = rows[:, first + 4 : first + 5]
    size = jnp.max(size_each)
    ratio = size_each / jnp.where(size > 0.0, size, 1.0)
    factor = ratio * ratio
    return (
        jnp.sum(rows[:, first : first + 1]),
        jnp.sum(rows[:, first + 1 : first + 2]),
        jnp.sum(rows[:, first + 2 : first + 3] * factor),
        jnp.sum(rows[:, first + 3 : first + 4] * factor),
        size,
    )


def middle_kernel(spot, gathered, image, out):
    values = combine(gathered[...], 0)
    lane = lax.broadcasted_iota(jnp.int32, (1, LANES), 1)
    scalars = jnp.zeros((1, LANES), jnp.float32)
    for place, value in enumerate(values):
        scalars = jnp.where(lane == 64 + place, value, scalars)
    line = lax.broadcasted_iota(jnp.int32, (64, LANES), 0)
    across = lax.broadcasted_iota(jnp.int32, (64, LANES), 1)
    first = jnp.sum(jnp.where(line == across, image[:, 0:1], 0.0), axis=0, keepdims=True)
    last = jnp.sum(
        jnp.where(line == across, image[:, LANES - 1 : LANES], 0.0), axis=0, keepdims=True
    )
    target = lax.broadcasted_iota(jnp.int32, out.shape, 0)
    me = spot[0]
    out[...] = scalars + jnp.where(
        target == me + 1, last, jnp.where(target == me - 1, first, 0.0)
    )


def middle(spot, gathered, image, devices):
    smem = pl.BlockSpec(memory_space=pltpu.SMEM)
    vmem = pl.BlockSpec(memory_space=pltpu.VMEM)
    return pl.pallas_call(
        middle_kernel,
        out_shape=jax.ShapeDtypeStruct((devices, LANES), jnp.float32),
        in_specs=[smem, vmem, vmem],
        out_specs=vmem,
        name="middle",
    )(spot, gathered, image)


def finish_kernel(spot, gathered, image, second, first, right_side, solution_out, residual_out):
    rows = gathered[...]
    rho, d, g_scaled, h_scaled, size = combine(rows, 64)
    me = spot[0]
    source = lax.broadcasted_iota(jnp.int32, rows.shape, 0)
    before = jnp.sum(jnp.where(source == me - 1, rows, 0.0), axis=0, keepdims=True)
    after = jnp.sum(jnp.where(source == me + 1, rows, 0.0), axis=0, keepdims=True)
    line = lax.broadcasted_iota(jnp.int32, (64, LANES), 0)
    across = lax.broadcasted_iota(jnp.int32, (64, LANES), 1)
    before = jnp.sum(jnp.where(line == across, before, 0.0), axis=1, keepdims=True)
    after = jnp.sum(jnp.where(line == across, after, 0.0), axis=1, keepdims=True)
    t = image[...]
    behind = pltpu.roll(t, 1, 1)
    ahead = pltpu.roll(t, LANES - 1, 1)
    t = t + jnp.where(
        across % 8 == 7,
        jnp.where(across == LANES - 1, after, ahead),
        jnp.where(across % 8 == 0, jnp.where(across == 0, before, behind), 0.0),
    )
    def splat(value):
        return jnp.full((1, LANES), value, jnp.float32)

    rho, d = splat(rho), splat(d)
    alpha_one = rho / d
    reach = alpha_one * splat(size)
    g = reach * reach * splat(g_scaled)
    h = reach * reach * splat(h_scaled)
    stretch = g / rho
    alpha_two = (g - rho) / (h - stretch * g / alpha_one)
    along = alpha_one + alpha_two * stretch
    turn = alpha_one * alpha_two
    solution_out[...] = along * first[0:64, :] - turn * second[0:64, :]
    residual_out[...] = right_side[...] - along * first[64:128, :] + turn * t


def finish(spot, gathered, image, second, first, right_side):
    smem = pl.BlockSpec(memory_space=pltpu.SMEM)
    vmem = pl.BlockSpec(memory_space=pltpu.VMEM)
    full = jax.ShapeDtypeStruct((64, LANES), jnp.float32)
    return pl.pallas_call(
        finish_kernel,
        out_shape=[full, full],
        in_specs=[smem] + [vmem] * 5,
        out_specs=[vmem, vmem],
        name="finish",
    )(spot, gathered, image, second, first, right_side)


def exchange(rows, axes):
    return lax.all_to_all(rows, axes, 0, 0, tiled=True)


def shared_sum(field, axis, dim):
    low, high = swap_ends(field, axis, dim, 1)
    return jnp.concatenate(
        [cut(field, 0, 1, dim) + low, cut(field, 1, 7, dim), cut(field, 7, 8, dim) + high],
        axis=dim,
    )


def on_lanes(field):
    split = field.reshape(field.shape[:-1] + (field.shape[-1] // 8, 8))
    turned = jnp.swapaxes(split, -1, -2)
    return jnp.pad(turned, [(0, 0)] * (turned.ndim - 1) + [(0, LANES - turned.shape[-1])])


def on_device(right_side, geometry, element_shape_class, fdm_vectors, fdm_values):
    count = element_shape_class.shape[2]
    classes = fdm_vectors.shape[0]
    depth = lax.axis_size("gz")
    plane = lax.axis_size("gx") * lax.axis_size("gy")
    me = lax.axis_index("gz")
    ends = 8 * REACH

    def deepen(field):
        low, high = swap_ends(field, "gz", field.ndim - 1, ends)
        return jnp.concatenate([low, field, high], axis=field.ndim - 1)

    class_line = jnp.repeat(element_shape_class.reshape(1, 1, -1), 8, axis=2).astype(jnp.float32)
    class_lines = jnp.broadcast_to(class_line, (1, 8, 8 * count))
    deep = deepen(jnp.concatenate([right_side, class_lines], axis=0))
    metric = on_lanes(deepen(geometry)).reshape(4 * 512, LANES)
    deep_class = deep[8, 0, ::8].astype(jnp.int32)
    deep_class = jnp.pad(deep_class, (0, LANES - deep_class.shape[0]))
    element = jnp.arange(LANES, dtype=jnp.int32) - REACH + me * count
    valid = ((element >= 0) & (element < depth * count)).astype(jnp.float32)[None, :]
    onehot = (jnp.arange(classes, dtype=jnp.int32)[:, None] == deep_class[None, :]).astype(
        jnp.float32
    )
    entries = jnp.concatenate(
        [fdm_vectors.reshape(classes, 300), fdm_values.reshape(classes, 30)], axis=1
    )
    table = lax.dot_general(
        entries, onehot, (((0,), (0,)), ((), ())), precision=HIGHEST
    )
    field = extend_one(on_lanes(deep[:8]), "gx", 0, False)
    low, high = swap_ends(field, "gy", 1, 2)
    folded, rho = block_solve(field, low, high, table, valid, count, False)
    folded = fold_one(folded, "gy", 1)
    low, high = swap_ends(folded, "gx", 0, 2)
    p, image, d = first_operator(folded, low, high, metric, count)
    field = extend_one(image.reshape(8, 8, 8, LANES), "gx", 0, True)
    low, high = swap_ends(field, "gy", 1, 2)
    folded, g, size, q = block_solve(field, low, high, table, valid, count, True)
    first = as_lines(p, q, count)
    folded = fold_one(folded, "gy", 1)
    low, high = swap_ends(folded, "gx", 0, 2)
    second, payload = second_operator(folded, low, high, metric, rho, d, g, size, count, plane)
    image = shared_sum(second[64:].reshape(8, 8, LANES), "gx", 0)
    image = shared_sum(image, "gy", 1).reshape(64, LANES)
    payload, image = lax.optimization_barrier((payload, image))
    spot = me.astype(jnp.int32).reshape(1)
    gathered = exchange(payload, ("gx", "gy"))
    gathered = exchange(middle(spot, gathered, image, depth), "gz")
    answer, left = finish(
        spot, gathered, image, second, first, right_side.reshape(64, LANES)
    )
    return (answer.reshape(8, 8, LANES), left.reshape(8, 8, LANES))


def solution(mesh):
    placed = (P("gx", "gy", "gz"), P(None, "gx", "gy", "gz"), P("gx", "gy", "gz"), P(), P())
    return jax.shard_map(
        on_device,
        mesh=mesh,
        in_specs=placed,
        out_specs=(P("gx", "gy", "gz"), P("gx", "gy", "gz")),
        check_vma=False,
    )
```

```python
import functools

import jax
import jax.numpy as jnp
import numpy as np
from jax import lax
from jax.experimental import pallas as pl
from jax.experimental.pallas import tpu as pltpu
from jax.sharding import PartitionSpec as P

HIGHEST = lax.Precision.HIGHEST
LANES = 128
REACH = 4
CHUNKS = ((0, 24), (24, 24), (48, 24), (72, 28))


def swap(backward_part, forward_part, axis):
    count = lax.axis_size(axis)
    forward = [(i, i + 1) for i in range(count - 1)]
    backward = [(target, source) for source, target in forward]
    return lax.ppermute(forward_part, axis, forward), lax.ppermute(backward_part, axis, backward)


def derivative_table():
    points = np.array(
        [
            -1.0,
            -0.8717401485096066,
            -0.5917001814331423,
            -0.2092992179024789,
            0.2092992179024789,
            0.5917001814331423,
            0.8717401485096066,
            1.0,
        ]
    )
    previous = np.ones(8)
    current = points * 1.0
    for order in range(1, 7):
        following = ((2 * order + 1) * points * current - order * previous) / (order + 1)
        previous = current
        current = following
    spacing = points[:, None] - points[None, :] + np.eye(8)
    off_diagonal = current[:, None] / (current[None, :] * spacing)
    positions = np.arange(8)
    end_values = np.where(positions == 0, -14.0, 0.0) + np.where(positions == 7, 14.0, 0.0)
    return np.where(np.eye(8) > 0, np.eye(8) * end_values[None, :], off_diagonal)


def own_lanes(count):
    lane = lax.broadcasted_iota(jnp.int32, (1, LANES), 1)
    return (lane >= REACH) & (lane < REACH + count)


def solve_step(source, target, table, base, transposed, scale=None):
    for start, size in CHUNKS:
        entries = [source[pl.ds(10 * start + k, size, stride=10), :] for k in range(10)]
        for out in range(10):
            total = None
            for k in range(10):
                row = base + (10 * out + k if transposed else 10 * k + out)
                term = table[row : row + 1, :] * entries[k]
                total = term if total is None else total + term
            if scale is not None:
                total = total / (table[300 + out : 301 + out, :] + scale[start : start + size, :])
            target[pl.ds(100 * out + start, size), :] = total


def extended_first(a, y, field, low, high, shared):
    if a == 0:
        return low[0, y]
    if a == 9:
        return high[1, y]
    nodes = field[pl.ds(64 * (a - 1) + 8 * y, 8), :]
    if shared and a == 1:
        nodes = nodes + low[1, y]
    if shared and a == 8:
        nodes = nodes + high[0, y]
    return nodes


def second_edges_kernel(shared, field, low, high, backward, forward):
    for a in range(10):
        for y in range(2):
            backward[a, y] = extended_first(a, y, field, low, high, shared)
            forward[a, y] = extended_first(a, 6 + y, field, low, high, shared)


def second_edges(field, low, high, shared):
    return pl.pallas_call(
        functools.partial(second_edges_kernel, shared),
        out_shape=[jax.ShapeDtypeStruct((10, 2, 8, LANES), jnp.float32)] * 2,
        name="second_edges",
    )(field, low, high)


def solve_kernel(count, shared, field, low, high, below, above, table, valid, *refs):
    if shared:
        folded, rims, backward, forward, inner, size_row, assembled, blocks, left, right, pair = refs
    else:
        folded, rims, backward, forward, inner, blocks, left, right, pair = refs
    blocks[pl.ds(1000, 40), :] = jnp.zeros((40, LANES), jnp.float32)
    left[pl.ds(1000, 40), :] = jnp.zeros((40, LANES), jnp.float32)
    right[pl.ds(1000, 40), :] = jnp.zeros((40, LANES), jnp.float32)
    for a in range(10):
        for b in range(10):
            if b == 0:
                nodes = below[a, 0]
            elif b == 9:
                nodes = above[a, 1]
            else:
                nodes = extended_first(a, b - 1, field, low, high, shared)
                if shared and b == 1:
                    nodes = nodes + below[a, 1]
                if shared and b == 8:
                    nodes = nodes + above[a, 0]
                if shared and 1 <= a <= 8:
                    assembled[pl.ds(64 * (a - 1) + 8 * (b - 1), 8), :] = nodes
            blocks[pl.ds(100 * a + 10 * b + 1, 8), :] = nodes
    blocks[pl.ds(0, 100, stride=10), :] = pltpu.roll(
        blocks[pl.ds(7, 100, stride=10), :], 1, 1
    )
    blocks[pl.ds(9, 100, stride=10), :] = pltpu.roll(
        blocks[pl.ds(2, 100, stride=10), :], LANES - 1, 1
    )
    for n in range(10):
        pair[pl.ds(10 * n, 10), :] = table[310 + n : 311 + n, :] + table[320:330, :]
    solve_step(blocks, left, table, 200, False)
    solve_step(left, right, table, 100, False)
    solve_step(right, left, table, 0, False, pair)
    solve_step(left, right, table, 200, True)
    solve_step(right, left, table, 100, True)
    solve_step(left, right, table, 0, True)
    exists = valid[...] > 0.0
    own = own_lanes(count)
    unit = 1.0
    if shared:
        largest = jnp.zeros((8, LANES), jnp.float32)
        for row in range(0, 1000, 8):
            largest = jnp.maximum(largest, jnp.abs(blocks[row : row + 8, :]))
        size = jnp.max(jnp.where(own, largest, 0.0))
        unit = 1.0 / jnp.where(size > 0.0, size, 1.0)
        size_row[...] = jnp.full((1, LANES), size, jnp.float32)
    total = jnp.zeros((8, LANES), jnp.float32)
    for row in range(0, 1000, 8):
        total = total + (blocks[row : row + 8, :] * unit) * (right[row : row + 8, :] * unit)
    inner[...] = jnp.sum(jnp.where(own, total, 0.0), axis=0, keepdims=True)

    def entry(c):
        return jnp.where(exists, right[pl.ds(c, 100, stride=10), :], 0.0)

    first, second, second_last, last = entry(0), entry(1), entry(8), entry(9)
    right[pl.ds(1, 100, stride=10), :] = second + pltpu.roll(second_last, 1, 1)
    right[pl.ds(2, 100, stride=10), :] = entry(2) + pltpu.roll(last, 1, 1)
    right[pl.ds(7, 100, stride=10), :] = entry(7) + pltpu.roll(first, LANES - 1, 1)
    right[pl.ds(8, 100, stride=10), :] = second_last + pltpu.roll(second, LANES - 1, 1)
    for a in range(10):
        for b in range(10):
            nodes = right[pl.ds(100 * a + 10 * b + 1, 8), :]
            folded[a, b] = nodes
            if b < 2:
                backward[a, b] = nodes
            if b > 7:
                forward[a, b - 8] = nodes
            if a < 2:
                rims[a, b] = nodes
            if a > 7:
                rims[a - 6, b] = nodes


def block_solve(field, low, high, below, above, table, valid, count, shared):
    row = jax.ShapeDtypeStruct((1, LANES), jnp.float32)
    edge = jax.ShapeDtypeStruct((10, 2, 8, LANES), jnp.float32)
    outs = [
        jax.ShapeDtypeStruct((10, 10, 8, LANES), jnp.float32),
        jax.ShapeDtypeStruct((4, 10, 8, LANES), jnp.float32),
        edge,
        edge,
        row,
    ]
    if shared:
        outs += [row, jax.ShapeDtypeStruct((512, LANES), jnp.float32)]
    return pl.pallas_call(
        functools.partial(solve_kernel, count, shared),
        out_shape=outs,
        scratch_shapes=[pltpu.VMEM((1040, LANES), jnp.float32)] * 3
        + [pltpu.VMEM((104, LANES), jnp.float32)],
        name="block_solve_shared" if shared else "block_solve_first",
    )(field, low, high, below, above, table, valid)


def folded_second(values, a, y, at, below, above):
    nodes = values[a, y + 1]
    if y < 2:
        nodes = nodes + below[at, y]
    if y > 5:
        nodes = nodes + above[at, y - 6]
    return nodes


def first_edges_kernel(rims, below, above, backward, forward):
    for a in range(2):
        for y in range(8):
            backward[a, y] = folded_second(rims, a, y, a, below, above)
            forward[a, y] = folded_second(rims, a + 2, y, a + 8, below, above)


def first_edges(rims, below, above):
    return pl.pallas_call(
        first_edges_kernel,
        out_shape=[jax.ShapeDtypeStruct((2, 8, 8, LANES), jnp.float32)] * 2,
        name="first_edges",
    )(rims, below, above)


def both_ways(nodes, metric, derivative):
    slopes = []
    for a in range(8):
        total = None
        for i in range(8):
            if derivative[a, i] != 0.0:
                term = float(derivative[a, i]) * nodes[i]
                total = term if total is None else total + term
        slopes.append(metric[a] * total)
    outs = []
    for i in range(8):
        total = None
        for a in range(8):
            if derivative[a, i] != 0.0:
                term = float(derivative[a, i]) * slopes[a]
                total = term if total is None else total + term
        outs.append(total)
    return outs


def to_lines(sources, count):
    lane = lax.broadcasted_iota(jnp.int32, (LANES, LANES), 0)
    place = lax.broadcasted_iota(jnp.int32, (LANES, LANES), 1)
    total = jnp.zeros((64 * len(sources), LANES), jnp.float32)
    for k in range(8):
        pick = (
            (place == 8 * (lane - REACH) + k) & (lane >= REACH) & (lane < REACH + count)
        ).astype(jnp.bfloat16)
        rest = jnp.concatenate([s[pl.ds(k, 64, stride=8), :] for s in sources], axis=0)
        rest = jnp.where(own_lanes(count), rest, 0.0)
        for _ in range(3):
            part = rest.astype(jnp.bfloat16)
            total = total + jnp.dot(part, pick, preferred_element_type=jnp.float32)
            rest = rest - part.astype(jnp.float32)
    return total


def in_parts(values):
    parts = []
    for _ in range(3):
        part = values.astype(jnp.bfloat16)
        parts.append(part)
        values = values - part.astype(jnp.float32)
    return parts


def spread_lines(lines, lane_of_element, out, base=None):
    count, length = lines.shape
    node = lax.broadcasted_iota(jnp.int32, (length, 2 * LANES), 0)
    place = lax.broadcasted_iota(jnp.int32, (length, 2 * LANES), 1)
    parts = in_parts(lines)
    for k in range(0, 8, 2):
        wanted = lane_of_element(node // 8) + LANES * (node % 8 - k)
        pick = ((node % 8 >= k) & (node % 8 < k + 2) & (place == wanted)).astype(jnp.bfloat16)
        total = None
        for part in parts:
            term = jnp.dot(part, pick, preferred_element_type=jnp.float32)
            total = term if total is None else total + term
        for half in range(2):
            value = total[:, half * LANES : (half + 1) * LANES]
            spot = pl.ds(k + half, count, stride=8)
            out[spot, :] = value if base is None else value + base[spot, :]


def own_lines_kernel(right_side, geometry, field, metric):
    spread_lines(right_side[...], lambda e: e + REACH, field)
    spread_lines(geometry[...], lambda e: e + REACH, metric)


def own_lines(right_side, geometry):
    return pl.pallas_call(
        own_lines_kernel,
        out_shape=[
            jax.ShapeDtypeStruct((512, LANES), jnp.float32),
            jax.ShapeDtypeStruct((2048, LANES), jnp.float32),
        ],
        name="own_lines",
    )(right_side, geometry)


def end_lines_kernel(count, with_edges, ends, own, out, *edges):
    spread_lines(ends[...], lambda e: jnp.where(e < REACH, e, e + count), out, own)
    if with_edges:
        backward, forward = edges
        for x in range(2):
            for y in range(8):
                backward[x, y] = out[pl.ds(64 * x + 8 * y, 8), :]
                forward[x, y] = out[pl.ds(64 * (6 + x) + 8 * y, 8), :]


def end_lines(ends, own, count, with_edges):
    outs = [jax.ShapeDtypeStruct(own.shape, jnp.float32)]
    if with_edges:
        outs += [jax.ShapeDtypeStruct((2, 8, 8, LANES), jnp.float32)] * 2
    return pl.pallas_call(
        functools.partial(end_lines_kernel, count, with_edges),
        out_shape=outs,
        name="end_lines_field" if with_edges else "end_lines_metric",
    )(ends, own)


def apply_local(derivative, folded, below, above, low, high, geometry, field, image):
    for x in range(8):
        for y in range(8):
            nodes = folded_second(folded, x + 1, y, x + 1, below, above)
            if x < 2:
                nodes = nodes + low[x, y]
            if x > 5:
                nodes = nodes + high[x - 6, y]
            field[pl.ds(64 * x + 8 * y, 8), :] = nodes
    for row in range(0, 512, 8):
        image[row : row + 8, :] = geometry[1536 + row : 1544 + row, :] * field[row : row + 8, :]
    for line in range(8):
        for dim in range(3):
            if dim == 0:
                spots = [pl.ds(64 * i + 8 * line, 8) for i in range(8)]
                places = spots
            elif dim == 1:
                spots = [pl.ds(64 * line + 8 * i, 8) for i in range(8)]
                places = [pl.ds(512 + 64 * line + 8 * i, 8) for i in range(8)]
            else:
                spots = [pl.ds(64 * line + i, 8, stride=8) for i in range(8)]
                places = [pl.ds(1024 + 64 * line + i, 8, stride=8) for i in range(8)]
            outs = both_ways(
                [field[s, :] for s in spots], [geometry[s, :] for s in places], derivative
            )
            for spot, out in zip(spots, outs):
                image[spot, :] = image[spot, :] + out


def first_operator_kernel(
    count, derivative, folded, below, above, low, high, geometry, field, image, backward, forward, inner
):
    apply_local(derivative, folded, below, above, low, high, geometry, field, image)
    total = jnp.zeros((8, LANES), jnp.float32)
    for row in range(0, 512, 8):
        total = total + field[row : row + 8, :] * image[row : row + 8, :]
    inner[...] = jnp.sum(jnp.where(own_lanes(count), total, 0.0), axis=0, keepdims=True)
    first = image[pl.ds(0, 64, stride=8), :]
    last = image[pl.ds(7, 64, stride=8), :]
    image[pl.ds(0, 64, stride=8), :] = first + pltpu.roll(last, 1, 1)
    image[pl.ds(7, 64, stride=8), :] = last + pltpu.roll(first, LANES - 1, 1)
    for x in range(2):
        for y in range(8):
            backward[x, y] = image[pl.ds(64 * x + 8 * y, 8), :]
            forward[x, y] = image[pl.ds(64 * (6 + x) + 8 * y, 8), :]


def first_operator(folded, below, above, low, high, geometry, count):
    full = jax.ShapeDtypeStruct((512, LANES), jnp.float32)
    edge = jax.ShapeDtypeStruct((2, 8, 8, LANES), jnp.float32)
    return pl.pallas_call(
        functools.partial(first_operator_kernel, count, derivative_table()),
        out_shape=[full, full, edge, edge, jax.ShapeDtypeStruct((1, LANES), jnp.float32)],
        name="first_operator",
    )(folded, below, above, low, high, geometry)


def second_operator_kernel(
    count,
    derivative,
    spot,
    folded,
    below,
    above,
    low,
    high,
    geometry,
    rho,
    d,
    g,
    size,
    lines,
    payload,
    field,
    image,
):
    apply_local(derivative, folded, below, above, low, high, geometry, field, image)
    largest = jnp.max(size[...])
    unit = 1.0 / jnp.where(largest > 0.0, largest, 1.0)
    own = own_lanes(count)
    total = jnp.zeros((8, LANES), jnp.float32)
    for row in range(0, 512, 8):
        total = total + (field[row : row + 8, :] * unit) * (image[row : row + 8, :] * unit)
    h = jnp.sum(jnp.where(own, total, 0.0))
    lane = lax.broadcasted_iota(jnp.int32, (1, LANES), 1)
    scalars = jnp.zeros((1, LANES), jnp.float32)
    sums = (jnp.sum(rho[...]), jnp.sum(d[...]), jnp.sum(g[...]), h, largest)
    for place, value in enumerate(sums):
        scalars = jnp.where(lane == 64 + place, value, scalars)
    both = to_lines([field, image], count)
    lines[...] = both
    line = lax.broadcasted_iota(jnp.int32, (64, LANES), 0)
    across = lax.broadcasted_iota(jnp.int32, (64, LANES), 1)
    first = jnp.sum(jnp.where(line == across, both[64:, 0:1], 0.0), axis=0, keepdims=True)
    last = jnp.sum(
        jnp.where(line == across, both[64:, LANES - 1 : LANES], 0.0), axis=0, keepdims=True
    )
    target = lax.broadcasted_iota(jnp.int32, payload.shape, 0)
    me = spot[2]
    payload[...] = scalars + jnp.where(
        target == me + 1, last, jnp.where(target == me - 1, first, 0.0)
    )


SMEM = pl.BlockSpec(memory_space=pltpu.SMEM)
VMEM = pl.BlockSpec(memory_space=pltpu.VMEM)


def second_operator(spot, folded, below, above, low, high, geometry, sums, count, devices):
    return pl.pallas_call(
        functools.partial(second_operator_kernel, count, derivative_table()),
        out_shape=[
            jax.ShapeDtypeStruct((128, LANES), jnp.float32),
            jax.ShapeDtypeStruct((devices, LANES), jnp.float32),
        ],
        in_specs=[SMEM] + [VMEM] * 10,
        out_specs=[VMEM, VMEM],
        scratch_shapes=[pltpu.VMEM((512, LANES), jnp.float32)] * 2,
        name="second_operator",
    )(spot, folded, below, above, low, high, geometry, *sums)


def lines_kernel(count, one, two, lines):
    lines[...] = to_lines([one, two], count)


def as_lines(one, two, count):
    return pl.pallas_call(
        functools.partial(lines_kernel, count),
        out_shape=jax.ShapeDtypeStruct((128, LANES), jnp.float32),
        name="as_lines",
    )(one, two)


def combine(columns):
    size = jnp.max(columns[4])
    ratio = columns[4] / jnp.where(size > 0.0, size, 1.0)
    factor = ratio * ratio
    return (
        jnp.sum(columns[0]),
        jnp.sum(columns[1]),
        jnp.sum(columns[2] * factor),
        jnp.sum(columns[3] * factor),
        size,
    )


NEIGHBOURS = [(dx, dy) for dx in (-1, 0, 1) for dy in (-1, 0, 1) if (dx, dy) != (0, 0)]


def middle_kernel(sizes, spot, gathered, lines, image, out):
    rows = gathered[...]
    values = combine([rows[:, 64 + i : 65 + i] for i in range(5)])
    source = lax.broadcasted_iota(jnp.int32, rows.shape, 0)
    before = jnp.sum(jnp.where(source == spot[2] - 1, rows, 0.0), axis=0, keepdims=True)
    after = jnp.sum(jnp.where(source == spot[2] + 1, rows, 0.0), axis=0, keepdims=True)
    line = lax.broadcasted_iota(jnp.int32, (64, LANES), 0)
    across = lax.broadcasted_iota(jnp.int32, (64, LANES), 1)
    before = jnp.sum(jnp.where(line == across, before, 0.0), axis=1, keepdims=True)
    after = jnp.sum(jnp.where(line == across, after, 0.0), axis=1, keepdims=True)
    t = lines[64:, :]
    behind = pltpu.roll(t, 1, 1)
    ahead = pltpu.roll(t, LANES - 1, 1)
    image[...] = t + jnp.where(
        across % 8 == 7,
        jnp.where(across == LANES - 1, after, ahead),
        jnp.where(across % 8 == 0, jnp.where(across == 0, before, behind), 0.0),
    )
    row = lax.broadcasted_iota(jnp.int32, (8, LANES), 0)
    lane = lax.broadcasted_iota(jnp.int32, (8, LANES), 1)
    scalars = jnp.zeros((8, LANES), jnp.float32)
    for place, value in enumerate(values):
        scalars = jnp.where(row == place, value, scalars)
    scalars = jnp.where(lane == 8, scalars, 0.0)
    for device in range(sizes[0] * sizes[1]):
        out[pl.ds(8 * device, 8), :] = scalars
    for dx, dy in NEIGHBOURS:
        x, y = spot[0] + dx, spot[1] + dy
        at_x, at_y = (7 if dx > 0 else 0), (7 if dy > 0 else 0)
        if dy == 0:
            face = image[pl.ds(8 * at_x, 8), :]
        elif dx == 0:
            face = image[pl.ds(at_y, 8, stride=8), :]
        else:
            face = jnp.broadcast_to(image[pl.ds(8 * at_x + at_y, 1), :], (8, LANES))
        tile = jnp.where(lane == 8, scalars, face)

        @pl.when((x >= 0) & (x < sizes[0]) & (y >= 0) & (y < sizes[1]))
        def _():
            out[pl.ds(pl.multiple_of(8 * (x * sizes[1] + y), 8), 8), :] = tile


def middle(spot, gathered, lines, sizes):
    return pl.pallas_call(
        functools.partial(middle_kernel, sizes),
        out_shape=[
            jax.ShapeDtypeStruct((64, LANES), jnp.float32),
            jax.ShapeDtypeStruct((8 * sizes[0] * sizes[1], LANES), jnp.float32),
        ],
        in_specs=[SMEM, VMEM, VMEM],
        out_specs=[VMEM, VMEM],
        name="middle",
    )(spot, gathered, lines)


def finish_kernel(
    sizes, spot, gathered, image, second, first, right_side, solution_out, residual_out, t
):
    plane = sizes[0] * sizes[1]
    columns = [gathered[pl.ds(i, plane, stride=8), :][:, 8:9] for i in range(5)]
    rho, d, g_scaled, h_scaled, size = combine(columns)
    t[...] = image[...]
    lane = lax.broadcasted_iota(jnp.int32, (8, LANES), 1)
    for dx, dy in NEIGHBOURS:
        x, y = spot[0] + dx, spot[1] + dy
        inside = (x >= 0) & (x < sizes[0]) & (y >= 0) & (y < sizes[1])
        source = jnp.where(inside, x * sizes[1] + y, 0)
        tile = gathered[pl.ds(pl.multiple_of(8 * source, 8), 8), :]
        tile = jnp.where(lane == 8, pltpu.roll(tile, 1, 1), tile)
        tile = jnp.where(inside, tile, 0.0)
        at_x, at_y = (7 if dx > 0 else 0), (7 if dy > 0 else 0)
        if dy == 0:
            spots = pl.ds(8 * at_x, 8)
        elif dx == 0:
            spots = pl.ds(at_y, 8, stride=8)
        else:
            spots = pl.ds(8 * at_x + at_y, 1)
            tile = tile[0:1, :]
        t[spots, :] = t[spots, :] + tile

    def splat(value):
        return jnp.full((1, LANES), value, jnp.float32)

    rho, d = splat(rho), splat(d)
    alpha_one = rho / d
    reach = alpha_one * splat(size)
    g = reach * reach * splat(g_scaled)
    h = reach * reach * splat(h_scaled)
    stretch = g / rho
    alpha_two = (g - rho) / (h - stretch * g / alpha_one)
    along = alpha_one + alpha_two * stretch
    turn = alpha_one * alpha_two
    solution_out[...] = along * first[0:64, :] - turn * second[0:64, :]
    residual_out[...] = right_side[...] - along * first[64:128, :] + turn * t[...]


def finish(spot, gathered, image, second, first, right_side, sizes):
    full = jax.ShapeDtypeStruct((64, LANES), jnp.float32)
    return pl.pallas_call(
        functools.partial(finish_kernel, sizes),
        out_shape=[full, full],
        in_specs=[SMEM] + [VMEM] * 5,
        out_specs=[VMEM, VMEM],
        scratch_shapes=[pltpu.VMEM((64, LANES), jnp.float32)],
        name="finish",
    )(spot, gathered, image, second, first, right_side)


def exchange(rows, axes):
    return lax.all_to_all(rows, axes, 0, 0, tiled=True)


def on_device(right_side, geometry, element_shape_class, fdm_vectors, fdm_values):
    count = element_shape_class.shape[2]
    classes = fdm_vectors.shape[0]
    depth = lax.axis_size("gz")
    sizes = (lax.axis_size("gx"), lax.axis_size("gy"))
    spot = jnp.stack([lax.axis_index(a).astype(jnp.int32) for a in ("gx", "gy", "gz")])
    ends = 8 * REACH
    lines = right_side.reshape(64, LANES)
    metric_lines = geometry.reshape(256, LANES)
    class_lines = jnp.broadcast_to(
        jnp.repeat(element_shape_class.reshape(1, -1), 8, axis=1).astype(jnp.float32),
        (8, 8 * count),
    )
    stack = jnp.concatenate([lines, class_lines, metric_lines], axis=0)
    low, high = swap(stack[:, :ends], stack[:, -ends:], "gz")
    own_field, own_metric = own_lines(lines, metric_lines)
    outer = jnp.concatenate([low, high], axis=1)
    deep_class = jnp.concatenate(
        [low[64, ::8], element_shape_class.reshape(-1).astype(jnp.float32), high[64, ::8]]
    ).astype(jnp.int32)
    deep_class = jnp.pad(deep_class, (0, LANES - deep_class.shape[0]))
    element = jnp.arange(LANES, dtype=jnp.int32) - REACH + spot[2] * count
    valid = ((element >= 0) & (element < depth * count)).astype(jnp.float32)[None, :]
    onehot = (jnp.arange(classes, dtype=jnp.int32)[:, None] == deep_class[None, :]).astype(
        jnp.float32
    )
    entries = jnp.concatenate(
        [fdm_vectors.reshape(classes, 300), fdm_values.reshape(classes, 30)], axis=1
    )
    table = lax.dot_general(
        entries, onehot, (((0,), (0,)), ((), ())), precision=HIGHEST
    )
    field, backward, forward = end_lines(outer[:64], own_field, count, True)
    low, high = swap(backward, forward, "gx")
    (metric,) = end_lines(outer[72:], own_metric, count, False)
    low, high, metric, table = lax.optimization_barrier((low, high, metric, table))
    below, above = swap(*second_edges(field, low, high, False), "gy")
    folded, rims, backward, forward, rho = block_solve(
        field, low, high, below, above, table, valid, count, False
    )
    below, above = swap(backward, forward, "gy")
    low, high = swap(*first_edges(rims, below, above), "gx")
    p, image, backward, forward, d = first_operator(
        folded, below, above, low, high, metric, count
    )
    low, high = swap(backward, forward, "gx")
    below, above = swap(*second_edges(image, low, high, True), "gy")
    folded, rims, backward, forward, g, size, q = block_solve(
        image, low, high, below, above, table, valid, count, True
    )
    below, above = swap(backward, forward, "gy")
    first = as_lines(p, q, count)
    below, above, first = lax.optimization_barrier((below, above, first))
    low, high = swap(*first_edges(rims, below, above), "gx")
    second, payload = second_operator(
        spot, folded, below, above, low, high, own_metric, (rho, d, g, size), count, depth
    )
    gathered = exchange(payload, "gz")
    image, tiles = middle(spot, gathered, second, sizes)
    gathered = exchange(tiles, ("gx", "gy"))
    answer, left = finish(spot, gathered, image, second, first, lines, sizes)
    return (answer.reshape(8, 8, LANES), left.reshape(8, 8, LANES))


def solution(mesh):
    placed = (P("gx", "gy", "gz"), P(None, "gx", "gy", "gz"), P("gx", "gy", "gz"), P(), P())
    return jax.shard_map(
        on_device,
        mesh=mesh,
        in_specs=placed,
        out_specs=(P("gx", "gy", "gz"), P("gx", "gy", "gz")),
        check_vma=False,
    )
```

```python
import functools

import jax
import jax.numpy as jnp
import numpy as np
from jax import lax
from jax.experimental import pallas as pl
from jax.experimental.pallas import tpu as pltpu
from jax.sharding import PartitionSpec as P

HIGHEST = lax.Precision.HIGHEST
LANES = 128
REACH = 4
SMEM = pl.BlockSpec(memory_space=pltpu.SMEM)
VMEM = pl.BlockSpec(memory_space=pltpu.VMEM)
CHUNKS = ((0, 24), (24, 24), (48, 24), (72, 28))


def swap(backward_part, forward_part, axis):
    count = lax.axis_size(axis)
    forward = [(i, i + 1) for i in range(count - 1)]
    backward = [(target, source) for source, target in forward]
    return lax.ppermute(forward_part, axis, forward), lax.ppermute(backward_part, axis, backward)


def derivative_table():
    points = np.array(
        [
            -1.0,
            -0.8717401485096066,
            -0.5917001814331423,
            -0.2092992179024789,
            0.2092992179024789,
            0.5917001814331423,
            0.8717401485096066,
            1.0,
        ]
    )
    previous = np.ones(8)
    current = points * 1.0
    for order in range(1, 7):
        following = ((2 * order + 1) * points * current - order * previous) / (order + 1)
        previous = current
        current = following
    spacing = points[:, None] - points[None, :] + np.eye(8)
    off_diagonal = current[:, None] / (current[None, :] * spacing)
    positions = np.arange(8)
    end_values = np.where(positions == 0, -14.0, 0.0) + np.where(positions == 7, 14.0, 0.0)
    return np.where(np.eye(8) > 0, np.eye(8) * end_values[None, :], off_diagonal)


def near(*arrays):
    return [pltpu.with_memory_space_constraint(array, pltpu.VMEM) for array in arrays]


def own_lanes(count):
    lane = lax.broadcasted_iota(jnp.int32, (1, LANES), 1)
    return (lane >= REACH) & (lane < REACH + count)


def solve_step(source, target, table, base, transposed, scale=None):
    for start, size in CHUNKS:
        entries = [source[pl.ds(10 * start + k, size, stride=10), :] for k in range(10)]
        for out in range(10):
            total = None
            for k in range(10):
                row = base + (10 * out + k if transposed else 10 * k + out)
                term = table[row : row + 1, :] * entries[k]
                total = term if total is None else total + term
            if scale is not None:
                total = total / (table[300 + out : 301 + out, :] + scale[start : start + size, :])
            target[pl.ds(100 * out + start, size), :] = total


def extended_first(a, y, field, low, high, shared):
    if a == 0:
        return low[0, y]
    if a == 9:
        return high[1, y]
    nodes = field[pl.ds(64 * (a - 1) + 8 * y, 8), :]
    if shared and a == 1:
        nodes = nodes + low[1, y]
    if shared and a == 8:
        nodes = nodes + high[0, y]
    return nodes


def second_edges_kernel(shared, field, low, high, backward, forward):
    for a in range(10):
        for y in range(2):
            backward[a, y] = extended_first(a, y, field, low, high, shared)
            forward[a, y] = extended_first(a, 6 + y, field, low, high, shared)


def second_edges(field, low, high, shared):
    return pl.pallas_call(
        functools.partial(second_edges_kernel, shared),
        out_shape=[pltpu.VMEM((10, 2, 8, LANES), jnp.float32)] * 2,
        in_specs=[VMEM] * 3,
        out_specs=[VMEM] * 2,
        name="second_edges",
    )(*near(field, low, high))


def solve_kernel(count, shared, field, low, high, below, above, table, valid, *refs):
    if shared:
        folded, rims, backward, forward, inner, size_row, assembled, blocks, left, right, pair = refs
    else:
        folded, rims, backward, forward, inner, blocks, left, right, pair = refs
    blocks[pl.ds(1000, 40), :] = jnp.zeros((40, LANES), jnp.float32)
    left[pl.ds(1000, 40), :] = jnp.zeros((40, LANES), jnp.float32)
    right[pl.ds(1000, 40), :] = jnp.zeros((40, LANES), jnp.float32)
    for a in range(10):
        for b in range(10):
            if b == 0:
                nodes = below[a, 0]
            elif b == 9:
                nodes = above[a, 1]
            else:
                nodes = extended_first(a, b - 1, field, low, high, shared)
                if shared and b == 1:
                    nodes = nodes + below[a, 1]
                if shared and b == 8:
                    nodes = nodes + above[a, 0]
                if shared and 1 <= a <= 8:
                    assembled[pl.ds(64 * (a - 1) + 8 * (b - 1), 8), :] = nodes
            blocks[pl.ds(100 * a + 10 * b + 1, 8), :] = nodes
    blocks[pl.ds(0, 100, stride=10), :] = pltpu.roll(
        blocks[pl.ds(7, 100, stride=10), :], 1, 1
    )
    blocks[pl.ds(9, 100, stride=10), :] = pltpu.roll(
        blocks[pl.ds(2, 100, stride=10), :], LANES - 1, 1
    )
    for n in range(10):
        pair[pl.ds(10 * n, 10), :] = table[310 + n : 311 + n, :] + table[320:330, :]
    solve_step(blocks, left, table, 200, False)
    solve_step(left, right, table, 100, False)
    solve_step(right, left, table, 0, False, pair)
    solve_step(left, right, table, 200, True)
    solve_step(right, left, table, 100, True)
    solve_step(left, right, table, 0, True)
    exists = valid[...] > 0.0
    own = own_lanes(count)
    unit = 1.0
    if shared:
        largest = jnp.zeros((8, LANES), jnp.float32)
        for row in range(0, 1000, 8):
            largest = jnp.maximum(largest, jnp.abs(blocks[row : row + 8, :]))
        size = jnp.max(jnp.where(own, largest, 0.0))
        unit = 1.0 / jnp.where(size > 0.0, size, 1.0)
        size_row[...] = jnp.full((1, LANES), size, jnp.float32)
    total = jnp.zeros((8, LANES), jnp.float32)
    for row in range(0, 1000, 8):
        total = total + (blocks[row : row + 8, :] * unit) * (right[row : row + 8, :] * unit)
    inner[...] = jnp.sum(jnp.where(own, total, 0.0), axis=0, keepdims=True)

    def entry(c):
        return jnp.where(exists, right[pl.ds(c, 100, stride=10), :], 0.0)

    first, second, second_last, last = entry(0), entry(1), entry(8), entry(9)
    right[pl.ds(1, 100, stride=10), :] = second + pltpu.roll(second_last, 1, 1)
    right[pl.ds(2, 100, stride=10), :] = entry(2) + pltpu.roll(last, 1, 1)
    right[pl.ds(7, 100, stride=10), :] = entry(7) + pltpu.roll(first, LANES - 1, 1)
    right[pl.ds(8, 100, stride=10), :] = second_last + pltpu.roll(second, LANES - 1, 1)
    for a in range(10):
        for b in range(10):
            nodes = right[pl.ds(100 * a + 10 * b + 1, 8), :]
            folded[a, b] = nodes
            if b < 2:
                backward[a, b] = nodes
            if b > 7:
                forward[a, b - 8] = nodes
            if a < 2:
                rims[a, b] = nodes
            if a > 7:
                rims[a - 6, b] = nodes


def block_solve(field, low, high, below, above, table, valid, count, shared):
    row = pltpu.VMEM((1, LANES), jnp.float32)
    edge = pltpu.VMEM((10, 2, 8, LANES), jnp.float32)
    outs = [
        pltpu.VMEM((10, 10, 8, LANES), jnp.float32),
        pltpu.VMEM((4, 10, 8, LANES), jnp.float32),
        edge,
        edge,
        row,
    ]
    if shared:
        outs += [row, pltpu.VMEM((512, LANES), jnp.float32)]
    return pl.pallas_call(
        functools.partial(solve_kernel, count, shared),
        out_shape=outs,
        scratch_shapes=[pltpu.VMEM((1040, LANES), jnp.float32)] * 3
        + [pltpu.VMEM((104, LANES), jnp.float32)],
        in_specs=[VMEM] * 7,
        out_specs=[VMEM] * len(outs),
        name="block_solve_shared" if shared else "block_solve_first",
    )(*near(field, low, high, below, above, table, valid))


def folded_second(values, a, y, at, below, above):
    nodes = values[a, y + 1]
    if y < 2:
        nodes = nodes + below[at, y]
    if y > 5:
        nodes = nodes + above[at, y - 6]
    return nodes


def first_edges_kernel(rims, below, above, backward, forward):
    for a in range(2):
        for y in range(8):
            backward[a, y] = folded_second(rims, a, y, a, below, above)
            forward[a, y] = folded_second(rims, a + 2, y, a + 8, below, above)


def first_edges(rims, below, above):
    return pl.pallas_call(
        first_edges_kernel,
        out_shape=[pltpu.VMEM((2, 8, 8, LANES), jnp.float32)] * 2,
        in_specs=[VMEM] * 3,
        out_specs=[VMEM] * 2,
        name="first_edges",
    )(*near(rims, below, above))


def both_ways(nodes, metric, derivative):
    slopes = []
    for a in range(8):
        total = None
        for i in range(8):
            if derivative[a, i] != 0.0:
                term = float(derivative[a, i]) * nodes[i]
                total = term if total is None else total + term
        slopes.append(metric[a] * total)
    outs = []
    for i in range(8):
        total = None
        for a in range(8):
            if derivative[a, i] != 0.0:
                term = float(derivative[a, i]) * slopes[a]
                total = term if total is None else total + term
        outs.append(total)
    return outs


def to_lines(sources, count):
    lane = lax.broadcasted_iota(jnp.int32, (LANES, LANES), 0)
    place = lax.broadcasted_iota(jnp.int32, (LANES, LANES), 1)
    total = jnp.zeros((64 * len(sources), LANES), jnp.float32)
    for k in range(8):
        pick = (
            (place == 8 * (lane - REACH) + k) & (lane >= REACH) & (lane < REACH + count)
        ).astype(jnp.bfloat16)
        rest = jnp.concatenate([s[pl.ds(k, 64, stride=8), :] for s in sources], axis=0)
        rest = jnp.where(own_lanes(count), rest, 0.0)
        for _ in range(3):
            part = rest.astype(jnp.bfloat16)
            total = total + jnp.dot(part, pick, preferred_element_type=jnp.float32)
            rest = rest - part.astype(jnp.float32)
    return total


def in_parts(values):
    parts = []
    for _ in range(3):
        part = values.astype(jnp.bfloat16)
        parts.append(part)
        values = values - part.astype(jnp.float32)
    return parts


def spread_lines(lines, lane_of_element, out, base=None):
    count, length = lines.shape
    node = lax.broadcasted_iota(jnp.int32, (length, 2 * LANES), 0)
    place = lax.broadcasted_iota(jnp.int32, (length, 2 * LANES), 1)
    parts = in_parts(lines)
    for k in range(0, 8, 2):
        wanted = lane_of_element(node // 8) + LANES * (node % 8 - k)
        pick = ((node % 8 >= k) & (node % 8 < k + 2) & (place == wanted)).astype(jnp.bfloat16)
        total = None
        for part in parts:
            term = jnp.dot(part, pick, preferred_element_type=jnp.float32)
            total = term if total is None else total + term
        for half in range(2):
            value = total[:, half * LANES : (half + 1) * LANES]
            spot = pl.ds(k + half, count, stride=8)
            out[spot, :] = value if base is None else value + base[spot, :]


def own_lines_kernel(right_side, geometry, field, metric):
    spread_lines(right_side[...], lambda e: e + REACH, field)
    spread_lines(geometry[...], lambda e: e + REACH, metric)


def own_lines(right_side, geometry):
    return pl.pallas_call(
        own_lines_kernel,
        out_shape=[
            pltpu.VMEM((512, LANES), jnp.float32),
            pltpu.VMEM((2048, LANES), jnp.float32),
        ],
        in_specs=[VMEM] * 2,
        out_specs=[VMEM] * 2,
        name="own_lines",
    )(*near(right_side, geometry))


def end_lines_kernel(count, with_edges, ends, own, out, *edges):
    spread_lines(ends[...], lambda e: jnp.where(e < REACH, e, e + count), out, own)
    if with_edges:
        backward, forward = edges
        for x in range(2):
            for y in range(8):
                backward[x, y] = out[pl.ds(64 * x + 8 * y, 8), :]
                forward[x, y] = out[pl.ds(64 * (6 + x) + 8 * y, 8), :]


def end_lines(ends, own, count, with_edges):
    outs = [pltpu.VMEM(own.shape, jnp.float32)]
    if with_edges:
        outs += [pltpu.VMEM((2, 8, 8, LANES), jnp.float32)] * 2
    return pl.pallas_call(
        functools.partial(end_lines_kernel, count, with_edges),
        out_shape=outs,
        in_specs=[VMEM] * 2,
        out_specs=[VMEM] * len(outs),
        name="end_lines_field" if with_edges else "end_lines_metric",
    )(*near(ends, own))


def apply_local(derivative, folded, below, above, low, high, geometry, field, image):
    for x in range(8):
        for y in range(8):
            nodes = folded_second(folded, x + 1, y, x + 1, below, above)
            if x < 2:
                nodes = nodes + low[x, y]
            if x > 5:
                nodes = nodes + high[x - 6, y]
            field[pl.ds(64 * x + 8 * y, 8), :] = nodes
    for row in range(0, 512, 8):
        image[row : row + 8, :] = geometry[1536 + row : 1544 + row, :] * field[row : row + 8, :]
    for line in range(8):
        for dim in range(3):
            if dim == 0:
                spots = [pl.ds(64 * i + 8 * line, 8) for i in range(8)]
                places = spots
            elif dim == 1:
                spots = [pl.ds(64 * line + 8 * i, 8) for i in range(8)]
                places = [pl.ds(512 + 64 * line + 8 * i, 8) for i in range(8)]
            else:
                spots = [pl.ds(64 * line + i, 8, stride=8) for i in range(8)]
                places = [pl.ds(1024 + 64 * line + i, 8, stride=8) for i in range(8)]
            outs = both_ways(
                [field[s, :] for s in spots], [geometry[s, :] for s in places], derivative
            )
            for spot, out in zip(spots, outs):
                image[spot, :] = image[spot, :] + out


def first_operator_kernel(
    count, derivative, folded, below, above, low, high, geometry, field, image, backward, forward, inner
):
    apply_local(derivative, folded, below, above, low, high, geometry, field, image)
    total = jnp.zeros((8, LANES), jnp.float32)
    for row in range(0, 512, 8):
        total = total + field[row : row + 8, :] * image[row : row + 8, :]
    inner[...] = jnp.sum(jnp.where(own_lanes(count), total, 0.0), axis=0, keepdims=True)
    first = image[pl.ds(0, 64, stride=8), :]
    last = image[pl.ds(7, 64, stride=8), :]
    image[pl.ds(0, 64, stride=8), :] = first + pltpu.roll(last, 1, 1)
    image[pl.ds(7, 64, stride=8), :] = last + pltpu.roll(first, LANES - 1, 1)
    for x in range(2):
        for y in range(8):
            backward[x, y] = image[pl.ds(64 * x + 8 * y, 8), :]
            forward[x, y] = image[pl.ds(64 * (6 + x) + 8 * y, 8), :]


def first_operator(folded, below, above, low, high, geometry, count):
    full = pltpu.VMEM((512, LANES), jnp.float32)
    edge = pltpu.VMEM((2, 8, 8, LANES), jnp.float32)
    return pl.pallas_call(
        functools.partial(first_operator_kernel, count, derivative_table()),
        out_shape=[full, full, edge, edge, pltpu.VMEM((1, LANES), jnp.float32)],
        in_specs=[VMEM] * 6,
        out_specs=[VMEM] * 5,
        name="first_operator",
    )(*near(folded, below, above, low, high, geometry))


def second_operator_kernel(
    count,
    derivative,
    spot,
    folded,
    below,
    above,
    low,
    high,
    geometry,
    rho,
    d,
    g,
    size,
    lines,
    payload,
    field,
    image,
):
    apply_local(derivative, folded, below, above, low, high, geometry, field, image)
    largest = jnp.max(size[...])
    unit = 1.0 / jnp.where(largest > 0.0, largest, 1.0)
    own = own_lanes(count)
    total = jnp.zeros((8, LANES), jnp.float32)
    for row in range(0, 512, 8):
        total = total + (field[row : row + 8, :] * unit) * (image[row : row + 8, :] * unit)
    h = jnp.sum(jnp.where(own, total, 0.0))
    lane = lax.broadcasted_iota(jnp.int32, (1, LANES), 1)
    scalars = jnp.zeros((1, LANES), jnp.float32)
    sums = (jnp.sum(rho[...]), jnp.sum(d[...]), jnp.sum(g[...]), h, largest)
    for place, value in enumerate(sums):
        scalars = jnp.where(lane == 64 + place, value, scalars)
    both = to_lines([field, image], count)
    lines[...] = both
    line = lax.broadcasted_iota(jnp.int32, (64, LANES), 0)
    across = lax.broadcasted_iota(jnp.int32, (64, LANES), 1)
    first = jnp.sum(jnp.where(line == across, both[64:, 0:1], 0.0), axis=0, keepdims=True)
    last = jnp.sum(
        jnp.where(line == across, both[64:, LANES - 1 : LANES], 0.0), axis=0, keepdims=True
    )
    for target in range(payload.shape[0]):
        end = jnp.where(target == spot[2] + 1, last, jnp.where(target == spot[2] - 1, first, 0.0))
        payload[target] = scalars + end


def second_operator(spot, folded, below, above, low, high, geometry, sums, count, devices):
    return pl.pallas_call(
        functools.partial(second_operator_kernel, count, derivative_table()),
        out_shape=[
            pltpu.VMEM((128, LANES), jnp.float32),
            pltpu.VMEM((devices, 1, LANES), jnp.float32),
        ],
        in_specs=[SMEM] + [VMEM] * 10,
        out_specs=[VMEM, VMEM],
        scratch_shapes=[pltpu.VMEM((512, LANES), jnp.float32)] * 2,
        name="second_operator",
    )(spot, *near(folded, below, above, low, high, geometry, *sums))


def lines_kernel(count, one, two, lines):
    lines[...] = to_lines([one, two], count)


def as_lines(one, two, count):
    return pl.pallas_call(
        functools.partial(lines_kernel, count),
        out_shape=pltpu.VMEM((128, LANES), jnp.float32),
        in_specs=[VMEM] * 2,
        out_specs=VMEM,
        name="as_lines",
    )(*near(one, two))


def combine(columns):
    size = jnp.max(columns[4])
    ratio = columns[4] / jnp.where(size > 0.0, size, 1.0)
    factor = ratio * ratio
    return (
        jnp.sum(columns[0]),
        jnp.sum(columns[1]),
        jnp.sum(columns[2] * factor),
        jnp.sum(columns[3] * factor),
        size,
    )


NEIGHBOURS = [(dx, dy) for dx in (-1, 0, 1) for dy in (-1, 0, 1) if (dx, dy) != (0, 0)]


def middle_kernel(sizes, spot, gathered, lines, image, out, joined):
    for device in range(gathered.shape[0]):
        joined[pl.ds(device, 1), :] = gathered[device]
    rows = joined[...]
    values = combine([rows[:, 64 + i : 65 + i] for i in range(5)])
    source = lax.broadcasted_iota(jnp.int32, rows.shape, 0)
    before = jnp.sum(jnp.where(source == spot[2] - 1, rows, 0.0), axis=0, keepdims=True)
    after = jnp.sum(jnp.where(source == spot[2] + 1, rows, 0.0), axis=0, keepdims=True)
    line = lax.broadcasted_iota(jnp.int32, (64, LANES), 0)
    across = lax.broadcasted_iota(jnp.int32, (64, LANES), 1)
    before = jnp.sum(jnp.where(line == across, before, 0.0), axis=1, keepdims=True)
    after = jnp.sum(jnp.where(line == across, after, 0.0), axis=1, keepdims=True)
    t = lines[64:, :]
    behind = pltpu.roll(t, 1, 1)
    ahead = pltpu.roll(t, LANES - 1, 1)
    image[...] = t + jnp.where(
        across % 8 == 7,
        jnp.where(across == LANES - 1, after, ahead),
        jnp.where(across % 8 == 0, jnp.where(across == 0, before, behind), 0.0),
    )
    row = lax.broadcasted_iota(jnp.int32, (8, LANES), 0)
    lane = lax.broadcasted_iota(jnp.int32, (8, LANES), 1)
    scalars = jnp.zeros((8, LANES), jnp.float32)
    for place, value in enumerate(values):
        scalars = jnp.where(row == place, value, scalars)
    scalars = jnp.where(lane == 8, scalars, 0.0)
    for device in range(sizes[0] * sizes[1]):
        out[pl.ds(8 * device, 8), :] = scalars
    for dx, dy in NEIGHBOURS:
        x, y = spot[0] + dx, spot[1] + dy
        at_x, at_y = (7 if dx > 0 else 0), (7 if dy > 0 else 0)
        if dy == 0:
            face = image[pl.ds(8 * at_x, 8), :]
        elif dx == 0:
            face = image[pl.ds(at_y, 8, stride=8), :]
        else:
            face = jnp.broadcast_to(image[pl.ds(8 * at_x + at_y, 1), :], (8, LANES))
        tile = jnp.where(lane == 8, scalars, face)

        @pl.when((x >= 0) & (x < sizes[0]) & (y >= 0) & (y < sizes[1]))
        def _():
            out[pl.ds(pl.multiple_of(8 * (x * sizes[1] + y), 8), 8), :] = tile


def middle(spot, gathered, lines, sizes):
    return pl.pallas_call(
        functools.partial(middle_kernel, sizes),
        out_shape=[
            pltpu.VMEM((64, LANES), jnp.float32),
            pltpu.VMEM((8 * sizes[0] * sizes[1], LANES), jnp.float32),
        ],
        in_specs=[SMEM, VMEM, VMEM],
        out_specs=[VMEM, VMEM],
        scratch_shapes=[pltpu.VMEM((gathered.shape[0], LANES), jnp.float32)],
        name="middle",
    )(spot, *near(gathered, lines))


def finish_kernel(
    sizes, spot, gathered, image, second, first, right_side, solution_out, residual_out, t
):
    plane = sizes[0] * sizes[1]
    columns = [gathered[pl.ds(i, plane, stride=8), :][:, 8:9] for i in range(5)]
    rho, d, g_scaled, h_scaled, size = combine(columns)
    t[...] = image[...]
    lane = lax.broadcasted_iota(jnp.int32, (8, LANES), 1)
    for dx, dy in NEIGHBOURS:
        x, y = spot[0] + dx, spot[1] + dy
        inside = (x >= 0) & (x < sizes[0]) & (y >= 0) & (y < sizes[1])
        source = jnp.where(inside, x * sizes[1] + y, 0)
        tile = gathered[pl.ds(pl.multiple_of(8 * source, 8), 8), :]
        tile = jnp.where(lane == 8, pltpu.roll(tile, 1, 1), tile)
        tile = jnp.where(inside, tile, 0.0)
        at_x, at_y = (7 if dx > 0 else 0), (7 if dy > 0 else 0)
        if dy == 0:
            spots = pl.ds(8 * at_x, 8)
        elif dx == 0:
            spots = pl.ds(at_y, 8, stride=8)
        else:
            spots = pl.ds(8 * at_x + at_y, 1)
            tile = tile[0:1, :]
        t[spots, :] = t[spots, :] + tile

    def splat(value):
        return jnp.full((1, LANES), value, jnp.float32)

    rho, d = splat(rho), splat(d)
    alpha_one = rho / d
    reach = alpha_one * splat(size)
    g = reach * reach * splat(g_scaled)
    h = reach * reach * splat(h_scaled)
    stretch = g / rho
    alpha_two = (g - rho) / (h - stretch * g / alpha_one)
    along = alpha_one + alpha_two * stretch
    turn = alpha_one * alpha_two
    solution_out[...] = along * first[0:64, :] - turn * second[0:64, :]
    residual_out[...] = right_side[...] - along * first[64:128, :] + turn * t[...]


def finish(spot, gathered, image, second, first, right_side, sizes):
    full = jax.ShapeDtypeStruct((64, LANES), jnp.float32)
    return pl.pallas_call(
        functools.partial(finish_kernel, sizes),
        out_shape=[full, full],
        in_specs=[SMEM] + [VMEM] * 5,
        out_specs=[VMEM, VMEM],
        scratch_shapes=[pltpu.VMEM((64, LANES), jnp.float32)],
        name="finish",
    )(spot, *near(gathered, image, second, first, right_side))


def exchange(rows, axes):
    return lax.all_to_all(rows, axes, 0, 0, tiled=True)


def on_device(right_side, geometry, element_shape_class, fdm_vectors, fdm_values):
    count = element_shape_class.shape[2]
    classes = fdm_vectors.shape[0]
    depth = lax.axis_size("gz")
    sizes = (lax.axis_size("gx"), lax.axis_size("gy"))
    spot = jnp.stack([lax.axis_index(a).astype(jnp.int32) for a in ("gx", "gy", "gz")])
    ends = 8 * REACH
    lines = right_side.reshape(64, LANES)
    metric_lines = geometry.reshape(256, LANES)
    class_lines = jnp.broadcast_to(
        jnp.repeat(element_shape_class.reshape(1, -1), 8, axis=1).astype(jnp.float32),
        (8, 8 * count),
    )
    stack = jnp.concatenate([lines, class_lines, metric_lines], axis=0)
    low, high = swap(stack[:, :ends], stack[:, -ends:], "gz")
    own_field, own_metric = own_lines(lines, metric_lines)
    outer = jnp.concatenate([low, high], axis=1)
    deep_class = jnp.concatenate(
        [low[64, ::8], element_shape_class.reshape(-1).astype(jnp.float32), high[64, ::8]]
    ).astype(jnp.int32)
    deep_class = jnp.pad(deep_class, (0, LANES - deep_class.shape[0]))
    element = jnp.arange(LANES, dtype=jnp.int32) - REACH + spot[2] * count
    valid = ((element >= 0) & (element < depth * count)).astype(jnp.float32)[None, :]
    onehot = (jnp.arange(classes, dtype=jnp.int32)[:, None] == deep_class[None, :]).astype(
        jnp.float32
    )
    entries = jnp.concatenate(
        [fdm_vectors.reshape(classes, 300), fdm_values.reshape(classes, 30)], axis=1
    )
    table = lax.dot_general(
        entries, onehot, (((0,), (0,)), ((), ())), precision=HIGHEST
    )
    field, backward, forward = end_lines(outer[:64], own_field, count, True)
    low, high = swap(backward, forward, "gx")
    (metric,) = end_lines(outer[72:], own_metric, count, False)
    low, high, metric, table = lax.optimization_barrier((low, high, metric, table))
    below, above = swap(*second_edges(field, low, high, False), "gy")
    folded, rims, backward, forward, rho = block_solve(
        field, low, high, below, above, table, valid, count, False
    )
    below, above = swap(backward, forward, "gy")
    low, high = swap(*first_edges(rims, below, above), "gx")
    p, image, backward, forward, d = first_operator(
        folded, below, above, low, high, metric, count
    )
    low, high = swap(backward, forward, "gx")
    below, above = swap(*second_edges(image, low, high, True), "gy")
    folded, rims, backward, forward, g, size, q = block_solve(
        image, low, high, below, above, table, valid, count, True
    )
    below, above = swap(backward, forward, "gy")
    first = as_lines(p, q, count)
    below, above, first = lax.optimization_barrier((below, above, first))
    low, high = swap(*first_edges(rims, below, above), "gx")
    second, payload = second_operator(
        spot, folded, below, above, low, high, own_metric, (rho, d, g, size), count, depth
    )
    gathered = exchange(payload, "gz")
    image, tiles = middle(spot, gathered, second, sizes)
    gathered = exchange(tiles, ("gx", "gy"))
    answer, left = finish(spot, gathered, image, second, first, lines, sizes)
    return (answer.reshape(8, 8, LANES), left.reshape(8, 8, LANES))


def solution(mesh):
    placed = (P("gx", "gy", "gz"), P(None, "gx", "gy", "gz"), P("gx", "gy", "gz"), P(), P())
    return jax.shard_map(
        on_device,
        mesh=mesh,
        in_specs=placed,
        out_specs=(P("gx", "gy", "gz"), P("gx", "gy", "gz")),
        check_vma=False,
    )
```

```python
import functools

import jax
import jax.numpy as jnp
import numpy as np
from jax import lax
from jax.experimental import pallas as pl
from jax.experimental.pallas import tpu as pltpu
from jax.sharding import PartitionSpec as P

HIGHEST = lax.Precision.HIGHEST
LANES = 128
REACH = 4
SMEM = pl.BlockSpec(memory_space=pltpu.SMEM)
VMEM = pl.BlockSpec(memory_space=pltpu.VMEM)
ROOM = pltpu.CompilerParams(vmem_limit_bytes=8 << 20)
CHUNKS = ((0, 24), (24, 24), (48, 24), (72, 28))


def swap(backward_part, forward_part, axis):
    count = lax.axis_size(axis)
    forward = [(i, i + 1) for i in range(count - 1)]
    backward = [(target, source) for source, target in forward]
    return lax.ppermute(forward_part, axis, forward), lax.ppermute(backward_part, axis, backward)


def derivative_table():
    points = np.array(
        [
            -1.0,
            -0.8717401485096066,
            -0.5917001814331423,
            -0.2092992179024789,
            0.2092992179024789,
            0.5917001814331423,
            0.8717401485096066,
            1.0,
        ]
    )
    previous = np.ones(8)
    current = points * 1.0
    for order in range(1, 7):
        following = ((2 * order + 1) * points * current - order * previous) / (order + 1)
        previous = current
        current = following
    spacing = points[:, None] - points[None, :] + np.eye(8)
    off_diagonal = current[:, None] / (current[None, :] * spacing)
    positions = np.arange(8)
    end_values = np.where(positions == 0, -14.0, 0.0) + np.where(positions == 7, 14.0, 0.0)
    return np.where(np.eye(8) > 0, np.eye(8) * end_values[None, :], off_diagonal)


def near(*arrays):
    return [pltpu.with_memory_space_constraint(array, pltpu.VMEM) for array in arrays]


def own_lanes(count):
    lane = lax.broadcasted_iota(jnp.int32, (1, LANES), 1)
    return (lane >= REACH) & (lane < REACH + count)


def solve_step(source, target, table, base, transposed, scale=None):
    for start, size in CHUNKS:
        entries = [source[pl.ds(10 * start + k, size, stride=10), :] for k in range(10)]
        for out in range(10):
            total = None
            for k in range(10):
                row = base + (10 * out + k if transposed else 10 * k + out)
                term = table[row : row + 1, :] * entries[k]
                total = term if total is None else total + term
            if scale is not None:
                total = total / (table[300 + out : 301 + out, :] + scale[start : start + size, :])
            target[pl.ds(100 * out + start, size), :] = total


def extended_first(a, y, field, low, high, shared):
    if a == 0:
        return low[0, y]
    if a == 9:
        return high[1, y]
    nodes = field[pl.ds(64 * (a - 1) + 8 * y, 8), :]
    if shared and a == 1:
        nodes = nodes + low[1, y]
    if shared and a == 8:
        nodes = nodes + high[0, y]
    return nodes


def second_edges_kernel(shared, field, low, high, backward, forward):
    for a in range(10):
        for y in range(2):
            backward[a, y] = extended_first(a, y, field, low, high, shared)
            forward[a, y] = extended_first(a, 6 + y, field, low, high, shared)


def second_edges(field, low, high, shared):
    return pl.pallas_call(
        functools.partial(second_edges_kernel, shared),
        out_shape=[pltpu.VMEM((10, 2, 8, LANES), jnp.float32)] * 2,
        in_specs=[VMEM] * 3,
        out_specs=[VMEM] * 2,
        compiler_params=ROOM,
        name="second_edges",
    )(*near(field, low, high))


def solve_kernel(count, shared, field, low, high, below, above, table, valid, *refs):
    if shared:
        folded, rims, backward, forward, inner, size_row, assembled, blocks, left, right, pair = refs
    else:
        folded, rims, backward, forward, inner, blocks, left, right, pair = refs
    blocks[pl.ds(1000, 40), :] = jnp.zeros((40, LANES), jnp.float32)
    left[pl.ds(1000, 40), :] = jnp.zeros((40, LANES), jnp.float32)
    right[pl.ds(1000, 40), :] = jnp.zeros((40, LANES), jnp.float32)
    for a in range(10):
        for b in range(10):
            if b == 0:
                nodes = below[a, 0]
            elif b == 9:
                nodes = above[a, 1]
            else:
                nodes = extended_first(a, b - 1, field, low, high, shared)
                if shared and b == 1:
                    nodes = nodes + below[a, 1]
                if shared and b == 8:
                    nodes = nodes + above[a, 0]
                if shared and 1 <= a <= 8:
                    assembled[pl.ds(64 * (a - 1) + 8 * (b - 1), 8), :] = nodes
            blocks[pl.ds(100 * a + 10 * b + 1, 8), :] = nodes
    blocks[pl.ds(0, 100, stride=10), :] = pltpu.roll(
        blocks[pl.ds(7, 100, stride=10), :], 1, 1
    )
    blocks[pl.ds(9, 100, stride=10), :] = pltpu.roll(
        blocks[pl.ds(2, 100, stride=10), :], LANES - 1, 1
    )
    for n in range(10):
        pair[pl.ds(10 * n, 10), :] = table[310 + n : 311 + n, :] + table[320:330, :]
    solve_step(blocks, left, table, 200, False)
    solve_step(left, right, table, 100, False)
    solve_step(right, left, table, 0, False, pair)
    solve_step(left, right, table, 200, True)
    solve_step(right, left, table, 100, True)
    solve_step(left, right, table, 0, True)
    exists = valid[...] > 0.0
    own = own_lanes(count)
    unit = 1.0
    if shared:
        largest = jnp.zeros((8, LANES), jnp.float32)
        for row in range(0, 1000, 8):
            largest = jnp.maximum(largest, jnp.abs(blocks[row : row + 8, :]))
        size = jnp.max(jnp.where(own, largest, 0.0))
        unit = 1.0 / jnp.where(size > 0.0, size, 1.0)
        size_row[...] = jnp.full((1, LANES), size, jnp.float32)
    total = jnp.zeros((8, LANES), jnp.float32)
    for row in range(0, 1000, 8):
        total = total + (blocks[row : row + 8, :] * unit) * (right[row : row + 8, :] * unit)
    inner[...] = jnp.sum(jnp.where(own, total, 0.0), axis=0, keepdims=True)

    def entry(c):
        return jnp.where(exists, right[pl.ds(c, 100, stride=10), :], 0.0)

    first, second, second_last, last = entry(0), entry(1), entry(8), entry(9)
    right[pl.ds(1, 100, stride=10), :] = second + pltpu.roll(second_last, 1, 1)
    right[pl.ds(2, 100, stride=10), :] = entry(2) + pltpu.roll(last, 1, 1)
    right[pl.ds(7, 100, stride=10), :] = entry(7) + pltpu.roll(first, LANES - 1, 1)
    right[pl.ds(8, 100, stride=10), :] = second_last + pltpu.roll(second, LANES - 1, 1)
    for a in range(10):
        for b in range(10):
            nodes = right[pl.ds(100 * a + 10 * b + 1, 8), :]
            folded[a, b] = nodes
            if b < 2:
                backward[a, b] = nodes
            if b > 7:
                forward[a, b - 8] = nodes
            if a < 2:
                rims[a, b] = nodes
            if a > 7:
                rims[a - 6, b] = nodes


def block_solve(field, low, high, below, above, table, valid, count, shared):
    row = pltpu.VMEM((1, LANES), jnp.float32)
    edge = pltpu.VMEM((10, 2, 8, LANES), jnp.float32)
    outs = [
        pltpu.VMEM((10, 10, 8, LANES), jnp.float32),
        pltpu.VMEM((4, 10, 8, LANES), jnp.float32),
        edge,
        edge,
        row,
    ]
    if shared:
        outs += [row, pltpu.VMEM((512, LANES), jnp.float32)]
    return pl.pallas_call(
        functools.partial(solve_kernel, count, shared),
        out_shape=outs,
        scratch_shapes=[pltpu.VMEM((1040, LANES), jnp.float32)] * 3
        + [pltpu.VMEM((104, LANES), jnp.float32)],
        in_specs=[VMEM] * 7,
        out_specs=[VMEM] * len(outs),
        compiler_params=ROOM,
        name="block_solve_shared" if shared else "block_solve_first",
    )(*near(field, low, high, below, above, table, valid))


def folded_second(values, a, y, at, below, above):
    nodes = values[a, y + 1]
    if y < 2:
        nodes = nodes + below[at, y]
    if y > 5:
        nodes = nodes + above[at, y - 6]
    return nodes


def first_edges_kernel(rims, below, above, backward, forward):
    for a in range(2):
        for y in range(8):
            backward[a, y] = folded_second(rims, a, y, a, below, above)
            forward[a, y] = folded_second(rims, a + 2, y, a + 8, below, above)


def first_edges(rims, below, above):
    return pl.pallas_call(
        first_edges_kernel,
        out_shape=[pltpu.VMEM((2, 8, 8, LANES), jnp.float32)] * 2,
        in_specs=[VMEM] * 3,
        out_specs=[VMEM] * 2,
        compiler_params=ROOM,
        name="first_edges",
    )(*near(rims, below, above))


def both_ways(nodes, metric, derivative):
    slopes = []
    for a in range(8):
        total = None
        for i in range(8):
            if derivative[a, i] != 0.0:
                term = float(derivative[a, i]) * nodes[i]
                total = term if total is None else total + term
        slopes.append(metric[a] * total)
    outs = []
    for i in range(8):
        total = None
        for a in range(8):
            if derivative[a, i] != 0.0:
                term = float(derivative[a, i]) * slopes[a]
                total = term if total is None else total + term
        outs.append(total)
    return outs


def to_lines(sources, count):
    lane = lax.broadcasted_iota(jnp.int32, (LANES, LANES), 0)
    place = lax.broadcasted_iota(jnp.int32, (LANES, LANES), 1)
    total = jnp.zeros((64 * len(sources), LANES), jnp.float32)
    for k in range(8):
        pick = (
            (place == 8 * (lane - REACH) + k) & (lane >= REACH) & (lane < REACH + count)
        ).astype(jnp.bfloat16)
        rest = jnp.concatenate([s[pl.ds(k, 64, stride=8), :] for s in sources], axis=0)
        rest = jnp.where(own_lanes(count), rest, 0.0)
        for _ in range(3):
            part = rest.astype(jnp.bfloat16)
            total = total + jnp.dot(part, pick, preferred_element_type=jnp.float32)
            rest = rest - part.astype(jnp.float32)
    return total


def in_parts(values):
    parts = []
    for _ in range(3):
        part = values.astype(jnp.bfloat16)
        parts.append(part)
        values = values - part.astype(jnp.float32)
    return parts


def spread_lines(lines, lane_of_element, out, base=None):
    count, length = lines.shape
    node = lax.broadcasted_iota(jnp.int32, (length, 2 * LANES), 0)
    place = lax.broadcasted_iota(jnp.int32, (length, 2 * LANES), 1)
    parts = in_parts(lines)
    for k in range(0, 8, 2):
        wanted = lane_of_element(node // 8) + LANES * (node % 8 - k)
        pick = ((node % 8 >= k) & (node % 8 < k + 2) & (place == wanted)).astype(jnp.bfloat16)
        total = None
        for part in parts:
            term = jnp.dot(part, pick, preferred_element_type=jnp.float32)
            total = term if total is None else total + term
        for half in range(2):
            value = total[:, half * LANES : (half + 1) * LANES]
            spot = pl.ds(k + half, count, stride=8)
            out[spot, :] = value if base is None else value + base[spot, :]


def own_lines_kernel(right_side, geometry, field, metric):
    spread_lines(right_side[...], lambda e: e + REACH, field)
    spread_lines(geometry[...], lambda e: e + REACH, metric)


def own_lines(right_side, geometry):
    return pl.pallas_call(
        own_lines_kernel,
        out_shape=[
            pltpu.VMEM((512, LANES), jnp.float32),
            pltpu.VMEM((2048, LANES), jnp.float32),
        ],
        in_specs=[VMEM] * 2,
        out_specs=[VMEM] * 2,
        compiler_params=ROOM,
        name="own_lines",
    )(*near(right_side, geometry))


def end_lines_kernel(count, with_edges, ends, own, out, *edges):
    spread_lines(ends[...], lambda e: jnp.where(e < REACH, e, e + count), out, own)
    if with_edges:
        backward, forward = edges
        for x in range(2):
            for y in range(8):
                backward[x, y] = out[pl.ds(64 * x + 8 * y, 8), :]
                forward[x, y] = out[pl.ds(64 * (6 + x) + 8 * y, 8), :]


def end_lines(ends, own, count, with_edges):
    outs = [pltpu.VMEM(own.shape, jnp.float32)]
    if with_edges:
        outs += [pltpu.VMEM((2, 8, 8, LANES), jnp.float32)] * 2
    return pl.pallas_call(
        functools.partial(end_lines_kernel, count, with_edges),
        out_shape=outs,
        in_specs=[VMEM] * 2,
        out_specs=[VMEM] * len(outs),
        compiler_params=ROOM,
        name="end_lines_field" if with_edges else "end_lines_metric",
    )(*near(ends, own))


def apply_local(derivative, folded, below, above, low, high, geometry, field, image):
    for x in range(8):
        for y in range(8):
            nodes = folded_second(folded, x + 1, y, x + 1, below, above)
            if x < 2:
                nodes = nodes + low[x, y]
            if x > 5:
                nodes = nodes + high[x - 6, y]
            field[pl.ds(64 * x + 8 * y, 8), :] = nodes
    for row in range(0, 512, 8):
        image[row : row + 8, :] = geometry[1536 + row : 1544 + row, :] * field[row : row + 8, :]
    for line in range(8):
        for dim in range(3):
            if dim == 0:
                spots = [pl.ds(64 * i + 8 * line, 8) for i in range(8)]
                places = spots
            elif dim == 1:
                spots = [pl.ds(64 * line + 8 * i, 8) for i in range(8)]
                places = [pl.ds(512 + 64 * line + 8 * i, 8) for i in range(8)]
            else:
                spots = [pl.ds(64 * line + i, 8, stride=8) for i in range(8)]
                places = [pl.ds(1024 + 64 * line + i, 8, stride=8) for i in range(8)]
            outs = both_ways(
                [field[s, :] for s in spots], [geometry[s, :] for s in places], derivative
            )
            for spot, out in zip(spots, outs):
                image[spot, :] = image[spot, :] + out


def first_operator_kernel(
    count, derivative, folded, below, above, low, high, geometry, field, image, backward, forward, inner
):
    apply_local(derivative, folded, below, above, low, high, geometry, field, image)
    total = jnp.zeros((8, LANES), jnp.float32)
    for row in range(0, 512, 8):
        total = total + field[row : row + 8, :] * image[row : row + 8, :]
    inner[...] = jnp.sum(jnp.where(own_lanes(count), total, 0.0), axis=0, keepdims=True)
    first = image[pl.ds(0, 64, stride=8), :]
    last = image[pl.ds(7, 64, stride=8), :]
    image[pl.ds(0, 64, stride=8), :] = first + pltpu.roll(last, 1, 1)
    image[pl.ds(7, 64, stride=8), :] = last + pltpu.roll(first, LANES - 1, 1)
    for x in range(2):
        for y in range(8):
            backward[x, y] = image[pl.ds(64 * x + 8 * y, 8), :]
            forward[x, y] = image[pl.ds(64 * (6 + x) + 8 * y, 8), :]


def first_operator(folded, below, above, low, high, geometry, count):
    full = pltpu.VMEM((512, LANES), jnp.float32)
    edge = pltpu.VMEM((2, 8, 8, LANES), jnp.float32)
    return pl.pallas_call(
        functools.partial(first_operator_kernel, count, derivative_table()),
        out_shape=[full, full, edge, edge, pltpu.VMEM((1, LANES), jnp.float32)],
        in_specs=[VMEM] * 6,
        out_specs=[VMEM] * 5,
        compiler_params=ROOM,
        name="first_operator",
    )(*near(folded, below, above, low, high, geometry))


def second_operator_kernel(
    count,
    derivative,
    spot,
    folded,
    below,
    above,
    low,
    high,
    geometry,
    rho,
    d,
    g,
    size,
    lines,
    payload,
    field,
    image,
):
    apply_local(derivative, folded, below, above, low, high, geometry, field, image)
    largest = jnp.max(size[...])
    unit = 1.0 / jnp.where(largest > 0.0, largest, 1.0)
    own = own_lanes(count)
    total = jnp.zeros((8, LANES), jnp.float32)
    for row in range(0, 512, 8):
        total = total + (field[row : row + 8, :] * unit) * (image[row : row + 8, :] * unit)
    h = jnp.sum(jnp.where(own, total, 0.0))
    lane = lax.broadcasted_iota(jnp.int32, (1, LANES), 1)
    scalars = jnp.zeros((1, LANES), jnp.float32)
    sums = (jnp.sum(rho[...]), jnp.sum(d[...]), jnp.sum(g[...]), h, largest)
    for place, value in enumerate(sums):
        scalars = jnp.where(lane == 64 + place, value, scalars)
    both = to_lines([field, image], count)
    lines[...] = both
    line = lax.broadcasted_iota(jnp.int32, (64, LANES), 0)
    across = lax.broadcasted_iota(jnp.int32, (64, LANES), 1)
    first = jnp.sum(jnp.where(line == across, both[64:, 0:1], 0.0), axis=0, keepdims=True)
    last = jnp.sum(
        jnp.where(line == across, both[64:, LANES - 1 : LANES], 0.0), axis=0, keepdims=True
    )
    for target in range(payload.shape[0]):
        end = jnp.where(target == spot[2] + 1, last, jnp.where(target == spot[2] - 1, first, 0.0))
        payload[target] = scalars + end


def second_operator(spot, folded, below, above, low, high, geometry, sums, count, devices):
    return pl.pallas_call(
        functools.partial(second_operator_kernel, count, derivative_table()),
        out_shape=[
            pltpu.VMEM((128, LANES), jnp.float32),
            pltpu.VMEM((devices, 1, LANES), jnp.float32),
        ],
        in_specs=[SMEM] + [VMEM] * 10,
        out_specs=[VMEM, VMEM],
        scratch_shapes=[pltpu.VMEM((512, LANES), jnp.float32)] * 2,
        compiler_params=ROOM,
        name="second_operator",
    )(spot, *near(folded, below, above, low, high, geometry, *sums))


def lines_kernel(count, one, two, lines):
    lines[...] = to_lines([one, two], count)


def as_lines(one, two, count):
    return pl.pallas_call(
        functools.partial(lines_kernel, count),
        out_shape=pltpu.VMEM((128, LANES), jnp.float32),
        in_specs=[VMEM] * 2,
        out_specs=VMEM,
        compiler_params=ROOM,
        name="as_lines",
    )(*near(one, two))


def combine(columns):
    size = jnp.max(columns[4])
    ratio = columns[4] / jnp.where(size > 0.0, size, 1.0)
    factor = ratio * ratio
    return (
        jnp.sum(columns[0]),
        jnp.sum(columns[1]),
        jnp.sum(columns[2] * factor),
        jnp.sum(columns[3] * factor),
        size,
    )


NEIGHBOURS = [(dx, dy) for dx in (-1, 0, 1) for dy in (-1, 0, 1) if (dx, dy) != (0, 0)]


def middle_kernel(sizes, spot, gathered, lines, image, out, joined):
    for device in range(gathered.shape[0]):
        joined[pl.ds(device, 1), :] = gathered[device]
    rows = joined[...]
    values = combine([rows[:, 64 + i : 65 + i] for i in range(5)])
    source = lax.broadcasted_iota(jnp.int32, rows.shape, 0)
    before = jnp.sum(jnp.where(source == spot[2] - 1, rows, 0.0), axis=0, keepdims=True)
    after = jnp.sum(jnp.where(source == spot[2] + 1, rows, 0.0), axis=0, keepdims=True)
    line = lax.broadcasted_iota(jnp.int32, (64, LANES), 0)
    across = lax.broadcasted_iota(jnp.int32, (64, LANES), 1)
    before = jnp.sum(jnp.where(line == across, before, 0.0), axis=1, keepdims=True)
    after = jnp.sum(jnp.where(line == across, after, 0.0), axis=1, keepdims=True)
    t = lines[64:, :]
    behind = pltpu.roll(t, 1, 1)
    ahead = pltpu.roll(t, LANES - 1, 1)
    image[...] = t + jnp.where(
        across % 8 == 7,
        jnp.where(across == LANES - 1, after, ahead),
        jnp.where(across % 8 == 0, jnp.where(across == 0, before, behind), 0.0),
    )
    row = lax.broadcasted_iota(jnp.int32, (8, LANES), 0)
    lane = lax.broadcasted_iota(jnp.int32, (8, LANES), 1)
    scalars = jnp.zeros((8, LANES), jnp.float32)
    for place, value in enumerate(values):
        scalars = jnp.where(row == place, value, scalars)
    scalars = jnp.where(lane == 8, scalars, 0.0)
    for device in range(sizes[0] * sizes[1]):
        out[pl.ds(8 * device, 8), :] = scalars
    for dx, dy in NEIGHBOURS:
        x, y = spot[0] + dx, spot[1] + dy
        at_x, at_y = (7 if dx > 0 else 0), (7 if dy > 0 else 0)
        if dy == 0:
            face = image[pl.ds(8 * at_x, 8), :]
        elif dx == 0:
            face = image[pl.ds(at_y, 8, stride=8), :]
        else:
            face = jnp.broadcast_to(image[pl.ds(8 * at_x + at_y, 1), :], (8, LANES))
        tile = jnp.where(lane == 8, scalars, face)

        @pl.when((x >= 0) & (x < sizes[0]) & (y >= 0) & (y < sizes[1]))
        def _():
            out[pl.ds(pl.multiple_of(8 * (x * sizes[1] + y), 8), 8), :] = tile


def middle(spot, gathered, lines, sizes):
    return pl.pallas_call(
        functools.partial(middle_kernel, sizes),
        out_shape=[
            pltpu.VMEM((64, LANES), jnp.float32),
            pltpu.VMEM((8 * sizes[0] * sizes[1], LANES), jnp.float32),
        ],
        in_specs=[SMEM, VMEM, VMEM],
        out_specs=[VMEM, VMEM],
        scratch_shapes=[pltpu.VMEM((gathered.shape[0], LANES), jnp.float32)],
        compiler_params=ROOM,
        name="middle",
    )(spot, *near(gathered, lines))


def finish_kernel(
    sizes, spot, gathered, image, second, first, right_side, solution_out, residual_out, t
):
    plane = sizes[0] * sizes[1]
    columns = [gathered[pl.ds(i, plane, stride=8), :][:, 8:9] for i in range(5)]
    rho, d, g_scaled, h_scaled, size = combine(columns)
    t[...] = image[...]
    lane = lax.broadcasted_iota(jnp.int32, (8, LANES), 1)
    for dx, dy in NEIGHBOURS:
        x, y = spot[0] + dx, spot[1] + dy
        inside = (x >= 0) & (x < sizes[0]) & (y >= 0) & (y < sizes[1])
        source = jnp.where(inside, x * sizes[1] + y, 0)
        tile = gathered[pl.ds(pl.multiple_of(8 * source, 8), 8), :]
        tile = jnp.where(lane == 8, pltpu.roll(tile, 1, 1), tile)
        tile = jnp.where(inside, tile, 0.0)
        at_x, at_y = (7 if dx > 0 else 0), (7 if dy > 0 else 0)
        if dy == 0:
            spots = pl.ds(8 * at_x, 8)
        elif dx == 0:
            spots = pl.ds(at_y, 8, stride=8)
        else:
            spots = pl.ds(8 * at_x + at_y, 1)
            tile = tile[0:1, :]
        t[spots, :] = t[spots, :] + tile

    def splat(value):
        return jnp.full((1, LANES), value, jnp.float32)

    rho, d = splat(rho), splat(d)
    alpha_one = rho / d
    reach = alpha_one * splat(size)
    g = reach * reach * splat(g_scaled)
    h = reach * reach * splat(h_scaled)
    stretch = g / rho
    alpha_two = (g - rho) / (h - stretch * g / alpha_one)
    along = alpha_one + alpha_two * stretch
    turn = alpha_one * alpha_two
    solution_out[...] = along * first[0:64, :] - turn * second[0:64, :]
    residual_out[...] = right_side[...] - along * first[64:128, :] + turn * t[...]


def finish(spot, gathered, image, second, first, right_side, sizes):
    full = jax.ShapeDtypeStruct((64, LANES), jnp.float32)
    return pl.pallas_call(
        functools.partial(finish_kernel, sizes),
        out_shape=[full, full],
        in_specs=[SMEM] + [VMEM] * 5,
        out_specs=[VMEM, VMEM],
        scratch_shapes=[pltpu.VMEM((64, LANES), jnp.float32)],
        compiler_params=ROOM,
        name="finish",
    )(spot, *near(gathered, image, second, first, right_side))


def exchange(rows, axes):
    return lax.all_to_all(rows, axes, 0, 0, tiled=True)


def on_device(right_side, geometry, element_shape_class, fdm_vectors, fdm_values):
    count = element_shape_class.shape[2]
    classes = fdm_vectors.shape[0]
    depth = lax.axis_size("gz")
    sizes = (lax.axis_size("gx"), lax.axis_size("gy"))
    spot = jnp.stack([lax.axis_index(a).astype(jnp.int32) for a in ("gx", "gy", "gz")])
    ends = 8 * REACH
    lines = right_side.reshape(64, LANES)
    metric_lines = geometry.reshape(256, LANES)
    class_lines = jnp.broadcast_to(
        jnp.repeat(element_shape_class.reshape(1, -1), 8, axis=1).astype(jnp.float32),
        (8, 8 * count),
    )
    stack = jnp.concatenate([lines, class_lines, metric_lines], axis=0)
    low, high = swap(stack[:, :ends], stack[:, -ends:], "gz")
    own_field, own_metric = own_lines(lines, metric_lines)
    outer = jnp.concatenate([low, high], axis=1)
    deep_class = jnp.concatenate(
        [low[64, ::8], element_shape_class.reshape(-1).astype(jnp.float32), high[64, ::8]]
    ).astype(jnp.int32)
    deep_class = jnp.pad(deep_class, (0, LANES - deep_class.shape[0]))
    element = jnp.arange(LANES, dtype=jnp.int32) - REACH + spot[2] * count
    valid = ((element >= 0) & (element < depth * count)).astype(jnp.float32)[None, :]
    onehot = (jnp.arange(classes, dtype=jnp.int32)[:, None] == deep_class[None, :]).astype(
        jnp.float32
    )
    entries = jnp.concatenate(
        [fdm_vectors.reshape(classes, 300), fdm_values.reshape(classes, 30)], axis=1
    )
    table = lax.dot_general(
        entries, onehot, (((0,), (0,)), ((), ())), precision=HIGHEST
    )
    field, backward, forward = end_lines(outer[:64], own_field, count, True)
    low, high = swap(backward, forward, "gx")
    (metric,) = end_lines(outer[72:], own_metric, count, False)
    low, high, metric, table = lax.optimization_barrier((low, high, metric, table))
    below, above = swap(*second_edges(field, low, high, False), "gy")
    folded, rims, backward, forward, rho = block_solve(
        field, low, high, below, above, table, valid, count, False
    )
    below, above = swap(backward, forward, "gy")
    low, high = swap(*first_edges(rims, below, above), "gx")
    p, image, backward, forward, d = first_operator(
        folded, below, above, low, high, metric, count
    )
    low, high = swap(backward, forward, "gx")
    below, above = swap(*second_edges(image, low, high, True), "gy")
    folded, rims, backward, forward, g, size, q = block_solve(
        image, low, high, below, above, table, valid, count, True
    )
    below, above = swap(backward, forward, "gy")
    first = as_lines(p, q, count)
    below, above, first = lax.optimization_barrier((below, above, first))
    low, high = swap(*first_edges(rims, below, above), "gx")
    second, payload = second_operator(
        spot, folded, below, above, low, high, own_metric, (rho, d, g, size), count, depth
    )
    gathered = exchange(payload, "gz")
    image, tiles = middle(spot, gathered, second, sizes)
    gathered = exchange(tiles, ("gx", "gy"))
    answer, left = finish(spot, gathered, image, second, first, lines, sizes)
    return (answer.reshape(8, 8, LANES), left.reshape(8, 8, LANES))


def solution(mesh):
    placed = (P("gx", "gy", "gz"), P(None, "gx", "gy", "gz"), P("gx", "gy", "gz"), P(), P())
    return jax.shard_map(
        on_device,
        mesh=mesh,
        in_specs=placed,
        out_specs=(P("gx", "gy", "gz"), P("gx", "gy", "gz")),
        check_vma=False,
    )
```

```python
import functools

import jax
import jax.numpy as jnp
import numpy as np
from jax import lax
from jax.experimental import pallas as pl
from jax.experimental.pallas import tpu as pltpu
from jax.sharding import PartitionSpec as P

HIGHEST = lax.Precision.HIGHEST
LANES = 128
REACH = 4
GROUP = 32
SMEM = pl.BlockSpec(memory_space=pltpu.SMEM)
VMEM = pl.BlockSpec(memory_space=pltpu.VMEM)
ROOM = pltpu.CompilerParams(vmem_limit_bytes=8 << 20)
CHUNKS = ((0, 24), (24, 24), (48, 24), (72, 28))


def swap(backward_part, forward_part, axis):
    count = lax.axis_size(axis)
    forward = [(i, i + 1) for i in range(count - 1)]
    backward = [(target, source) for source, target in forward]
    return lax.ppermute(forward_part, axis, forward), lax.ppermute(backward_part, axis, backward)


def derivative_table():
    points = np.array(
        [
            -1.0,
            -0.8717401485096066,
            -0.5917001814331423,
            -0.2092992179024789,
            0.2092992179024789,
            0.5917001814331423,
            0.8717401485096066,
            1.0,
        ]
    )
    previous = np.ones(8)
    current = points * 1.0
    for order in range(1, 7):
        following = ((2 * order + 1) * points * current - order * previous) / (order + 1)
        previous = current
        current = following
    spacing = points[:, None] - points[None, :] + np.eye(8)
    off_diagonal = current[:, None] / (current[None, :] * spacing)
    positions = np.arange(8)
    end_values = np.where(positions == 0, -14.0, 0.0) + np.where(positions == 7, 14.0, 0.0)
    return np.where(np.eye(8) > 0, np.eye(8) * end_values[None, :], off_diagonal)


def near(*arrays):
    return [pltpu.with_memory_space_constraint(array, pltpu.VMEM) for array in arrays]


def own_lanes(count):
    lane = lax.broadcasted_iota(jnp.int32, (1, LANES), 1)
    return (lane >= REACH) & (lane < REACH + count)


def solve_step(source, target, table, base, transposed, scale=None):
    for start, size in CHUNKS:
        entries = [source[pl.ds(10 * start + k, size, stride=10), :] for k in range(10)]
        for out in range(10):
            total = None
            for k in range(10):
                row = base + (10 * out + k if transposed else 10 * k + out)
                term = table[row : row + 1, :] * entries[k]
                total = term if total is None else total + term
            if scale is not None:
                total = total / (table[300 + out : 301 + out, :] + scale[start : start + size, :])
            target[pl.ds(100 * out + start, size), :] = total


def pack(out, pieces):
    lane = lax.broadcasted_iota(jnp.int32, (8, LANES), 1)
    for place in range(len(pieces) // 4):
        total = pieces[4 * place]
        for slot in range(1, 4):
            moved = pltpu.roll(pieces[4 * place + slot], GROUP * slot, 1)
            total = jnp.where(lane >= GROUP * slot, moved, total)
        out[place] = total


class Unpacked:
    def __init__(self, ref, width):
        self.ref, self.width = ref, width

    def __getitem__(self, index):
        place = self.width * index[0] + index[1]
        piece = self.ref[place // 4]
        slot = place % 4
        return piece if slot == 0 else pltpu.roll(piece, LANES - GROUP * slot, 1)


def extended_first(a, y, field, low, high, shared):
    if a == 0:
        return low[0, y]
    if a == 9:
        return high[1, y]
    nodes = field[pl.ds(64 * (a - 1) + 8 * y, 8), :]
    if shared and a == 1:
        nodes = nodes + low[1, y]
    if shared and a == 8:
        nodes = nodes + high[0, y]
    return nodes


def second_edges_kernel(shared, field, low, high, backward, forward):
    low, high = Unpacked(low, 8), Unpacked(high, 8)
    pairs = [(a, y) for a in range(10) for y in range(2)]
    pack(backward, [extended_first(a, y, field, low, high, shared) for a, y in pairs])
    pack(forward, [extended_first(a, 6 + y, field, low, high, shared) for a, y in pairs])


def second_edges(field, low, high, shared):
    return pl.pallas_call(
        functools.partial(second_edges_kernel, shared),
        out_shape=[pltpu.VMEM((5, 8, LANES), jnp.float32)] * 2,
        in_specs=[VMEM] * 3,
        out_specs=[VMEM] * 2,
        compiler_params=ROOM,
        name="second_edges",
    )(*near(field, low, high))


def solve_kernel(count, shared, field, low, high, below, above, table, valid, *refs):
    if shared:
        folded, rims, backward, forward, inner, size_row, assembled, blocks, left, right, pair = refs
    else:
        folded, rims, backward, forward, inner, blocks, left, right, pair = refs
    low, high = Unpacked(low, 8), Unpacked(high, 8)
    below, above = Unpacked(below, 2), Unpacked(above, 2)
    blocks[pl.ds(1000, 40), :] = jnp.zeros((40, LANES), jnp.float32)
    left[pl.ds(1000, 40), :] = jnp.zeros((40, LANES), jnp.float32)
    right[pl.ds(1000, 40), :] = jnp.zeros((40, LANES), jnp.float32)
    for a in range(10):
        for b in range(10):
            if b == 0:
                nodes = below[a, 0]
            elif b == 9:
                nodes = above[a, 1]
            else:
                nodes = extended_first(a, b - 1, field, low, high, shared)
                if shared and b == 1:
                    nodes = nodes + below[a, 1]
                if shared and b == 8:
                    nodes = nodes + above[a, 0]
                if shared and 1 <= a <= 8:
                    assembled[pl.ds(64 * (a - 1) + 8 * (b - 1), 8), :] = nodes
            blocks[pl.ds(100 * a + 10 * b + 1, 8), :] = nodes
    blocks[pl.ds(0, 100, stride=10), :] = pltpu.roll(
        blocks[pl.ds(7, 100, stride=10), :], 1, 1
    )
    blocks[pl.ds(9, 100, stride=10), :] = pltpu.roll(
        blocks[pl.ds(2, 100, stride=10), :], LANES - 1, 1
    )
    for n in range(10):
        pair[pl.ds(10 * n, 10), :] = table[310 + n : 311 + n, :] + table[320:330, :]
    solve_step(blocks, left, table, 200, False)
    solve_step(left, right, table, 100, False)
    solve_step(right, left, table, 0, False, pair)
    solve_step(left, right, table, 200, True)
    solve_step(right, left, table, 100, True)
    solve_step(left, right, table, 0, True)
    exists = valid[...] > 0.0
    own = own_lanes(count)
    unit = 1.0
    if shared:
        largest = jnp.zeros((8, LANES), jnp.float32)
        for row in range(0, 1000, 8):
            largest = jnp.maximum(largest, jnp.abs(blocks[row : row + 8, :]))
        size = jnp.max(jnp.where(own, largest, 0.0))
        unit = 1.0 / jnp.where(size > 0.0, size, 1.0)
        size_row[...] = jnp.full((1, LANES), size, jnp.float32)
    total = jnp.zeros((8, LANES), jnp.float32)
    for row in range(0, 1000, 8):
        total = total + (blocks[row : row + 8, :] * unit) * (right[row : row + 8, :] * unit)
    inner[...] = jnp.sum(jnp.where(own, total, 0.0), axis=0, keepdims=True)

    def entry(c):
        return jnp.where(exists, right[pl.ds(c, 100, stride=10), :], 0.0)

    first, second, second_last, last = entry(0), entry(1), entry(8), entry(9)
    right[pl.ds(1, 100, stride=10), :] = second + pltpu.roll(second_last, 1, 1)
    right[pl.ds(2, 100, stride=10), :] = entry(2) + pltpu.roll(last, 1, 1)
    right[pl.ds(7, 100, stride=10), :] = entry(7) + pltpu.roll(first, LANES - 1, 1)
    right[pl.ds(8, 100, stride=10), :] = second_last + pltpu.roll(second, LANES - 1, 1)
    for a in range(10):
        for b in range(10):
            nodes = right[pl.ds(100 * a + 10 * b + 1, 8), :]
            folded[a, b] = nodes
            if a < 2:
                rims[a, b] = nodes
            if a > 7:
                rims[a - 6, b] = nodes
    pairs = [(a, b) for a in range(10) for b in range(2)]
    pack(backward, [folded[a, b] for a, b in pairs])
    pack(forward, [folded[a, b + 8] for a, b in pairs])


def block_solve(field, low, high, below, above, table, valid, count, shared):
    row = pltpu.VMEM((1, LANES), jnp.float32)
    edge = pltpu.VMEM((5, 8, LANES), jnp.float32)
    outs = [
        pltpu.VMEM((10, 10, 8, LANES), jnp.float32),
        pltpu.VMEM((4, 10, 8, LANES), jnp.float32),
        edge,
        edge,
        row,
    ]
    if shared:
        outs += [row, pltpu.VMEM((512, LANES), jnp.float32)]
    return pl.pallas_call(
        functools.partial(solve_kernel, count, shared),
        out_shape=outs,
        scratch_shapes=[pltpu.VMEM((1040, LANES), jnp.float32)] * 3
        + [pltpu.VMEM((104, LANES), jnp.float32)],
        in_specs=[VMEM] * 7,
        out_specs=[VMEM] * len(outs),
        compiler_params=ROOM,
        name="block_solve_shared" if shared else "block_solve_first",
    )(*near(field, low, high, below, above, table, valid))


def folded_second(values, a, y, at, below, above):
    nodes = values[a, y + 1]
    if y < 2:
        nodes = nodes + below[at, y]
    if y > 5:
        nodes = nodes + above[at, y - 6]
    return nodes


def first_edges_kernel(rims, below, above, backward, forward):
    below, above = Unpacked(below, 2), Unpacked(above, 2)
    pairs = [(a, y) for a in range(2) for y in range(8)]
    pack(backward, [folded_second(rims, a, y, a, below, above) for a, y in pairs])
    pack(forward, [folded_second(rims, a + 2, y, a + 8, below, above) for a, y in pairs])


def first_edges(rims, below, above):
    return pl.pallas_call(
        first_edges_kernel,
        out_shape=[pltpu.VMEM((4, 8, LANES), jnp.float32)] * 2,
        in_specs=[VMEM] * 3,
        out_specs=[VMEM] * 2,
        compiler_params=ROOM,
        name="first_edges",
    )(*near(rims, below, above))


def both_ways(nodes, metric, derivative):
    slopes = []
    for a in range(8):
        total = None
        for i in range(8):
            if derivative[a, i] != 0.0:
                term = float(derivative[a, i]) * nodes[i]
                total = term if total is None else total + term
        slopes.append(metric[a] * total)
    outs = []
    for i in range(8):
        total = None
        for a in range(8):
            if derivative[a, i] != 0.0:
                term = float(derivative[a, i]) * slopes[a]
                total = term if total is None else total + term
        outs.append(total)
    return outs


def to_lines(sources, count):
    lane = lax.broadcasted_iota(jnp.int32, (LANES, LANES), 0)
    place = lax.broadcasted_iota(jnp.int32, (LANES, LANES), 1)
    total = jnp.zeros((64 * len(sources), LANES), jnp.float32)
    for k in range(8):
        pick = (
            (place == 8 * (lane - REACH) + k) & (lane >= REACH) & (lane < REACH + count)
        ).astype(jnp.bfloat16)
        rest = jnp.concatenate([s[pl.ds(k, 64, stride=8), :] for s in sources], axis=0)
        rest = jnp.where(own_lanes(count), rest, 0.0)
        for _ in range(3):
            part = rest.astype(jnp.bfloat16)
            total = total + jnp.dot(part, pick, preferred_element_type=jnp.float32)
            rest = rest - part.astype(jnp.float32)
    return total


def in_parts(values):
    parts = []
    for _ in range(3):
        part = values.astype(jnp.bfloat16)
        parts.append(part)
        values = values - part.astype(jnp.float32)
    return parts


def spread_lines(lines, lane_of_element, out, base=None):
    count, length = lines.shape
    node = lax.broadcasted_iota(jnp.int32, (length, 2 * LANES), 0)
    place = lax.broadcasted_iota(jnp.int32, (length, 2 * LANES), 1)
    parts = in_parts(lines)
    for k in range(0, 8, 2):
        wanted = lane_of_element(node // 8) + LANES * (node % 8 - k)
        pick = ((node % 8 >= k) & (node % 8 < k + 2) & (place == wanted)).astype(jnp.bfloat16)
        total = None
        for part in parts:
            term = jnp.dot(part, pick, preferred_element_type=jnp.float32)
            total = term if total is None else total + term
        for half in range(2):
            value = total[:, half * LANES : (half + 1) * LANES]
            spot = pl.ds(k + half, count, stride=8)
            out[spot, :] = value if base is None else value + base[spot, :]


def own_lines_kernel(right_side, geometry, field, metric):
    spread_lines(right_side[...], lambda e: e + REACH, field)
    spread_lines(geometry[...], lambda e: e + REACH, metric)


def own_lines(right_side, geometry):
    return pl.pallas_call(
        own_lines_kernel,
        out_shape=[
            pltpu.VMEM((512, LANES), jnp.float32),
            pltpu.VMEM((2048, LANES), jnp.float32),
        ],
        in_specs=[VMEM] * 2,
        out_specs=[VMEM] * 2,
        compiler_params=ROOM,
        name="own_lines",
    )(*near(right_side, geometry))


def pack_ends(field, backward, forward):
    pack(backward, [field[pl.ds(8 * i, 8), :] for i in range(16)])
    pack(forward, [field[pl.ds(384 + 8 * i, 8), :] for i in range(16)])


def end_lines_kernel(count, with_edges, ends, own, out, *edges):
    spread_lines(ends[...], lambda e: jnp.where(e < REACH, e, e + count), out, own)
    if with_edges:
        pack_ends(out, *edges)


def end_lines(ends, own, count, with_edges):
    outs = [pltpu.VMEM(own.shape, jnp.float32)]
    if with_edges:
        outs += [pltpu.VMEM((4, 8, LANES), jnp.float32)] * 2
    return pl.pallas_call(
        functools.partial(end_lines_kernel, count, with_edges),
        out_shape=outs,
        in_specs=[VMEM] * 2,
        out_specs=[VMEM] * len(outs),
        compiler_params=ROOM,
        name="end_lines_field" if with_edges else "end_lines_metric",
    )(*near(ends, own))


def apply_local(derivative, folded, below, above, low, high, geometry, field, image):
    below, above = Unpacked(below, 2), Unpacked(above, 2)
    low, high = Unpacked(low, 8), Unpacked(high, 8)
    for x in range(8):
        for y in range(8):
            nodes = folded_second(folded, x + 1, y, x + 1, below, above)
            if x < 2:
                nodes = nodes + low[x, y]
            if x > 5:
                nodes = nodes + high[x - 6, y]
            field[pl.ds(64 * x + 8 * y, 8), :] = nodes
    for row in range(0, 512, 8):
        image[row : row + 8, :] = geometry[1536 + row : 1544 + row, :] * field[row : row + 8, :]
    for line in range(8):
        for dim in range(3):
            if dim == 0:
                spots = [pl.ds(64 * i + 8 * line, 8) for i in range(8)]
                places = spots
            elif dim == 1:
                spots = [pl.ds(64 * line + 8 * i, 8) for i in range(8)]
                places = [pl.ds(512 + 64 * line + 8 * i, 8) for i in range(8)]
            else:
                spots = [pl.ds(64 * line + i, 8, stride=8) for i in range(8)]
                places = [pl.ds(1024 + 64 * line + i, 8, stride=8) for i in range(8)]
            outs = both_ways(
                [field[s, :] for s in spots], [geometry[s, :] for s in places], derivative
            )
            for spot, out in zip(spots, outs):
                image[spot, :] = image[spot, :] + out


def first_operator_kernel(
    count, derivative, folded, below, above, low, high, geometry, field, image, backward, forward, inner
):
    apply_local(derivative, folded, below, above, low, high, geometry, field, image)
    total = jnp.zeros((8, LANES), jnp.float32)
    for row in range(0, 512, 8):
        total = total + field[row : row + 8, :] * image[row : row + 8, :]
    inner[...] = jnp.sum(jnp.where(own_lanes(count), total, 0.0), axis=0, keepdims=True)
    first = image[pl.ds(0, 64, stride=8), :]
    last = image[pl.ds(7, 64, stride=8), :]
    image[pl.ds(0, 64, stride=8), :] = first + pltpu.roll(last, 1, 1)
    image[pl.ds(7, 64, stride=8), :] = last + pltpu.roll(first, LANES - 1, 1)
    pack_ends(image, backward, forward)


def first_operator(folded, below, above, low, high, geometry, count):
    full = pltpu.VMEM((512, LANES), jnp.float32)
    edge = pltpu.VMEM((4, 8, LANES), jnp.float32)
    return pl.pallas_call(
        functools.partial(first_operator_kernel, count, derivative_table()),
        out_shape=[full, full, edge, edge, pltpu.VMEM((1, LANES), jnp.float32)],
        in_specs=[VMEM] * 6,
        out_specs=[VMEM] * 5,
        compiler_params=ROOM,
        name="first_operator",
    )(*near(folded, below, above, low, high, geometry))


def second_operator_kernel(
    count,
    derivative,
    spot,
    folded,
    below,
    above,
    low,
    high,
    geometry,
    rho,
    d,
    g,
    size,
    lines,
    payload,
    field,
    image,
):
    apply_local(derivative, folded, below, above, low, high, geometry, field, image)
    largest = jnp.max(size[...])
    unit = 1.0 / jnp.where(largest > 0.0, largest, 1.0)
    own = own_lanes(count)
    total = jnp.zeros((8, LANES), jnp.float32)
    for row in range(0, 512, 8):
        total = total + (field[row : row + 8, :] * unit) * (image[row : row + 8, :] * unit)
    h = jnp.sum(jnp.where(own, total, 0.0))
    lane = lax.broadcasted_iota(jnp.int32, (1, LANES), 1)
    scalars = jnp.zeros((1, LANES), jnp.float32)
    sums = (jnp.sum(rho[...]), jnp.sum(d[...]), jnp.sum(g[...]), h, largest)
    for place, value in enumerate(sums):
        scalars = jnp.where(lane == 64 + place, value, scalars)
    both = to_lines([field, image], count)
    lines[...] = both
    line = lax.broadcasted_iota(jnp.int32, (64, LANES), 0)
    across = lax.broadcasted_iota(jnp.int32, (64, LANES), 1)
    first = jnp.sum(jnp.where(line == across, both[64:, 0:1], 0.0), axis=0, keepdims=True)
    last = jnp.sum(
        jnp.where(line == across, both[64:, LANES - 1 : LANES], 0.0), axis=0, keepdims=True
    )
    for target in range(payload.shape[0]):
        end = jnp.where(target == spot[2] + 1, last, jnp.where(target == spot[2] - 1, first, 0.0))
        payload[target] = scalars + end


def second_operator(spot, folded, below, above, low, high, geometry, sums, count, devices):
    return pl.pallas_call(
        functools.partial(second_operator_kernel, count, derivative_table()),
        out_shape=[
            pltpu.VMEM((128, LANES), jnp.float32),
            pltpu.VMEM((devices, 1, LANES), jnp.float32),
        ],
        in_specs=[SMEM] + [VMEM] * 10,
        out_specs=[VMEM, VMEM],
        scratch_shapes=[pltpu.VMEM((512, LANES), jnp.float32)] * 2,
        compiler_params=ROOM,
        name="second_operator",
    )(spot, *near(folded, below, above, low, high, geometry, *sums))


def lines_kernel(count, one, two, lines):
    lines[...] = to_lines([one, two], count)


def as_lines(one, two, count):
    return pl.pallas_call(
        functools.partial(lines_kernel, count),
        out_shape=pltpu.VMEM((128, LANES), jnp.float32),
        in_specs=[VMEM] * 2,
        out_specs=VMEM,
        compiler_params=ROOM,
        name="as_lines",
    )(*near(one, two))


def combine(columns):
    size = jnp.max(columns[4])
    ratio = columns[4] / jnp.where(size > 0.0, size, 1.0)
    factor = ratio * ratio
    return (
        jnp.sum(columns[0]),
        jnp.sum(columns[1]),
        jnp.sum(columns[2] * factor),
        jnp.sum(columns[3] * factor),
        size,
    )


NEIGHBOURS = [(dx, dy) for dx in (-1, 0, 1) for dy in (-1, 0, 1) if (dx, dy) != (0, 0)]


def middle_kernel(sizes, spot, gathered, lines, image, out, joined):
    for device in range(gathered.shape[0]):
        joined[pl.ds(device, 1), :] = gathered[device]
    rows = joined[...]
    values = combine([rows[:, 64 + i : 65 + i] for i in range(5)])
    source = lax.broadcasted_iota(jnp.int32, rows.shape, 0)
    before = jnp.sum(jnp.where(source == spot[2] - 1, rows, 0.0), axis=0, keepdims=True)
    after = jnp.sum(jnp.where(source == spot[2] + 1, rows, 0.0), axis=0, keepdims=True)
    line = lax.broadcasted_iota(jnp.int32, (64, LANES), 0)
    across = lax.broadcasted_iota(jnp.int32, (64, LANES), 1)
    before = jnp.sum(jnp.where(line == across, before, 0.0), axis=1, keepdims=True)
    after = jnp.sum(jnp.where(line == across, after, 0.0), axis=1, keepdims=True)
    t = lines[64:, :]
    behind = pltpu.roll(t, 1, 1)
    ahead = pltpu.roll(t, LANES - 1, 1)
    image[...] = t + jnp.where(
        across % 8 == 7,
        jnp.where(across == LANES - 1, after, ahead),
        jnp.where(across % 8 == 0, jnp.where(across == 0, before, behind), 0.0),
    )
    row = lax.broadcasted_iota(jnp.int32, (8, LANES), 0)
    lane = lax.broadcasted_iota(jnp.int32, (8, LANES), 1)
    scalars = jnp.zeros((8, LANES), jnp.float32)
    for place, value in enumerate(values):
        scalars = jnp.where(row == place, value, scalars)
    scalars = jnp.where(lane == 8, scalars, 0.0)
    for device in range(sizes[0] * sizes[1]):
        out[pl.ds(8 * device, 8), :] = scalars
    for dx, dy in NEIGHBOURS:
        x, y = spot[0] + dx, spot[1] + dy
        at_x, at_y = (7 if dx > 0 else 0), (7 if dy > 0 else 0)
        if dy == 0:
            face = image[pl.ds(8 * at_x, 8), :]
        elif dx == 0:
            face = image[pl.ds(at_y, 8, stride=8), :]
        else:
            face = jnp.broadcast_to(image[pl.ds(8 * at_x + at_y, 1), :], (8, LANES))
        tile = jnp.where(lane == 8, scalars, face)

        @pl.when((x >= 0) & (x < sizes[0]) & (y >= 0) & (y < sizes[1]))
        def _():
            out[pl.ds(pl.multiple_of(8 * (x * sizes[1] + y), 8), 8), :] = tile


def middle(spot, gathered, lines, sizes):
    return pl.pallas_call(
        functools.partial(middle_kernel, sizes),
        out_shape=[
            pltpu.VMEM((64, LANES), jnp.float32),
            pltpu.VMEM((8 * sizes[0] * sizes[1], LANES), jnp.float32),
        ],
        in_specs=[SMEM, VMEM, VMEM],
        out_specs=[VMEM, VMEM],
        scratch_shapes=[pltpu.VMEM((gathered.shape[0], LANES), jnp.float32)],
        compiler_params=ROOM,
        name="middle",
    )(spot, *near(gathered, lines))


def finish_kernel(
    sizes, spot, gathered, image, second, first, right_side, solution_out, residual_out, t
):
    plane = sizes[0] * sizes[1]
    columns = [gathered[pl.ds(i, plane, stride=8), :][:, 8:9] for i in range(5)]
    rho, d, g_scaled, h_scaled, size = combine(columns)
    t[...] = image[...]
    lane = lax.broadcasted_iota(jnp.int32, (8, LANES), 1)
    for dx, dy in NEIGHBOURS:
        x, y = spot[0] + dx, spot[1] + dy
        inside = (x >= 0) & (x < sizes[0]) & (y >= 0) & (y < sizes[1])
        source = jnp.where(inside, x * sizes[1] + y, 0)
        tile = gathered[pl.ds(pl.multiple_of(8 * source, 8), 8), :]
        tile = jnp.where(lane == 8, pltpu.roll(tile, 1, 1), tile)
        tile = jnp.where(inside, tile, 0.0)
        at_x, at_y = (7 if dx > 0 else 0), (7 if dy > 0 else 0)
        if dy == 0:
            spots = pl.ds(8 * at_x, 8)
        elif dx == 0:
            spots = pl.ds(at_y, 8, stride=8)
        else:
            spots = pl.ds(8 * at_x + at_y, 1)
            tile = tile[0:1, :]
        t[spots, :] = t[spots, :] + tile

    def splat(value):
        return jnp.full((1, LANES), value, jnp.float32)

    rho, d = splat(rho), splat(d)
    alpha_one = rho / d
    reach = alpha_one * splat(size)
    g = reach * reach * splat(g_scaled)
    h = reach * reach * splat(h_scaled)
    stretch = g / rho
    alpha_two = (g - rho) / (h - stretch * g / alpha_one)
    along = alpha_one + alpha_two * stretch
    turn = alpha_one * alpha_two
    solution_out[...] = along * first[0:64, :] - turn * second[0:64, :]
    residual_out[...] = right_side[...] - along * first[64:128, :] + turn * t[...]


def finish(spot, gathered, image, second, first, right_side, sizes):
    full = jax.ShapeDtypeStruct((64, LANES), jnp.float32)
    return pl.pallas_call(
        functools.partial(finish_kernel, sizes),
        out_shape=[full, full],
        in_specs=[SMEM] + [VMEM] * 5,
        out_specs=[VMEM, VMEM],
        scratch_shapes=[pltpu.VMEM((64, LANES), jnp.float32)],
        compiler_params=ROOM,
        name="finish",
    )(spot, *near(gathered, image, second, first, right_side))


def exchange(rows, axes):
    return lax.all_to_all(rows, axes, 0, 0, tiled=True)


def on_device(right_side, geometry, element_shape_class, fdm_vectors, fdm_values):
    count = element_shape_class.shape[2]
    classes = fdm_vectors.shape[0]
    depth = lax.axis_size("gz")
    sizes = (lax.axis_size("gx"), lax.axis_size("gy"))
    spot = jnp.stack([lax.axis_index(a).astype(jnp.int32) for a in ("gx", "gy", "gz")])
    ends = 8 * REACH
    lines = right_side.reshape(64, LANES)
    metric_lines = geometry.reshape(256, LANES)
    class_lines = jnp.broadcast_to(
        jnp.repeat(element_shape_class.reshape(1, -1), 8, axis=1).astype(jnp.float32),
        (8, 8 * count),
    )
    stack = jnp.concatenate([lines, class_lines, metric_lines], axis=0)
    low, high = swap(stack[:, :ends], stack[:, -ends:], "gz")
    own_field, own_metric = own_lines(lines, metric_lines)
    outer = jnp.concatenate([low, high], axis=1)
    deep_class = jnp.concatenate(
        [low[64, ::8], element_shape_class.reshape(-1).astype(jnp.float32), high[64, ::8]]
    ).astype(jnp.int32)
    deep_class = jnp.pad(deep_class, (0, LANES - deep_class.shape[0]))
    element = jnp.arange(LANES, dtype=jnp.int32) - REACH + spot[2] * count
    valid = ((element >= 0) & (element < depth * count)).astype(jnp.float32)[None, :]
    onehot = (jnp.arange(classes, dtype=jnp.int32)[:, None] == deep_class[None, :]).astype(
        jnp.float32
    )
    entries = jnp.concatenate(
        [fdm_vectors.reshape(classes, 300), fdm_values.reshape(classes, 30)], axis=1
    )
    table = lax.dot_general(
        entries, onehot, (((0,), (0,)), ((), ())), precision=HIGHEST
    )
    field, backward, forward = end_lines(outer[:64], own_field, count, True)
    low, high = swap(backward, forward, "gx")
    (metric,) = end_lines(outer[72:], own_metric, count, False)
    low, high, metric, table = lax.optimization_barrier((low, high, metric, table))
    below, above = swap(*second_edges(field, low, high, False), "gy")
    folded, rims, backward, forward, rho = block_solve(
        field, low, high, below, above, table, valid, count, False
    )
    below, above = swap(backward, forward, "gy")
    low, high = swap(*first_edges(rims, below, above), "gx")
    p, image, backward, forward, d = first_operator(
        folded, below, above, low, high, metric, count
    )
    low, high = swap(backward, forward, "gx")
    below, above = swap(*second_edges(image, low, high, True), "gy")
    folded, rims, backward, forward, g, size, q = block_solve(
        image, low, high, below, above, table, valid, count, True
    )
    below, above = swap(backward, forward, "gy")
    first = as_lines(p, q, count)
    below, above, first = lax.optimization_barrier((below, above, first))
    low, high = swap(*first_edges(rims, below, above), "gx")
    second, payload = second_operator(
        spot, folded, below, above, low, high, own_metric, (rho, d, g, size), count, depth
    )
    gathered = exchange(payload, "gz")
    image, tiles = middle(spot, gathered, second, sizes)
    gathered = exchange(tiles, ("gx", "gy"))
    answer, left = finish(spot, gathered, image, second, first, lines, sizes)
    return (answer.reshape(8, 8, LANES), left.reshape(8, 8, LANES))


def solution(mesh):
    placed = (P("gx", "gy", "gz"), P(None, "gx", "gy", "gz"), P("gx", "gy", "gz"), P(), P())
    return jax.shard_map(
        on_device,
        mesh=mesh,
        in_specs=placed,
        out_specs=(P("gx", "gy", "gz"), P("gx", "gy", "gz")),
        check_vma=False,
    )
```

```python
import functools

import jax
import jax.numpy as jnp
import numpy as np
from jax import lax
from jax.experimental import pallas as pl
from jax.experimental.pallas import tpu as pltpu
from jax.sharding import PartitionSpec as P

HIGHEST = lax.Precision.HIGHEST
LANES = 128
REACH = 4
GROUP = 32
SMEM = pl.BlockSpec(memory_space=pltpu.SMEM)
VMEM = pl.BlockSpec(memory_space=pltpu.VMEM)
ROOM = pltpu.CompilerParams(vmem_limit_bytes=8 << 20)
CHUNKS = ((0, 24), (24, 24), (48, 24), (72, 28))


def swap(backward_part, forward_part, axis):
    count = lax.axis_size(axis)
    forward = [(i, i + 1) for i in range(count - 1)]
    backward = [(target, source) for source, target in forward]
    return lax.ppermute(forward_part, axis, forward), lax.ppermute(backward_part, axis, backward)


def derivative_table():
    points = np.array(
        [
            -1.0,
            -0.8717401485096066,
            -0.5917001814331423,
            -0.2092992179024789,
            0.2092992179024789,
            0.5917001814331423,
            0.8717401485096066,
            1.0,
        ]
    )
    previous = np.ones(8)
    current = points * 1.0
    for order in range(1, 7):
        following = ((2 * order + 1) * points * current - order * previous) / (order + 1)
        previous = current
        current = following
    spacing = points[:, None] - points[None, :] + np.eye(8)
    off_diagonal = current[:, None] / (current[None, :] * spacing)
    positions = np.arange(8)
    end_values = np.where(positions == 0, -14.0, 0.0) + np.where(positions == 7, 14.0, 0.0)
    return np.where(np.eye(8) > 0, np.eye(8) * end_values[None, :], off_diagonal)


def near(*arrays):
    return [pltpu.with_memory_space_constraint(array, pltpu.VMEM) for array in arrays]


def own_lanes(count):
    lane = lax.broadcasted_iota(jnp.int32, (1, LANES), 1)
    return (lane >= REACH) & (lane < REACH + count)


def solve_step(source, target, table, base, transposed, scale=None):
    for start, size in CHUNKS:
        entries = [source[pl.ds(10 * start + k, size, stride=10), :] for k in range(10)]
        for out in range(10):
            total = None
            for k in range(10):
                row = base + (10 * out + k if transposed else 10 * k + out)
                term = table[row : row + 1, :] * entries[k]
                total = term if total is None else total + term
            if scale is not None:
                total = total / (table[300 + out : 301 + out, :] + scale[start : start + size, :])
            target[pl.ds(100 * out + start, size), :] = total


def pack(out, pieces):
    lane = lax.broadcasted_iota(jnp.int32, (8, LANES), 1)
    for place in range(len(pieces) // 4):
        total = pieces[4 * place]
        for slot in range(1, 4):
            moved = pltpu.roll(pieces[4 * place + slot], GROUP * slot, 1)
            total = jnp.where(lane >= GROUP * slot, moved, total)
        out[place] = total


class Unpacked:
    def __init__(self, ref, width):
        self.ref, self.width = ref, width

    def __getitem__(self, index):
        place = self.width * index[0] + index[1]
        piece = self.ref[place // 4]
        slot = place % 4
        return piece if slot == 0 else pltpu.roll(piece, LANES - GROUP * slot, 1)


def extended_first(a, y, field, low, high, shared):
    if a == 0:
        return low[0, y]
    if a == 9:
        return high[1, y]
    nodes = field[pl.ds(64 * (a - 1) + 8 * y, 8), :]
    if shared and a == 1:
        nodes = nodes + low[1, y]
    if shared and a == 8:
        nodes = nodes + high[0, y]
    return nodes


def second_edges_kernel(shared, field, low, high, backward, forward):
    low, high = Unpacked(low, 8), Unpacked(high, 8)
    pairs = [(a, y) for a in range(10) for y in range(2)]
    pack(backward, [extended_first(a, y, field, low, high, shared) for a, y in pairs])
    pack(forward, [extended_first(a, 6 + y, field, low, high, shared) for a, y in pairs])


def second_edges(field, low, high, shared):
    return pl.pallas_call(
        functools.partial(second_edges_kernel, shared),
        out_shape=[pltpu.VMEM((5, 8, LANES), jnp.float32)] * 2,
        in_specs=[VMEM] * 3,
        out_specs=[VMEM] * 2,
        compiler_params=ROOM,
        name="second_edges",
    )(*near(field, low, high))


def solve_kernel(count, shared, field, low, high, below, above, table, valid, *refs):
    if shared:
        folded, rims, backward, forward, inner, size_row, assembled, blocks, left, right, pair = refs
    else:
        folded, rims, backward, forward, inner, blocks, left, right, pair = refs
    low, high = Unpacked(low, 8), Unpacked(high, 8)
    below, above = Unpacked(below, 2), Unpacked(above, 2)
    blocks[pl.ds(1000, 40), :] = jnp.zeros((40, LANES), jnp.float32)
    left[pl.ds(1000, 40), :] = jnp.zeros((40, LANES), jnp.float32)
    right[pl.ds(1000, 40), :] = jnp.zeros((40, LANES), jnp.float32)
    for a in range(10):
        for b in range(10):
            if b == 0:
                nodes = below[a, 0]
            elif b == 9:
                nodes = above[a, 1]
            else:
                nodes = extended_first(a, b - 1, field, low, high, shared)
                if shared and b == 1:
                    nodes = nodes + below[a, 1]
                if shared and b == 8:
                    nodes = nodes + above[a, 0]
                if shared and 1 <= a <= 8:
                    assembled[pl.ds(64 * (a - 1) + 8 * (b - 1), 8), :] = nodes
            blocks[pl.ds(100 * a + 10 * b + 1, 8), :] = nodes
    blocks[pl.ds(0, 100, stride=10), :] = pltpu.roll(
        blocks[pl.ds(7, 100, stride=10), :], 1, 1
    )
    blocks[pl.ds(9, 100, stride=10), :] = pltpu.roll(
        blocks[pl.ds(2, 100, stride=10), :], LANES - 1, 1
    )
    for n in range(10):
        pair[pl.ds(10 * n, 10), :] = table[310 + n : 311 + n, :] + table[320:330, :]
    solve_step(blocks, left, table, 200, False)
    solve_step(left, right, table, 100, False)
    solve_step(right, left, table, 0, False, pair)
    solve_step(left, right, table, 200, True)
    solve_step(right, left, table, 100, True)
    solve_step(left, right, table, 0, True)
    exists = valid[...] > 0.0
    own = own_lanes(count)
    unit = 1.0
    if shared:
        largest = jnp.zeros((8, LANES), jnp.float32)
        for row in range(0, 1000, 8):
            largest = jnp.maximum(largest, jnp.abs(blocks[row : row + 8, :]))
        size = jnp.max(jnp.where(own, largest, 0.0))
        unit = 1.0 / jnp.where(size > 0.0, size, 1.0)
        size_row[...] = jnp.full((1, LANES), size, jnp.float32)
    total = jnp.zeros((8, LANES), jnp.float32)
    for row in range(0, 1000, 8):
        total = total + (blocks[row : row + 8, :] * unit) * (right[row : row + 8, :] * unit)
    inner[...] = jnp.sum(jnp.where(own, total, 0.0), axis=0, keepdims=True)

    def entry(c):
        return jnp.where(exists, right[pl.ds(c, 100, stride=10), :], 0.0)

    first, second, second_last, last = entry(0), entry(1), entry(8), entry(9)
    right[pl.ds(1, 100, stride=10), :] = second + pltpu.roll(second_last, 1, 1)
    right[pl.ds(2, 100, stride=10), :] = entry(2) + pltpu.roll(last, 1, 1)
    right[pl.ds(7, 100, stride=10), :] = entry(7) + pltpu.roll(first, LANES - 1, 1)
    right[pl.ds(8, 100, stride=10), :] = second_last + pltpu.roll(second, LANES - 1, 1)
    for a in range(10):
        for b in range(10):
            nodes = right[pl.ds(100 * a + 10 * b + 1, 8), :]
            folded[a, b] = nodes
            if a < 2:
                rims[a, b] = nodes
            if a > 7:
                rims[a - 6, b] = nodes
    pairs = [(a, b) for a in range(10) for b in range(2)]
    pack(backward, [folded[a, b] for a, b in pairs])
    pack(forward, [folded[a, b + 8] for a, b in pairs])


def block_solve(field, low, high, below, above, table, valid, count, shared):
    row = pltpu.VMEM((1, LANES), jnp.float32)
    edge = pltpu.VMEM((5, 8, LANES), jnp.float32)
    outs = [
        pltpu.VMEM((10, 10, 8, LANES), jnp.float32),
        pltpu.VMEM((4, 10, 8, LANES), jnp.float32),
        edge,
        edge,
        row,
    ]
    if shared:
        outs += [row, pltpu.VMEM((512, LANES), jnp.float32)]
    return pl.pallas_call(
        functools.partial(solve_kernel, count, shared),
        out_shape=outs,
        scratch_shapes=[pltpu.VMEM((1040, LANES), jnp.float32)] * 3
        + [pltpu.VMEM((112, LANES), jnp.float32)],
        in_specs=[VMEM] * 7,
        out_specs=[VMEM] * len(outs),
        compiler_params=ROOM,
        name="block_solve_shared" if shared else "block_solve_first",
    )(*near(field, low, high, below, above, table, valid))


def folded_second(values, a, y, at, below, above):
    nodes = values[a, y + 1]
    if y < 2:
        nodes = nodes + below[at, y]
    if y > 5:
        nodes = nodes + above[at, y - 6]
    return nodes


def first_edges_kernel(rims, below, above, backward, forward):
    below, above = Unpacked(below, 2), Unpacked(above, 2)
    pairs = [(a, y) for a in range(2) for y in range(8)]
    pack(backward, [folded_second(rims, a, y, a, below, above) for a, y in pairs])
    pack(forward, [folded_second(rims, a + 2, y, a + 8, below, above) for a, y in pairs])


def first_edges(rims, below, above):
    return pl.pallas_call(
        first_edges_kernel,
        out_shape=[pltpu.VMEM((4, 8, LANES), jnp.float32)] * 2,
        in_specs=[VMEM] * 3,
        out_specs=[VMEM] * 2,
        compiler_params=ROOM,
        name="first_edges",
    )(*near(rims, below, above))


def both_ways(nodes, metric, derivative):
    slopes = []
    for a in range(8):
        total = None
        for i in range(8):
            if derivative[a, i] != 0.0:
                term = float(derivative[a, i]) * nodes[i]
                total = term if total is None else total + term
        slopes.append(metric[a] * total)
    outs = []
    for i in range(8):
        total = None
        for a in range(8):
            if derivative[a, i] != 0.0:
                term = float(derivative[a, i]) * slopes[a]
                total = term if total is None else total + term
        outs.append(total)
    return outs


def to_lines(sources, count):
    lane = lax.broadcasted_iota(jnp.int32, (LANES, LANES), 0)
    place = lax.broadcasted_iota(jnp.int32, (LANES, LANES), 1)
    total = jnp.zeros((64 * len(sources), LANES), jnp.float32)
    for k in range(8):
        pick = (
            (place == 8 * (lane - REACH) + k) & (lane >= REACH) & (lane < REACH + count)
        ).astype(jnp.bfloat16)
        rest = jnp.concatenate([s[pl.ds(k, 64, stride=8), :] for s in sources], axis=0)
        rest = jnp.where(own_lanes(count), rest, 0.0)
        for _ in range(3):
            part = rest.astype(jnp.bfloat16)
            total = total + jnp.dot(part, pick, preferred_element_type=jnp.float32)
            rest = rest - part.astype(jnp.float32)
    return total


def in_parts(values):
    parts = []
    for _ in range(3):
        part = values.astype(jnp.bfloat16)
        parts.append(part)
        values = values - part.astype(jnp.float32)
    return parts


def spread_lines(lines, lane_of_element, out, base=None):
    count, length = lines.shape
    node = lax.broadcasted_iota(jnp.int32, (length, 2 * LANES), 0)
    place = lax.broadcasted_iota(jnp.int32, (length, 2 * LANES), 1)
    parts = in_parts(lines)
    for k in range(0, 8, 2):
        wanted = lane_of_element(node // 8) + LANES * (node % 8 - k)
        pick = ((node % 8 >= k) & (node % 8 < k + 2) & (place == wanted)).astype(jnp.bfloat16)
        total = None
        for part in parts:
            term = jnp.dot(part, pick, preferred_element_type=jnp.float32)
            total = term if total is None else total + term
        for half in range(2):
            value = total[:, half * LANES : (half + 1) * LANES]
            spot = pl.ds(k + half, count, stride=8)
            out[spot, :] = value if base is None else value + base[spot, :]


def lane_groups(width, pieces, start):
    lane = lax.broadcasted_iota(jnp.int32, pieces[0].shape, 1)
    total = jnp.zeros(pieces[0].shape, jnp.float32)
    for slot, piece in enumerate(pieces):
        shift = (width * slot - start) % LANES
        moved = pltpu.roll(piece, shift, 1) if shift else piece
        total = jnp.where(lane // width == slot, moved, total)
    return total


def ends_kernel(right_side, geometry, classes, backward, forward):
    field = [right_side[pl.ds(16 * i, 16), :] for i in range(4)]
    metric = [geometry[pl.ds(32 * i, 32), :] for i in range(8)]
    for out, from_end in ((backward, False), (forward, True)):
        out[pl.ds(0, 16), :] = lane_groups(32, field, LANES - 32 if from_end else 0)
        out[pl.ds(16, 32), :] = lane_groups(16, metric, LANES - 16 if from_end else 0)
        out[pl.ds(48, 8), :] = jnp.zeros((8, LANES), jnp.float32)
        out[pl.ds(48, 1), 0 : classes.shape[1]] = classes[...].astype(jnp.float32)


def end_messages(right_side, geometry, classes):
    return pl.pallas_call(
        ends_kernel,
        out_shape=[pltpu.VMEM((56, LANES), jnp.float32)] * 2,
        in_specs=[VMEM] * 3,
        out_specs=[VMEM] * 2,
        compiler_params=ROOM,
        name="end_messages",
    )(*near(right_side, geometry, classes))


def received_lines(low, high, first, rows, width):
    low, high = low[pl.ds(first, rows), :], high[pl.ds(first, rows), :]
    lane = lax.broadcasted_iota(jnp.int32, (rows, LANES), 1)
    lines = []
    for slot in range(LANES // width):
        before = pltpu.roll(low, (-width * slot) % LANES, 1) if slot else low
        after = pltpu.roll(high, (width - width * slot) % LANES, 1) if slot != 1 else high
        lines.append(jnp.where(lane < width, before, jnp.where(lane < 2 * width, after, 0.0)))
    return jnp.concatenate(lines, axis=0)


def own_lines_kernel(right_side, geometry, field, metric):
    spread_lines(right_side[...], lambda e: e + REACH, field)
    spread_lines(geometry[...], lambda e: e + REACH, metric)


def own_lines(right_side, geometry):
    return pl.pallas_call(
        own_lines_kernel,
        out_shape=[
            pltpu.VMEM((512, LANES), jnp.float32),
            pltpu.VMEM((2048, LANES), jnp.float32),
        ],
        in_specs=[VMEM] * 2,
        out_specs=[VMEM] * 2,
        compiler_params=ROOM,
        name="own_lines",
    )(*near(right_side, geometry))


def pack_ends(field, backward, forward):
    pack(backward, [field[pl.ds(8 * i, 8), :] for i in range(16)])
    pack(forward, [field[pl.ds(384 + 8 * i, 8), :] for i in range(16)])


def end_lines_kernel(count, field_too, low, high, own, out, *edges):
    if field_too:
        lines = received_lines(low, high, 0, 16, 32)
        spread_lines(lines, lambda e: jnp.where(e < REACH, e, e + count), out, own)
        pack_ends(out, *edges)
    else:
        lines = received_lines(low, high, 16, 32, 16)
        spread_lines(lines, lambda e: e + REACH - 2 + jnp.where(e < 2, 0, count), out, own)


def end_lines(low, high, own, count, field_too):
    outs = [pltpu.VMEM(own.shape, jnp.float32)]
    if field_too:
        outs += [pltpu.VMEM((4, 8, LANES), jnp.float32)] * 2
    return pl.pallas_call(
        functools.partial(end_lines_kernel, count, field_too),
        out_shape=outs,
        in_specs=[VMEM] * 3,
        out_specs=[VMEM] * len(outs),
        compiler_params=ROOM,
        name="end_lines_field" if field_too else "end_lines_metric",
    )(*near(low, high, own))


def apply_local(derivative, folded, below, above, low, high, geometry, field, image):
    below, above = Unpacked(below, 2), Unpacked(above, 2)
    low, high = Unpacked(low, 8), Unpacked(high, 8)
    for x in range(8):
        for y in range(8):
            nodes = folded_second(folded, x + 1, y, x + 1, below, above)
            if x < 2:
                nodes = nodes + low[x, y]
            if x > 5:
                nodes = nodes + high[x - 6, y]
            field[pl.ds(64 * x + 8 * y, 8), :] = nodes
    for row in range(0, 512, 8):
        image[row : row + 8, :] = geometry[1536 + row : 1544 + row, :] * field[row : row + 8, :]
    for line in range(8):
        for dim in range(3):
            if dim == 0:
                spots = [pl.ds(64 * i + 8 * line, 8) for i in range(8)]
                places = spots
            elif dim == 1:
                spots = [pl.ds(64 * line + 8 * i, 8) for i in range(8)]
                places = [pl.ds(512 + 64 * line + 8 * i, 8) for i in range(8)]
            else:
                spots = [pl.ds(64 * line + i, 8, stride=8) for i in range(8)]
                places = [pl.ds(1024 + 64 * line + i, 8, stride=8) for i in range(8)]
            outs = both_ways(
                [field[s, :] for s in spots], [geometry[s, :] for s in places], derivative
            )
            for spot, out in zip(spots, outs):
                image[spot, :] = image[spot, :] + out


def first_operator_kernel(
    count, derivative, folded, below, above, low, high, geometry, field, image, backward, forward, inner
):
    apply_local(derivative, folded, below, above, low, high, geometry, field, image)
    total = jnp.zeros((8, LANES), jnp.float32)
    for row in range(0, 512, 8):
        total = total + field[row : row + 8, :] * image[row : row + 8, :]
    inner[...] = jnp.sum(jnp.where(own_lanes(count), total, 0.0), axis=0, keepdims=True)
    first = image[pl.ds(0, 64, stride=8), :]
    last = image[pl.ds(7, 64, stride=8), :]
    image[pl.ds(0, 64, stride=8), :] = first + pltpu.roll(last, 1, 1)
    image[pl.ds(7, 64, stride=8), :] = last + pltpu.roll(first, LANES - 1, 1)
    pack_ends(image, backward, forward)


def first_operator(folded, below, above, low, high, geometry, count):
    full = pltpu.VMEM((512, LANES), jnp.float32)
    edge = pltpu.VMEM((4, 8, LANES), jnp.float32)
    return pl.pallas_call(
        functools.partial(first_operator_kernel, count, derivative_table()),
        out_shape=[full, full, edge, edge, pltpu.VMEM((1, LANES), jnp.float32)],
        in_specs=[VMEM] * 6,
        out_specs=[VMEM] * 5,
        compiler_params=ROOM,
        name="first_operator",
    )(*near(folded, below, above, low, high, geometry))


def second_operator_kernel(
    count,
    derivative,
    spot,
    folded,
    below,
    above,
    low,
    high,
    geometry,
    rho,
    d,
    g,
    size,
    lines,
    payload,
    field,
    image,
):
    apply_local(derivative, folded, below, above, low, high, geometry, field, image)
    largest = jnp.max(size[...])
    unit = 1.0 / jnp.where(largest > 0.0, largest, 1.0)
    own = own_lanes(count)
    total = jnp.zeros((8, LANES), jnp.float32)
    for row in range(0, 512, 8):
        total = total + (field[row : row + 8, :] * unit) * (image[row : row + 8, :] * unit)
    h = jnp.sum(jnp.where(own, total, 0.0))
    lane = lax.broadcasted_iota(jnp.int32, (1, LANES), 1)
    scalars = jnp.zeros((1, LANES), jnp.float32)
    sums = (jnp.sum(rho[...]), jnp.sum(d[...]), jnp.sum(g[...]), h, largest)
    for place, value in enumerate(sums):
        scalars = jnp.where(lane == 64 + place, value, scalars)
    both = to_lines([field, image], count)
    lines[...] = both
    line = lax.broadcasted_iota(jnp.int32, (64, LANES), 0)
    across = lax.broadcasted_iota(jnp.int32, (64, LANES), 1)
    first = jnp.sum(jnp.where(line == across, both[64:, 0:1], 0.0), axis=0, keepdims=True)
    last = jnp.sum(
        jnp.where(line == across, both[64:, LANES - 1 : LANES], 0.0), axis=0, keepdims=True
    )
    for target in range(payload.shape[0]):
        end = jnp.where(target == spot[2] + 1, last, jnp.where(target == spot[2] - 1, first, 0.0))
        payload[target] = scalars + end


def second_operator(spot, folded, below, above, low, high, geometry, sums, count, devices):
    return pl.pallas_call(
        functools.partial(second_operator_kernel, count, derivative_table()),
        out_shape=[
            pltpu.VMEM((128, LANES), jnp.float32),
            pltpu.VMEM((devices, 1, LANES), jnp.float32),
        ],
        in_specs=[SMEM] + [VMEM] * 10,
        out_specs=[VMEM, VMEM],
        scratch_shapes=[pltpu.VMEM((512, LANES), jnp.float32)] * 2,
        compiler_params=ROOM,
        name="second_operator",
    )(spot, *near(folded, below, above, low, high, geometry, *sums))


def lines_kernel(count, one, two, lines):
    lines[...] = to_lines([one, two], count)


def as_lines(one, two, count):
    return pl.pallas_call(
        functools.partial(lines_kernel, count),
        out_shape=pltpu.VMEM((128, LANES), jnp.float32),
        in_specs=[VMEM] * 2,
        out_specs=VMEM,
        compiler_params=ROOM,
        name="as_lines",
    )(*near(one, two))


def combine(columns):
    size = jnp.max(columns[4])
    ratio = columns[4] / jnp.where(size > 0.0, size, 1.0)
    factor = ratio * ratio
    return (
        jnp.sum(columns[0]),
        jnp.sum(columns[1]),
        jnp.sum(columns[2] * factor),
        jnp.sum(columns[3] * factor),
        size,
    )


NEIGHBOURS = [(dx, dy) for dx in (-1, 0, 1) for dy in (-1, 0, 1) if (dx, dy) != (0, 0)]


def middle_kernel(sizes, spot, gathered, lines, image, out, joined):
    for device in range(gathered.shape[0]):
        joined[pl.ds(device, 1), :] = gathered[device]
    rows = joined[...]
    values = combine([rows[:, 64 + i : 65 + i] for i in range(5)])
    source = lax.broadcasted_iota(jnp.int32, rows.shape, 0)
    before = jnp.sum(jnp.where(source == spot[2] - 1, rows, 0.0), axis=0, keepdims=True)
    after = jnp.sum(jnp.where(source == spot[2] + 1, rows, 0.0), axis=0, keepdims=True)
    line = lax.broadcasted_iota(jnp.int32, (64, LANES), 0)
    across = lax.broadcasted_iota(jnp.int32, (64, LANES), 1)
    before = jnp.sum(jnp.where(line == across, before, 0.0), axis=1, keepdims=True)
    after = jnp.sum(jnp.where(line == across, after, 0.0), axis=1, keepdims=True)
    t = lines[64:, :]
    behind = pltpu.roll(t, 1, 1)
    ahead = pltpu.roll(t, LANES - 1, 1)
    image[...] = t + jnp.where(
        across % 8 == 7,
        jnp.where(across == LANES - 1, after, ahead),
        jnp.where(across % 8 == 0, jnp.where(across == 0, before, behind), 0.0),
    )
    row = lax.broadcasted_iota(jnp.int32, (8, LANES), 0)
    lane = lax.broadcasted_iota(jnp.int32, (8, LANES), 1)
    scalars = jnp.zeros((8, LANES), jnp.float32)
    for place, value in enumerate(values):
        scalars = jnp.where(row == place, value, scalars)
    scalars = jnp.where(lane == 8, scalars, 0.0)
    for device in range(sizes[0] * sizes[1]):
        out[pl.ds(8 * device, 8), :] = scalars
    for dx, dy in NEIGHBOURS:
        x, y = spot[0] + dx, spot[1] + dy
        at_x, at_y = (7 if dx > 0 else 0), (7 if dy > 0 else 0)
        if dy == 0:
            face = image[pl.ds(8 * at_x, 8), :]
        elif dx == 0:
            face = image[pl.ds(at_y, 8, stride=8), :]
        else:
            face = jnp.broadcast_to(image[pl.ds(8 * at_x + at_y, 1), :], (8, LANES))
        tile = jnp.where(lane == 8, scalars, face)

        @pl.when((x >= 0) & (x < sizes[0]) & (y >= 0) & (y < sizes[1]))
        def _():
            out[pl.ds(pl.multiple_of(8 * (x * sizes[1] + y), 8), 8), :] = tile


def middle(spot, gathered, lines, sizes):
    return pl.pallas_call(
        functools.partial(middle_kernel, sizes),
        out_shape=[
            pltpu.VMEM((64, LANES), jnp.float32),
            pltpu.VMEM((8 * sizes[0] * sizes[1], LANES), jnp.float32),
        ],
        in_specs=[SMEM, VMEM, VMEM],
        out_specs=[VMEM, VMEM],
        scratch_shapes=[pltpu.VMEM((gathered.shape[0], LANES), jnp.float32)],
        compiler_params=ROOM,
        name="middle",
    )(spot, *near(gathered, lines))


def finish_kernel(
    sizes, spot, gathered, image, second, first, right_side, solution_out, residual_out, t
):
    plane = sizes[0] * sizes[1]
    columns = [gathered[pl.ds(i, plane, stride=8), :][:, 8:9] for i in range(5)]
    rho, d, g_scaled, h_scaled, size = combine(columns)
    t[...] = image[...]
    lane = lax.broadcasted_iota(jnp.int32, (8, LANES), 1)
    for dx, dy in NEIGHBOURS:
        x, y = spot[0] + dx, spot[1] + dy
        inside = (x >= 0) & (x < sizes[0]) & (y >= 0) & (y < sizes[1])
        source = jnp.where(inside, x * sizes[1] + y, 0)
        tile = gathered[pl.ds(pl.multiple_of(8 * source, 8), 8), :]
        tile = jnp.where(lane == 8, pltpu.roll(tile, 1, 1), tile)
        tile = jnp.where(inside, tile, 0.0)
        at_x, at_y = (7 if dx > 0 else 0), (7 if dy > 0 else 0)
        if dy == 0:
            spots = pl.ds(8 * at_x, 8)
        elif dx == 0:
            spots = pl.ds(at_y, 8, stride=8)
        else:
            spots = pl.ds(8 * at_x + at_y, 1)
            tile = tile[0:1, :]
        t[spots, :] = t[spots, :] + tile

    def splat(value):
        return jnp.full((1, LANES), value, jnp.float32)

    rho, d = splat(rho), splat(d)
    alpha_one = rho / d
    reach = alpha_one * splat(size)
    g = reach * reach * splat(g_scaled)
    h = reach * reach * splat(h_scaled)
    stretch = g / rho
    alpha_two = (g - rho) / (h - stretch * g / alpha_one)
    along = alpha_one + alpha_two * stretch
    turn = alpha_one * alpha_two
    solution_out[...] = along * first[0:64, :] - turn * second[0:64, :]
    residual_out[...] = right_side[...] - along * first[64:128, :] + turn * t[...]


def finish(spot, gathered, image, second, first, right_side, sizes):
    full = jax.ShapeDtypeStruct((64, LANES), jnp.float32)
    return pl.pallas_call(
        functools.partial(finish_kernel, sizes),
        out_shape=[full, full],
        in_specs=[SMEM] + [VMEM] * 5,
        out_specs=[VMEM, VMEM],
        scratch_shapes=[pltpu.VMEM((64, LANES), jnp.float32)],
        compiler_params=ROOM,
        name="finish",
    )(spot, *near(gathered, image, second, first, right_side))


def exchange(rows, axes):
    return lax.all_to_all(rows, axes, 0, 0, tiled=True)


def on_device(right_side, geometry, element_shape_class, fdm_vectors, fdm_values):
    count = element_shape_class.shape[2]
    classes = fdm_vectors.shape[0]
    depth = lax.axis_size("gz")
    sizes = (lax.axis_size("gx"), lax.axis_size("gy"))
    spot = jnp.stack([lax.axis_index(a).astype(jnp.int32) for a in ("gx", "gy", "gz")])
    lines = right_side.reshape(64, LANES)
    metric_lines = geometry.reshape(256, LANES)
    flat_class = element_shape_class.reshape(1, count)
    before, after = swap(*end_messages(lines, metric_lines, flat_class), "gz")
    own_field, own_metric = own_lines(lines, metric_lines)
    deep_class = jnp.concatenate(
        [
            before[48, count - REACH : count].astype(jnp.int32),
            flat_class[0],
            after[48, :REACH].astype(jnp.int32),
        ]
    )
    deep_class = jnp.pad(deep_class, (0, LANES - deep_class.shape[0]))
    element = jnp.arange(LANES, dtype=jnp.int32) - REACH + spot[2] * count
    valid = ((element >= 0) & (element < depth * count)).astype(jnp.float32)[None, :]
    onehot = (jnp.arange(classes, dtype=jnp.int32)[:, None] == deep_class[None, :]).astype(
        jnp.float32
    )
    entries = jnp.concatenate(
        [fdm_vectors.reshape(classes, 300), fdm_values.reshape(classes, 30)], axis=1
    )
    table = lax.dot_general(
        entries, onehot, (((0,), (0,)), ((), ())), precision=HIGHEST
    )
    field, backward, forward = end_lines(before, after, own_field, count, True)
    low, high = swap(backward, forward, "gx")
    (metric,) = end_lines(before, after, own_metric, count, False)
    low, high, metric, table = lax.optimization_barrier((low, high, metric, table))
    below, above = swap(*second_edges(field, low, high, False), "gy")
    folded, rims, backward, forward, rho = block_solve(
        field, low, high, below, above, table, valid, count, False
    )
    below, above = swap(backward, forward, "gy")
    low, high = swap(*first_edges(rims, below, above), "gx")
    p, image, backward, forward, d = first_operator(
        folded, below, above, low, high, metric, count
    )
    low, high = swap(backward, forward, "gx")
    below, above = swap(*second_edges(image, low, high, True), "gy")
    folded, rims, backward, forward, g, size, q = block_solve(
        image, low, high, below, above, table, valid, count, True
    )
    below, above = swap(backward, forward, "gy")
    first = as_lines(p, q, count)
    below, above, first = lax.optimization_barrier((below, above, first))
    low, high = swap(*first_edges(rims, below, above), "gx")
    second, payload = second_operator(
        spot, folded, below, above, low, high, own_metric, (rho, d, g, size), count, depth
    )
    gathered = exchange(payload, "gz")
    image, tiles = middle(spot, gathered, second, sizes)
    gathered = exchange(tiles, ("gx", "gy"))
    answer, left = finish(spot, gathered, image, second, first, lines, sizes)
    return (answer.reshape(8, 8, LANES), left.reshape(8, 8, LANES))


def solution(mesh):
    placed = (P("gx", "gy", "gz"), P(None, "gx", "gy", "gz"), P("gx", "gy", "gz"), P(), P())
    return jax.shard_map(
        on_device,
        mesh=mesh,
        in_specs=placed,
        out_specs=(P("gx", "gy", "gz"), P("gx", "gy", "gz")),
        check_vma=False,
    )
```

```python
import functools

import jax
import jax.numpy as jnp
import numpy as np
from jax import lax
from jax.experimental import pallas as pl
from jax.experimental.pallas import tpu as pltpu
from jax.sharding import PartitionSpec as P

HIGHEST = lax.Precision.HIGHEST
LANES = 128
REACH = 4
GROUP = 32
SMEM = pl.BlockSpec(memory_space=pltpu.SMEM)
VMEM = pl.BlockSpec(memory_space=pltpu.VMEM)
ROOM = pltpu.CompilerParams(vmem_limit_bytes=8 << 20)
CHUNKS = ((0, 24), (24, 24), (48, 24), (72, 28))


def swap(backward_part, forward_part, axis):
    count = lax.axis_size(axis)
    forward = [(i, i + 1) for i in range(count - 1)]
    backward = [(target, source) for source, target in forward]
    return lax.ppermute(forward_part, axis, forward), lax.ppermute(backward_part, axis, backward)


def derivative_table():
    points = np.array(
        [
            -1.0,
            -0.8717401485096066,
            -0.5917001814331423,
            -0.2092992179024789,
            0.2092992179024789,
            0.5917001814331423,
            0.8717401485096066,
            1.0,
        ]
    )
    previous = np.ones(8)
    current = points * 1.0
    for order in range(1, 7):
        following = ((2 * order + 1) * points * current - order * previous) / (order + 1)
        previous = current
        current = following
    spacing = points[:, None] - points[None, :] + np.eye(8)
    off_diagonal = current[:, None] / (current[None, :] * spacing)
    positions = np.arange(8)
    end_values = np.where(positions == 0, -14.0, 0.0) + np.where(positions == 7, 14.0, 0.0)
    return np.where(np.eye(8) > 0, np.eye(8) * end_values[None, :], off_diagonal)


def near(*arrays):
    return [pltpu.with_memory_space_constraint(array, pltpu.VMEM) for array in arrays]


def own_lanes(count):
    lane = lax.broadcasted_iota(jnp.int32, (1, LANES), 1)
    return (lane >= REACH) & (lane < REACH + count)


def solve_step(source, target, table, base, transposed, scale=None):
    for start, size in CHUNKS:
        entries = [source[pl.ds(10 * start + k, size, stride=10), :] for k in range(10)]
        for out in range(10):
            total = None
            for k in range(10):
                row = base + (10 * out + k if transposed else 10 * k + out)
                term = table[row : row + 1, :] * entries[k]
                total = term if total is None else total + term
            if scale is not None:
                total = total / (table[300 + out : 301 + out, :] + scale[start : start + size, :])
            target[pl.ds(100 * out + start, size), :] = total


def pack(out, pieces):
    lane = lax.broadcasted_iota(jnp.int32, (8, LANES), 1)
    for place in range(len(pieces) // 4):
        total = pieces[4 * place]
        for slot in range(1, 4):
            moved = pltpu.roll(pieces[4 * place + slot], GROUP * slot, 1)
            total = jnp.where(lane >= GROUP * slot, moved, total)
        out[place] = total


class Unpacked:
    def __init__(self, ref, width):
        self.ref, self.width = ref, width

    def __getitem__(self, index):
        place = self.width * index[0] + index[1]
        piece = self.ref[place // 4]
        slot = place % 4
        return piece if slot == 0 else pltpu.roll(piece, LANES - GROUP * slot, 1)


def extended_first(a, y, field, low, high, shared):
    if a == 0:
        return low[0, y]
    if a == 9:
        return high[1, y]
    nodes = field[pl.ds(64 * (a - 1) + 8 * y, 8), :]
    if shared and a == 1:
        nodes = nodes + low[1, y]
    if shared and a == 8:
        nodes = nodes + high[0, y]
    return nodes


def second_edges_kernel(shared, field, low, high, backward, forward):
    low, high = Unpacked(low, 8), Unpacked(high, 8)
    pairs = [(a, y) for a in range(10) for y in range(2)]
    pack(backward, [extended_first(a, y, field, low, high, shared) for a, y in pairs])
    pack(forward, [extended_first(a, 6 + y, field, low, high, shared) for a, y in pairs])


def second_edges(field, low, high, shared):
    return pl.pallas_call(
        functools.partial(second_edges_kernel, shared),
        out_shape=[pltpu.VMEM((5, 8, LANES), jnp.float32)] * 2,
        in_specs=[VMEM] * 3,
        out_specs=[VMEM] * 2,
        compiler_params=ROOM,
        name="second_edges",
    )(*near(field, low, high))


def solve_kernel(count, shared, field, low, high, below, above, table, valid, *refs):
    if shared:
        folded, rims, backward, forward, inner, size_row, assembled, blocks, left, right, pair = refs
    else:
        folded, rims, backward, forward, inner, blocks, left, right, pair = refs
    low, high = Unpacked(low, 8), Unpacked(high, 8)
    below, above = Unpacked(below, 2), Unpacked(above, 2)
    blocks[pl.ds(1000, 40), :] = jnp.zeros((40, LANES), jnp.float32)
    left[pl.ds(1000, 40), :] = jnp.zeros((40, LANES), jnp.float32)
    right[pl.ds(1000, 40), :] = jnp.zeros((40, LANES), jnp.float32)
    for a in range(10):
        for b in range(10):
            if b == 0:
                nodes = below[a, 0]
            elif b == 9:
                nodes = above[a, 1]
            else:
                nodes = extended_first(a, b - 1, field, low, high, shared)
                if shared and b == 1:
                    nodes = nodes + below[a, 1]
                if shared and b == 8:
                    nodes = nodes + above[a, 0]
                if shared and 1 <= a <= 8:
                    assembled[pl.ds(64 * (a - 1) + 8 * (b - 1), 8), :] = nodes
            blocks[pl.ds(100 * a + 10 * b + 1, 8), :] = nodes
    blocks[pl.ds(0, 100, stride=10), :] = pltpu.roll(
        blocks[pl.ds(7, 100, stride=10), :], 1, 1
    )
    blocks[pl.ds(9, 100, stride=10), :] = pltpu.roll(
        blocks[pl.ds(2, 100, stride=10), :], LANES - 1, 1
    )
    for n in range(10):
        pair[pl.ds(10 * n, 10), :] = table[310 + n : 311 + n, :] + table[320:330, :]
    solve_step(blocks, left, table, 200, False)
    solve_step(left, right, table, 100, False)
    solve_step(right, left, table, 0, False, pair)
    solve_step(left, right, table, 200, True)
    solve_step(right, left, table, 100, True)
    solve_step(left, right, table, 0, True)
    exists = valid[...] > 0.0
    own = own_lanes(count)
    unit = 1.0
    if shared:
        largest = jnp.zeros((8, LANES), jnp.float32)
        for row in range(0, 1000, 8):
            largest = jnp.maximum(largest, jnp.abs(blocks[row : row + 8, :]))
        size = jnp.max(jnp.where(own, largest, 0.0))
        unit = 1.0 / jnp.where(size > 0.0, size, 1.0)
        size_row[...] = jnp.full((1, LANES), size, jnp.float32)
    total = jnp.zeros((8, LANES), jnp.float32)
    for row in range(0, 1000, 8):
        total = total + (blocks[row : row + 8, :] * unit) * (right[row : row + 8, :] * unit)
    inner[...] = jnp.sum(jnp.where(own, total, 0.0), axis=0, keepdims=True)

    def entry(c):
        return jnp.where(exists, right[pl.ds(c, 100, stride=10), :], 0.0)

    first, second, second_last, last = entry(0), entry(1), entry(8), entry(9)
    right[pl.ds(1, 100, stride=10), :] = second + pltpu.roll(second_last, 1, 1)
    right[pl.ds(2, 100, stride=10), :] = entry(2) + pltpu.roll(last, 1, 1)
    right[pl.ds(7, 100, stride=10), :] = entry(7) + pltpu.roll(first, LANES - 1, 1)
    right[pl.ds(8, 100, stride=10), :] = second_last + pltpu.roll(second, LANES - 1, 1)
    for a in range(10):
        for b in range(10):
            nodes = right[pl.ds(100 * a + 10 * b + 1, 8), :]
            folded[a, b] = nodes
            if a < 2:
                rims[a, b] = nodes
            if a > 7:
                rims[a - 6, b] = nodes
    pairs = [(a, b) for a in range(10) for b in range(2)]
    pack(backward, [folded[a, b] for a, b in pairs])
    pack(forward, [folded[a, b + 8] for a, b in pairs])


def block_solve(field, low, high, below, above, table, valid, count, shared):
    row = pltpu.VMEM((1, LANES), jnp.float32)
    edge = pltpu.VMEM((5, 8, LANES), jnp.float32)
    outs = [
        pltpu.VMEM((10, 10, 8, LANES), jnp.float32),
        pltpu.VMEM((4, 10, 8, LANES), jnp.float32),
        edge,
        edge,
        row,
    ]
    if shared:
        outs += [row, pltpu.VMEM((512, LANES), jnp.float32)]
    return pl.pallas_call(
        functools.partial(solve_kernel, count, shared),
        out_shape=outs,
        scratch_shapes=[pltpu.VMEM((1040, LANES), jnp.float32)] * 3
        + [pltpu.VMEM((112, LANES), jnp.float32)],
        in_specs=[VMEM] * 7,
        out_specs=[VMEM] * len(outs),
        compiler_params=ROOM,
        name="block_solve_shared" if shared else "block_solve_first",
    )(*near(field, low, high, below, above, table, valid))


def folded_second(values, a, y, at, below, above):
    nodes = values[a, y + 1]
    if y < 2:
        nodes = nodes + below[at, y]
    if y > 5:
        nodes = nodes + above[at, y - 6]
    return nodes


def first_edges_kernel(rims, below, above, backward, forward):
    below, above = Unpacked(below, 2), Unpacked(above, 2)
    pairs = [(a, y) for a in range(2) for y in range(8)]
    pack(backward, [folded_second(rims, a, y, a, below, above) for a, y in pairs])
    pack(forward, [folded_second(rims, a + 2, y, a + 8, below, above) for a, y in pairs])


def first_edges(rims, below, above):
    return pl.pallas_call(
        first_edges_kernel,
        out_shape=[pltpu.VMEM((4, 8, LANES), jnp.float32)] * 2,
        in_specs=[VMEM] * 3,
        out_specs=[VMEM] * 2,
        compiler_params=ROOM,
        name="first_edges",
    )(*near(rims, below, above))


def both_ways(nodes, metric, derivative):
    slopes = []
    for a in range(8):
        total = None
        for i in range(8):
            if derivative[a, i] != 0.0:
                term = float(derivative[a, i]) * nodes[i]
                total = term if total is None else total + term
        slopes.append(metric[a] * total)
    outs = []
    for i in range(8):
        total = None
        for a in range(8):
            if derivative[a, i] != 0.0:
                term = float(derivative[a, i]) * slopes[a]
                total = term if total is None else total + term
        outs.append(total)
    return outs


def to_lines(sources, count):
    lane = lax.broadcasted_iota(jnp.int32, (LANES, LANES), 0)
    place = lax.broadcasted_iota(jnp.int32, (LANES, LANES), 1)
    total = jnp.zeros((64 * len(sources), LANES), jnp.float32)
    for k in range(8):
        pick = (
            (place == 8 * (lane - REACH) + k) & (lane >= REACH) & (lane < REACH + count)
        ).astype(jnp.bfloat16)
        rest = jnp.concatenate([s[pl.ds(k, 64, stride=8), :] for s in sources], axis=0)
        rest = jnp.where(own_lanes(count), rest, 0.0)
        for _ in range(3):
            part = rest.astype(jnp.bfloat16)
            total = total + jnp.dot(part, pick, preferred_element_type=jnp.float32)
            rest = rest - part.astype(jnp.float32)
    return total


def in_parts(values):
    parts = []
    for _ in range(3):
        part = values.astype(jnp.bfloat16)
        parts.append(part)
        values = values - part.astype(jnp.float32)
    return parts


def spread_lines(lines, lane_of_element, out, base=None):
    count, length = lines.shape
    node = lax.broadcasted_iota(jnp.int32, (length, 2 * LANES), 0)
    place = lax.broadcasted_iota(jnp.int32, (length, 2 * LANES), 1)
    parts = in_parts(lines)
    for k in range(0, 8, 2):
        wanted = lane_of_element(node // 8) + LANES * (node % 8 - k)
        pick = ((node % 8 >= k) & (node % 8 < k + 2) & (place == wanted)).astype(jnp.bfloat16)
        total = None
        for part in parts:
            term = jnp.dot(part, pick, preferred_element_type=jnp.float32)
            total = term if total is None else total + term
        for half in range(2):
            value = total[:, half * LANES : (half + 1) * LANES]
            spot = pl.ds(k + half, count, stride=8)
            out[spot, :] = value if base is None else value + base[spot, :]


def lane_groups(width, pieces, start):
    lane = lax.broadcasted_iota(jnp.int32, pieces[0].shape, 1)
    total = jnp.zeros(pieces[0].shape, jnp.float32)
    for slot, piece in enumerate(pieces):
        shift = (width * slot - start) % LANES
        moved = pltpu.roll(piece, shift, 1) if shift else piece
        total = jnp.where(lane // width == slot, moved, total)
    return total


def ends_kernel(right_side, geometry, classes, backward, forward):
    field = [right_side[pl.ds(16 * i, 16), :] for i in range(4)]
    metric = [geometry[pl.ds(32 * i, 32), :] for i in range(8)]
    for out, from_end in ((backward, False), (forward, True)):
        out[pl.ds(0, 16), :] = lane_groups(32, field, LANES - 32 if from_end else 0)
        out[pl.ds(16, 32), :] = lane_groups(16, metric, LANES - 16 if from_end else 0)
        out[pl.ds(48, 8), :] = jnp.zeros((8, LANES), jnp.float32)
        out[pl.ds(48, 1), 0 : classes.shape[1]] = classes[...].astype(jnp.float32)


def end_messages(right_side, geometry, classes):
    return pl.pallas_call(
        ends_kernel,
        out_shape=[pltpu.VMEM((56, LANES), jnp.float32)] * 2,
        in_specs=[VMEM] * 3,
        out_specs=[VMEM] * 2,
        compiler_params=ROOM,
        name="end_messages",
    )(
        *[
            pltpu.with_memory_space_constraint(array, pltpu.HBM)
            for array in (right_side, geometry, classes)
        ]
    )


def received_lines(low, high, first, rows, width):
    low, high = low[pl.ds(first, rows), :], high[pl.ds(first, rows), :]
    lane = lax.broadcasted_iota(jnp.int32, (rows, LANES), 1)
    lines = []
    for slot in range(LANES // width):
        before = pltpu.roll(low, (-width * slot) % LANES, 1) if slot else low
        after = pltpu.roll(high, (width - width * slot) % LANES, 1) if slot != 1 else high
        lines.append(jnp.where(lane < width, before, jnp.where(lane < 2 * width, after, 0.0)))
    return jnp.concatenate(lines, axis=0)


def own_lines_kernel(right_side, geometry, field, metric):
    spread_lines(right_side[...], lambda e: e + REACH, field)
    spread_lines(geometry[...], lambda e: e + REACH, metric)


def own_lines(right_side, geometry):
    return pl.pallas_call(
        own_lines_kernel,
        out_shape=[
            pltpu.VMEM((512, LANES), jnp.float32),
            pltpu.VMEM((2048, LANES), jnp.float32),
        ],
        in_specs=[VMEM] * 2,
        out_specs=[VMEM] * 2,
        compiler_params=ROOM,
        name="own_lines",
    )(*near(right_side, geometry))


def pack_ends(field, backward, forward):
    pack(backward, [field[pl.ds(8 * i, 8), :] for i in range(16)])
    pack(forward, [field[pl.ds(384 + 8 * i, 8), :] for i in range(16)])


def end_lines_kernel(count, field_too, low, high, own, out, *edges):
    if field_too:
        lines = received_lines(low, high, 0, 16, 32)
        spread_lines(lines, lambda e: jnp.where(e < REACH, e, e + count), out, own)
        pack_ends(out, *edges)
    else:
        lines = received_lines(low, high, 16, 32, 16)
        spread_lines(lines, lambda e: e + REACH - 2 + jnp.where(e < 2, 0, count), out, own)


def end_lines(low, high, own, count, field_too):
    outs = [pltpu.VMEM(own.shape, jnp.float32)]
    if field_too:
        outs += [pltpu.VMEM((4, 8, LANES), jnp.float32)] * 2
    return pl.pallas_call(
        functools.partial(end_lines_kernel, count, field_too),
        out_shape=outs,
        in_specs=[VMEM] * 3,
        out_specs=[VMEM] * len(outs),
        compiler_params=ROOM,
        name="end_lines_field" if field_too else "end_lines_metric",
    )(*near(low, high, own))


def apply_local(derivative, folded, below, above, low, high, geometry, field, image):
    below, above = Unpacked(below, 2), Unpacked(above, 2)
    low, high = Unpacked(low, 8), Unpacked(high, 8)
    for x in range(8):
        for y in range(8):
            nodes = folded_second(folded, x + 1, y, x + 1, below, above)
            if x < 2:
                nodes = nodes + low[x, y]
            if x > 5:
                nodes = nodes + high[x - 6, y]
            field[pl.ds(64 * x + 8 * y, 8), :] = nodes
    for row in range(0, 512, 8):
        image[row : row + 8, :] = geometry[1536 + row : 1544 + row, :] * field[row : row + 8, :]
    for line in range(8):
        for dim in range(3):
            if dim == 0:
                spots = [pl.ds(64 * i + 8 * line, 8) for i in range(8)]
                places = spots
            elif dim == 1:
                spots = [pl.ds(64 * line + 8 * i, 8) for i in range(8)]
                places = [pl.ds(512 + 64 * line + 8 * i, 8) for i in range(8)]
            else:
                spots = [pl.ds(64 * line + i, 8, stride=8) for i in range(8)]
                places = [pl.ds(1024 + 64 * line + i, 8, stride=8) for i in range(8)]
            outs = both_ways(
                [field[s, :] for s in spots], [geometry[s, :] for s in places], derivative
            )
            for spot, out in zip(spots, outs):
                image[spot, :] = image[spot, :] + out


def first_operator_kernel(
    count, derivative, folded, below, above, low, high, geometry, field, image, backward, forward, inner
):
    apply_local(derivative, folded, below, above, low, high, geometry, field, image)
    total = jnp.zeros((8, LANES), jnp.float32)
    for row in range(0, 512, 8):
        total = total + field[row : row + 8, :] * image[row : row + 8, :]
    inner[...] = jnp.sum(jnp.where(own_lanes(count), total, 0.0), axis=0, keepdims=True)
    first = image[pl.ds(0, 64, stride=8), :]
    last = image[pl.ds(7, 64, stride=8), :]
    image[pl.ds(0, 64, stride=8), :] = first + pltpu.roll(last, 1, 1)
    image[pl.ds(7, 64, stride=8), :] = last + pltpu.roll(first, LANES - 1, 1)
    pack_ends(image, backward, forward)


def first_operator(folded, below, above, low, high, geometry, count):
    full = pltpu.VMEM((512, LANES), jnp.float32)
    edge = pltpu.VMEM((4, 8, LANES), jnp.float32)
    return pl.pallas_call(
        functools.partial(first_operator_kernel, count, derivative_table()),
        out_shape=[full, full, edge, edge, pltpu.VMEM((1, LANES), jnp.float32)],
        in_specs=[VMEM] * 6,
        out_specs=[VMEM] * 5,
        compiler_params=ROOM,
        name="first_operator",
    )(*near(folded, below, above, low, high, geometry))


def second_operator_kernel(
    count,
    derivative,
    spot,
    folded,
    below,
    above,
    low,
    high,
    geometry,
    rho,
    d,
    g,
    size,
    lines,
    payload,
    field,
    image,
):
    apply_local(derivative, folded, below, above, low, high, geometry, field, image)
    largest = jnp.max(size[...])
    unit = 1.0 / jnp.where(largest > 0.0, largest, 1.0)
    own = own_lanes(count)
    total = jnp.zeros((8, LANES), jnp.float32)
    for row in range(0, 512, 8):
        total = total + (field[row : row + 8, :] * unit) * (image[row : row + 8, :] * unit)
    h = jnp.sum(jnp.where(own, total, 0.0))
    lane = lax.broadcasted_iota(jnp.int32, (1, LANES), 1)
    scalars = jnp.zeros((1, LANES), jnp.float32)
    sums = (jnp.sum(rho[...]), jnp.sum(d[...]), jnp.sum(g[...]), h, largest)
    for place, value in enumerate(sums):
        scalars = jnp.where(lane == 64 + place, value, scalars)
    both = to_lines([field, image], count)
    lines[...] = both
    line = lax.broadcasted_iota(jnp.int32, (64, LANES), 0)
    across = lax.broadcasted_iota(jnp.int32, (64, LANES), 1)
    first = jnp.sum(jnp.where(line == across, both[64:, 0:1], 0.0), axis=0, keepdims=True)
    last = jnp.sum(
        jnp.where(line == across, both[64:, LANES - 1 : LANES], 0.0), axis=0, keepdims=True
    )
    for target in range(payload.shape[0]):
        end = jnp.where(target == spot[2] + 1, last, jnp.where(target == spot[2] - 1, first, 0.0))
        payload[target] = scalars + end


def second_operator(spot, folded, below, above, low, high, geometry, sums, count, devices):
    return pl.pallas_call(
        functools.partial(second_operator_kernel, count, derivative_table()),
        out_shape=[
            pltpu.VMEM((128, LANES), jnp.float32),
            pltpu.VMEM((devices, 1, LANES), jnp.float32),
        ],
        in_specs=[SMEM] + [VMEM] * 10,
        out_specs=[VMEM, VMEM],
        scratch_shapes=[pltpu.VMEM((512, LANES), jnp.float32)] * 2,
        compiler_params=ROOM,
        name="second_operator",
    )(spot, *near(folded, below, above, low, high, geometry, *sums))


def lines_kernel(count, one, two, lines):
    lines[...] = to_lines([one, two], count)


def as_lines(one, two, count):
    return pl.pallas_call(
        functools.partial(lines_kernel, count),
        out_shape=pltpu.VMEM((128, LANES), jnp.float32),
        in_specs=[VMEM] * 2,
        out_specs=VMEM,
        compiler_params=ROOM,
        name="as_lines",
    )(*near(one, two))


def combine(columns):
    size = jnp.max(columns[4])
    ratio = columns[4] / jnp.where(size > 0.0, size, 1.0)
    factor = ratio * ratio
    return (
        jnp.sum(columns[0]),
        jnp.sum(columns[1]),
        jnp.sum(columns[2] * factor),
        jnp.sum(columns[3] * factor),
        size,
    )


NEIGHBOURS = [(dx, dy) for dx in (-1, 0, 1) for dy in (-1, 0, 1) if (dx, dy) != (0, 0)]


def middle_kernel(sizes, spot, gathered, lines, image, out, joined):
    for device in range(gathered.shape[0]):
        joined[pl.ds(device, 1), :] = gathered[device]
    rows = joined[...]
    values = combine([rows[:, 64 + i : 65 + i] for i in range(5)])
    source = lax.broadcasted_iota(jnp.int32, rows.shape, 0)
    before = jnp.sum(jnp.where(source == spot[2] - 1, rows, 0.0), axis=0, keepdims=True)
    after = jnp.sum(jnp.where(source == spot[2] + 1, rows, 0.0), axis=0, keepdims=True)
    line = lax.broadcasted_iota(jnp.int32, (64, LANES), 0)
    across = lax.broadcasted_iota(jnp.int32, (64, LANES), 1)
    before = jnp.sum(jnp.where(line == across, before, 0.0), axis=1, keepdims=True)
    after = jnp.sum(jnp.where(line == across, after, 0.0), axis=1, keepdims=True)
    t = lines[64:, :]
    behind = pltpu.roll(t, 1, 1)
    ahead = pltpu.roll(t, LANES - 1, 1)
    image[...] = t + jnp.where(
        across % 8 == 7,
        jnp.where(across == LANES - 1, after, ahead),
        jnp.where(across % 8 == 0, jnp.where(across == 0, before, behind), 0.0),
    )
    row = lax.broadcasted_iota(jnp.int32, (8, LANES), 0)
    lane = lax.broadcasted_iota(jnp.int32, (8, LANES), 1)
    scalars = jnp.zeros((8, LANES), jnp.float32)
    for place, value in enumerate(values):
        scalars = jnp.where(row == place, value, scalars)
    scalars = jnp.where(lane == 8, scalars, 0.0)
    for device in range(sizes[0] * sizes[1]):
        out[pl.ds(8 * device, 8), :] = scalars
    for dx, dy in NEIGHBOURS:
        x, y = spot[0] + dx, spot[1] + dy
        at_x, at_y = (7 if dx > 0 else 0), (7 if dy > 0 else 0)
        if dy == 0:
            face = image[pl.ds(8 * at_x, 8), :]
        elif dx == 0:
            face = image[pl.ds(at_y, 8, stride=8), :]
        else:
            face = jnp.broadcast_to(image[pl.ds(8 * at_x + at_y, 1), :], (8, LANES))
        tile = jnp.where(lane == 8, scalars, face)

        @pl.when((x >= 0) & (x < sizes[0]) & (y >= 0) & (y < sizes[1]))
        def _():
            out[pl.ds(pl.multiple_of(8 * (x * sizes[1] + y), 8), 8), :] = tile


def middle(spot, gathered, lines, sizes):
    return pl.pallas_call(
        functools.partial(middle_kernel, sizes),
        out_shape=[
            pltpu.VMEM((64, LANES), jnp.float32),
            pltpu.VMEM((8 * sizes[0] * sizes[1], LANES), jnp.float32),
        ],
        in_specs=[SMEM, VMEM, VMEM],
        out_specs=[VMEM, VMEM],
        scratch_shapes=[pltpu.VMEM((gathered.shape[0], LANES), jnp.float32)],
        compiler_params=ROOM,
        name="middle",
    )(spot, *near(gathered, lines))


def finish_kernel(
    sizes, spot, gathered, image, second, first, right_side, solution_out, residual_out, t
):
    plane = sizes[0] * sizes[1]
    columns = [gathered[pl.ds(i, plane, stride=8), :][:, 8:9] for i in range(5)]
    rho, d, g_scaled, h_scaled, size = combine(columns)
    t[...] = image[...]
    lane = lax.broadcasted_iota(jnp.int32, (8, LANES), 1)
    for dx, dy in NEIGHBOURS:
        x, y = spot[0] + dx, spot[1] + dy
        inside = (x >= 0) & (x < sizes[0]) & (y >= 0) & (y < sizes[1])
        source = jnp.where(inside, x * sizes[1] + y, 0)
        tile = gathered[pl.ds(pl.multiple_of(8 * source, 8), 8), :]
        tile = jnp.where(lane == 8, pltpu.roll(tile, 1, 1), tile)
        tile = jnp.where(inside, tile, 0.0)
        at_x, at_y = (7 if dx > 0 else 0), (7 if dy > 0 else 0)
        if dy == 0:
            spots = pl.ds(8 * at_x, 8)
        elif dx == 0:
            spots = pl.ds(at_y, 8, stride=8)
        else:
            spots = pl.ds(8 * at_x + at_y, 1)
            tile = tile[0:1, :]
        t[spots, :] = t[spots, :] + tile

    def splat(value):
        return jnp.full((1, LANES), value, jnp.float32)

    rho, d = splat(rho), splat(d)
    alpha_one = rho / d
    reach = alpha_one * splat(size)
    g = reach * reach * splat(g_scaled)
    h = reach * reach * splat(h_scaled)
    stretch = g / rho
    alpha_two = (g - rho) / (h - stretch * g / alpha_one)
    along = alpha_one + alpha_two * stretch
    turn = alpha_one * alpha_two
    solution_out[...] = along * first[0:64, :] - turn * second[0:64, :]
    residual_out[...] = right_side[...] - along * first[64:128, :] + turn * t[...]


def finish(spot, gathered, image, second, first, right_side, sizes):
    full = jax.ShapeDtypeStruct((64, LANES), jnp.float32)
    return pl.pallas_call(
        functools.partial(finish_kernel, sizes),
        out_shape=[full, full],
        in_specs=[SMEM] + [VMEM] * 5,
        out_specs=[VMEM, VMEM],
        scratch_shapes=[pltpu.VMEM((64, LANES), jnp.float32)],
        compiler_params=ROOM,
        name="finish",
    )(spot, *near(gathered, image, second, first, right_side))


def exchange(rows, axes):
    return lax.all_to_all(rows, axes, 0, 0, tiled=True)


def on_device(right_side, geometry, element_shape_class, fdm_vectors, fdm_values):
    count = element_shape_class.shape[2]
    classes = fdm_vectors.shape[0]
    depth = lax.axis_size("gz")
    sizes = (lax.axis_size("gx"), lax.axis_size("gy"))
    spot = jnp.stack([lax.axis_index(a).astype(jnp.int32) for a in ("gx", "gy", "gz")])
    lines = right_side.reshape(64, LANES)
    metric_lines = geometry.reshape(256, LANES)
    flat_class = element_shape_class.reshape(1, count)
    before, after = swap(*end_messages(lines, metric_lines, flat_class), "gz")
    own_field, own_metric = own_lines(lines, metric_lines)
    deep_class = jnp.concatenate(
        [
            before[48, count - REACH : count].astype(jnp.int32),
            flat_class[0],
            after[48, :REACH].astype(jnp.int32),
        ]
    )
    deep_class = jnp.pad(deep_class, (0, LANES - deep_class.shape[0]))
    element = jnp.arange(LANES, dtype=jnp.int32) - REACH + spot[2] * count
    valid = ((element >= 0) & (element < depth * count)).astype(jnp.float32)[None, :]
    onehot = (jnp.arange(classes, dtype=jnp.int32)[:, None] == deep_class[None, :]).astype(
        jnp.float32
    )
    entries = jnp.concatenate(
        [fdm_vectors.reshape(classes, 300), fdm_values.reshape(classes, 30)], axis=1
    )
    table = lax.dot_general(
        entries, onehot, (((0,), (0,)), ((), ())), precision=HIGHEST
    )
    field, backward, forward = end_lines(before, after, own_field, count, True)
    low, high = swap(backward, forward, "gx")
    (metric,) = end_lines(before, after, own_metric, count, False)
    low, high, metric, table = lax.optimization_barrier((low, high, metric, table))
    below, above = swap(*second_edges(field, low, high, False), "gy")
    folded, rims, backward, forward, rho = block_solve(
        field, low, high, below, above, table, valid, count, False
    )
    below, above = swap(backward, forward, "gy")
    low, high = swap(*first_edges(rims, below, above), "gx")
    p, image, backward, forward, d = first_operator(
        folded, below, above, low, high, metric, count
    )
    low, high = swap(backward, forward, "gx")
    below, above = swap(*second_edges(image, low, high, True), "gy")
    folded, rims, backward, forward, g, size, q = block_solve(
        image, low, high, below, above, table, valid, count, True
    )
    below, above = swap(backward, forward, "gy")
    first = as_lines(p, q, count)
    below, above, first = lax.optimization_barrier((below, above, first))
    low, high = swap(*first_edges(rims, below, above), "gx")
    second, payload = second_operator(
        spot, folded, below, above, low, high, own_metric, (rho, d, g, size), count, depth
    )
    gathered = exchange(payload, "gz")
    image, tiles = middle(spot, gathered, second, sizes)
    gathered = exchange(tiles, ("gx", "gy"))
    answer, left = finish(spot, gathered, image, second, first, lines, sizes)
    return (answer.reshape(8, 8, LANES), left.reshape(8, 8, LANES))


def solution(mesh):
    placed = (P("gx", "gy", "gz"), P(None, "gx", "gy", "gz"), P("gx", "gy", "gz"), P(), P())
    return jax.shard_map(
        on_device,
        mesh=mesh,
        in_specs=placed,
        out_specs=(P("gx", "gy", "gz"), P("gx", "gy", "gz")),
        check_vma=False,
    )
```
